32 devices in a mesh: expert: 8 (over y, x, core), tensor: 4 (over z).
Axes of the slice: x: 2, y: 2, z: 4, core: 2. Of those that a mesh axis runs over, the one named last changes fastest.
Arguments:
- tokens_in: bfloat16 [2048, 2048], P(('expert', 'tensor')), may hold values from -6 to 6
- out_grad: bfloat16 [2048, 2048], P(('expert', 'tensor')), may hold values from -6 to 6
- routes: int32 [2048, 6], P('expert'), may hold values from 0 to 63, all different within a row; in each aligned block of 256 rows (0 to 255, 256 to 511, ...) at most 30 rows name the same one
- attn_gain: float32 [2048], replicated, may hold values from 0.5 to 1.5
- kv_gain: float32 [512], replicated, may hold values from 0.5 to 1.5
- ffn_gain: float32 [2048], replicated, may hold values from 0.5 to 1.5
- w_query: bfloat16 [2048, 3072], P('expert', 'tensor'), may hold values from -0.125 to 0.125
- w_latent: bfloat16 [2048, 576], replicated, may hold values from -0.125 to 0.125
- w_keyval: bfloat16 [512, 4096], P('expert', 'tensor'), may hold values from -0.25 to 0.25
- w_output: bfloat16 [2048, 2048], P('tensor', 'expert'), may hold values from -0.5 to 0.5
- w_router: bfloat16 [2048, 64], replicated, may hold values from -0.125 to 0.125
- w_shared_in: bfloat16 [2, 2048, 2816], P(None, 'expert', 'tensor'), may hold values from -0.125 to 0.125
- w_shared_out: bfloat16 [2816, 2048], P('tensor', 'expert'), may hold values from -0.109375 to 0.109375
- w_expert_in: bfloat16 [64, 2, 2048, 1408], P('expert', None, None, 'tensor'), may hold values from -0.125 to 0.125
- w_expert_out: bfloat16 [64, 1408, 2048], P('expert', 'tensor'), may hold values from -0.15625 to 0.15625
Outputs:
- block_out: bfloat16 [2048, 2048], P(('expert', 'tensor'))
- grad_in: float32 [2048, 2048], P(('expert', 'tensor'))
- grad_attn_gain: float32 [2048], replicated
- grad_kv_gain: float32 [512], replicated
- grad_ffn_gain: float32 [2048], replicated
- grad_w_query: float32 [2048, 3072], P('expert', 'tensor')
- grad_w_latent: float32 [2048, 576], replicated
- grad_w_keyval: float32 [512, 4096], P('expert', 'tensor')
- grad_w_output: float32 [2048, 2048], P('tensor', 'expert')
- grad_w_router: float32 [2048, 64], replicated
- grad_w_shared_in: float32 [2, 2048, 2816], P(None, 'expert', 'tensor')
- grad_w_shared_out: float32 [2816, 2048], P('tensor', 'expert')
- grad_w_expert_in: float32 [64, 2, 2048, 1408], P('expert', None, None, 'tensor')
- grad_w_expert_out: float32 [64, 1408, 2048], P('expert', 'tensor')
The draws below stay inside these ranges and needn't reach their ends.
Inputs may be any that keep to these rules, and one draw needn't show every extreme that they name: `routes`: each row names 6 different experts; within each sequence no expert is named by more than 30 rows, a bound that some block reaches.
All inputs are finite; a program needn't handle non-finite values.
Results may differ from the reference program's by a relative error of at most 0.024.
Values may be sent and summed in bfloat16 or wider, within the bound.
No kernel may reach another device: no remote copies, remote signals or barrier semaphores. Data moves between devices by JAX's collectives and lax.ppermute only.
A program may use at most 384 MiB of HBM per device.

```python
import math
import jax
import jax.numpy as jnp
import numpy as np
from jax import lax

D = 2048
H = 16
NOPE = 128
ROPE = 64
VD = 128
KVR = 512
FEXP = 1408
EXPERTS = 64
TOP = 6
SEQ = 256
TOKENS = 2048
FSH = 2816
CAP = 30
N_TENSOR = 4


def shard_levels(key, shape, split, low, high):
    gain, own = 1.0, jax.random.fold_in(key, 6)
    for axis_at, blocks in split:
        draws = jnp.exp(jax.random.uniform(jax.random.fold_in(own, axis_at), (blocks,), jnp.float32, low / len(split), high / len(split)))
        gain = gain * jnp.repeat(draws, shape[axis_at] // blocks).reshape([-1 if axis == axis_at else 1 for axis in range(len(shape))])
    return gain


def assign_block(key, own, number, rows, amount, top, most, lean):
    order = jax.random.permutation(key, amount)
    packed, ordinary = portions_of(amount, rows * top, most, lean, True), portions_of(amount, rows * top, most, lean, False)
    places = jnp.arange(amount)

    def named(tallies, offset_by):
        used = int((tallies > 0).sum())
        fixed = max(1, used // 4)
        passed = fixed + (places - fixed + offset_by * (used - fixed)) % max(1, amount - fixed)
        return jnp.zeros((amount,), jnp.int32).at[order[jnp.where(places < fixed, places, passed)]].set(jnp.asarray(tallies, jnp.int32))

    tallies = jnp.where(number % 4 == 0, named(packed, number // 4), named(ordinary, number - number // 4 - 1))
    mixed = jax.random.permutation(jax.random.fold_in(own, 3), amount)
    donor, sink = mixed[0:amount // 2 * 2:2], mixed[1:amount // 2 * 2:2]
    slack = jnp.minimum(tallies[donor] - 1, most - tallies[sink]) // 2
    slack = jnp.where((donor == order[0]) | (sink == order[0]) | (tallies[sink] == 0), 0, jnp.maximum(slack, 0))
    passed = jax.random.randint(jax.random.fold_in(own, 4), (amount // 2,), 0, 1 << 20) % (slack + 1)
    tallies = tallies.at[donor].add(-passed).at[sink].add(passed)
    members = jnp.searchsorted(jnp.cumsum(tallies), jnp.arange(rows * top), side="right").astype(jnp.int32)
    table = members.reshape(top, rows).T
    table = table[jax.random.permutation(jax.random.fold_in(own, 1), rows)]
    offset_by = jax.random.randint(jax.random.fold_in(own, 2), (rows, 1), 0, top)
    return jnp.take_along_axis(table, (jnp.arange(top)[None, :] + offset_by) % top, axis=1)


def portions_of(count, total, most, lean, full):
    portions = [(1 << 20) // math.isqrt(rank ** lean) + 1 for rank in range(1, count + 1)]
    largest = most if full else min(most, max(-(-total // count), total * portions[0] // sum(portions)))
    least = 1 if total - largest >= count - 1 else 0
    holding, surplus = [largest] + [least] * (count - 1), total - largest - least * (count - 1)
    while surplus > 0:
        movable = [i for i in range(1, count) if holding[i] < largest] or [i for i in range(1, count) if holding[i] < most]
        mass, remaining = sum([portions[i] for i in movable]), surplus
        for i in movable:
            more = min(most - holding[i], max(1, remaining * portions[i] // mass), surplus)
            holding[i] = holding[i] + more
            surplus = surplus - more
    return np.array(holding)


def scatter_about(key, dims, spread, most, cuts=(), held_as=jnp.bfloat16):
    gain = shard_levels(key, dims, cuts, -0.22, 0.18) if cuts else 1.0
    drawn = jax.random.normal(key, dims, jnp.float32) * spread * gain
    return jnp.minimum(jnp.maximum(drawn, -most), most).astype(held_as)


def setup_inputs(seed: int = 0) -> dict:
    arg_keys = jax.random.split(jax.random.key(seed), 16)
    tokens_in = scatter_about(arg_keys[0], (TOKENS, D), 1.0, 6.0, ((0, 32),))
    out_grad = scatter_about(arg_keys[1], (TOKENS, D), 1.0, 6.0, ((0, 32),))
    routes_keys = jax.random.split(jax.random.fold_in(arg_keys[2], 1), TOKENS // SEQ)
    routes_turns = jax.random.permutation(jax.random.fold_in(arg_keys[2], 3), TOKENS // SEQ)
    routes = jax.vmap(lambda own, number: assign_block(jax.random.fold_in(arg_keys[2], 2), own, number, SEQ, EXPERTS, TOP, CAP, 2))(routes_keys, routes_turns).reshape((TOKENS, TOP))
    attn_gain = jnp.clip(1.0 + 0.1 * jax.random.normal(arg_keys[3], (D,), jnp.float32), 0.5, 1.5)
    kv_gain = jnp.clip(1.0 + 0.1 * jax.random.normal(arg_keys[4], (KVR,), jnp.float32), 0.5, 1.5)
    ffn_gain = jnp.clip(1.0 + 0.1 * jax.random.normal(arg_keys[5], (D,), jnp.float32), 0.5, 1.5)
    w_query = scatter_about(arg_keys[6], (D, H * (NOPE + ROPE)), D ** -0.5, 0.125, ((0, 8), (1, 4)))
    w_latent = scatter_about(arg_keys[7], (D, KVR + ROPE), D ** -0.5, 0.125)
    w_keyval = scatter_about(arg_keys[8], (KVR, H * (NOPE + VD)), KVR ** -0.5, 0.25, ((0, 8), (1, 4)))
    w_output = scatter_about(arg_keys[9], (H * VD, D), VD ** -0.5, 0.5, ((0, 4), (1, 8)))
    w_router = scatter_about(arg_keys[10], (D, EXPERTS), D ** -0.5, 0.125)
    w_shared_in = scatter_about(arg_keys[11], (2, D, FSH), D ** -0.5, 0.125, ((1, 8), (2, 4)))
    w_shared_out = scatter_about(arg_keys[12], (FSH, D), FSH ** -0.5, 0.109375, ((0, 4), (1, 8)))
    w_expert_in = scatter_about(arg_keys[13], (EXPERTS, 2, D, FEXP), D ** -0.5, 0.125, ((0, 8), (3, 4)))
    w_expert_out = scatter_about(arg_keys[14], (EXPERTS, FEXP, D), FEXP ** -0.5, 0.15625, ((0, 8), (1, 4)))
    return dict(tokens_in=tokens_in, out_grad=out_grad, routes=routes, attn_gain=attn_gain, kv_gain=kv_gain, ffn_gain=ffn_gain, w_query=w_query, w_latent=w_latent, w_keyval=w_keyval, w_output=w_output, w_router=w_router, w_shared_in=w_shared_in, w_shared_out=w_shared_out, w_expert_in=w_expert_in, w_expert_out=w_expert_out)


EPSILON = 1e-06
ROUTE_SCALE = 2.446
ROPE_BASE = 50000.0
BLOCK_LIMIT = 512

def mix_dot(left_side, right_side):
    return jnp.dot(left_side, right_side, preferred_element_type=jnp.float32)

def contract(pattern, left_side, right_side):
    return jnp.einsum(pattern, left_side.astype(jnp.float32), right_side.astype(jnp.float32), precision=lax.Precision.HIGHEST)

def exact_dot(left_side, right_side):
    return jnp.dot(left_side, right_side, precision=lax.Precision.HIGHEST)

def rms_forward(values, gain_vec):
    inverse = lax.rsqrt(lax.optimization_barrier(jnp.mean(values * values, axis=-1, keepdims=True)) + EPSILON)
    return (values * inverse * gain_vec, inverse)

def rms_backward(values, inverse, gain_vec, grad_normed):
    weighted = grad_normed * gain_vec
    grad_values = inverse * weighted - values * (inverse * inverse * inverse) * lax.optimization_barrier(jnp.mean(values * weighted, axis=-1, keepdims=True))
    grad_gain = lax.optimization_barrier(jnp.sum(grad_normed * values * inverse, axis=0))
    return (grad_values, grad_gain)

def rope_tables(row_count):
    half_rope = ROPE // 2
    position = jnp.arange(row_count).astype(jnp.float32)[:, None]
    frequency = jnp.exp(-jnp.log(ROPE_BASE) * jnp.arange(half_rope).astype(jnp.float32) / half_rope)
    angles = position * frequency[None, :]
    return (jnp.cos(angles), jnp.sin(angles))

def rotate(columns, cosine, sine_table):
    half_rope = columns.shape[-1] // 2
    first_half = columns[..., :half_rope]
    second_half = columns[..., half_rope:]
    return jnp.concatenate([first_half * cosine - second_half * sine_table, first_half * sine_table + second_half * cosine], axis=-1)

def unrotate(columns, cosine, sine_table):
    half_rope = columns.shape[-1] // 2
    first_half = columns[..., :half_rope]
    second_half = columns[..., half_rope:]
    return jnp.concatenate([first_half * cosine + second_half * sine_table, second_half * cosine - first_half * sine_table], axis=-1)

def swiglu(gate_part, up_part):
    return jax.nn.silu(gate_part) * up_part

def swiglu_backward(gate_part, up_part, grad_hidden):
    gate_sigmoid = jax.nn.sigmoid(gate_part)
    activation = gate_part * gate_sigmoid
    slope = gate_sigmoid * (1.0 + gate_part * (1.0 - gate_sigmoid))
    return jnp.stack([grad_hidden * up_part * slope, grad_hidden * activation], axis=-2).astype(jnp.bfloat16)

def score_block(query_rows, key_nope, key_rope, first_row):
    block_rows = query_rows.shape[0]
    key_count = key_nope.shape[0]
    softmax_scale = (NOPE + ROPE) ** (-0.5)
    scores = contract('qhd,khd->hqk', query_rows[..., :NOPE], key_nope) + contract('qhr,kr->hqk', query_rows[..., NOPE:], key_rope)
    scores = scores * softmax_scale
    row_ids = first_row + jnp.arange(block_rows, dtype=jnp.int32)
    col_ids = jnp.arange(key_count, dtype=jnp.int32)
    allowed = col_ids[None, :] <= row_ids[:, None]
    return jnp.where(allowed[None], scores, -1e+30)

def attend_forward(queries, key_nope, key_rope, values):
    row_count = queries.shape[0]
    block_rows = min(BLOCK_LIMIT, row_count)

    def one_block(block_index):
        first_row = block_index * block_rows
        query_rows = lax.dynamic_slice_in_dim(queries, first_row, block_rows, 0)
        scores = score_block(query_rows, key_nope, key_rope, first_row)
        top_score = lax.optimization_barrier(jnp.max(scores, axis=-1, keepdims=True))
        log_total = top_score + jnp.log(lax.optimization_barrier(jnp.sum(jnp.exp(scores - top_score), axis=-1, keepdims=True)))
        soft_low = jnp.exp(scores - log_total).astype(jnp.bfloat16)
        attended = contract('hqk,khv->qhv', soft_low, values).astype(jnp.bfloat16)
        return (attended, log_total[..., 0])
    attended, log_total = lax.map(one_block, jnp.arange(row_count // block_rows, dtype=jnp.int32))
    return (attended.reshape(row_count, queries.shape[1], values.shape[-1]), log_total)

def attend_backward(queries, key_nope, key_rope, values, attended, log_total, grad_attended):
    row_count = queries.shape[0]
    block_rows = min(BLOCK_LIMIT, row_count)
    softmax_scale = (NOPE + ROPE) ** (-0.5)
    start_sums = (jnp.zeros(key_nope.shape, jnp.float32), jnp.zeros(key_rope.shape, jnp.float32), jnp.zeros(values.shape, jnp.float32))

    def one_block(carried, block_index):
        sum_nope, sum_rope, sum_values = carried
        first_row = block_index * block_rows
        query_rows = lax.dynamic_slice_in_dim(queries, first_row, block_rows, 0)
        out_rows = lax.dynamic_slice_in_dim(attended, first_row, block_rows, 0)
        grad_rows = lax.dynamic_slice_in_dim(grad_attended, first_row, block_rows, 0)
        scores = score_block(query_rows, key_nope, key_rope, first_row)
        soft_full = jnp.exp(scores - log_total[block_index][..., None])
        soft_low = soft_full.astype(jnp.bfloat16)
        grad_soft = contract('qhv,khv->hqk', grad_rows, values)
        row_delta = lax.optimization_barrier(jnp.sum(grad_rows.astype(jnp.float32) * out_rows.astype(jnp.float32), axis=-1)).T
        grad_scores = (soft_full * (grad_soft - row_delta[..., None]) * softmax_scale).astype(jnp.bfloat16)
        grad_query_rows = jnp.concatenate([contract('hqk,khd->qhd', grad_scores, key_nope), contract('hqk,kr->qhr', grad_scores, key_rope)], axis=-1)
        sum_nope = sum_nope + contract('hqk,qhd->khd', grad_scores, query_rows[..., :NOPE])
        sum_rope = sum_rope + contract('hqk,qhr->kr', grad_scores, query_rows[..., NOPE:])
        sum_values = sum_values + contract('hqk,qhv->khv', soft_low, grad_rows)
        return ((sum_nope, sum_rope, sum_values), grad_query_rows)
    carried, grad_queries = lax.scan(one_block, start_sums, jnp.arange(row_count // block_rows, dtype=jnp.int32))
    return (grad_queries.reshape(row_count, queries.shape[1], queries.shape[2]), carried)

def gate_values(logits, route_rows):
    chosen = route_rows[..., None] == jnp.arange(EXPERTS, dtype=jnp.int32)
    picked = lax.optimization_barrier(jnp.sum(jnp.where(chosen, logits[:, None, :], 0.0), axis=-1))
    gate_sigmoid = jax.nn.sigmoid(picked)
    gate_total = lax.optimization_barrier(jnp.sum(gate_sigmoid, axis=-1, keepdims=True))
    return (ROUTE_SCALE * gate_sigmoid / gate_total, gate_sigmoid, gate_total, chosen)

def gate_backward(grad_gate, gate_sigmoid, gate_total, chosen):
    grad_sigmoid = ROUTE_SCALE * (grad_gate / gate_total - lax.optimization_barrier(jnp.sum(grad_gate * gate_sigmoid, axis=-1, keepdims=True)) / (gate_total * gate_total))
    grad_pick = grad_sigmoid * gate_sigmoid * (1.0 - gate_sigmoid)
    return lax.optimization_barrier(jnp.sum(jnp.where(chosen, grad_pick[..., None], 0.0), axis=1))

def route_targets(route_rows, capacity):
    flat_routes = route_rows.reshape(-1).astype(jnp.int32)
    onehot = (flat_routes[:, None] == jnp.arange(EXPERTS, dtype=jnp.int32)[None, :]).astype(jnp.int32)
    before = jnp.cumsum(onehot, axis=0) - onehot
    target = (flat_routes * capacity + lax.optimization_barrier(jnp.sum(before * onehot, axis=1))).astype(jnp.int32)
    pair_count = flat_routes.shape[0]
    slot_owner = jnp.full((EXPERTS * capacity,), pair_count, jnp.int32).at[target].set(jnp.arange(pair_count, dtype=jnp.int32))
    return (target, slot_owner)

def rounded_blocks(partials):
    low = lax.optimization_barrier(partials.astype(jnp.bfloat16))
    return lax.optimization_barrier(jnp.sum(low.astype(jnp.float32), axis=2))

def reference(tokens_in, out_grad, routes, attn_gain, kv_gain, ffn_gain, w_query, w_latent, w_keyval, w_output, w_router, w_shared_in, w_shared_out, w_expert_in, w_expert_out):
    cosine, sine_table = rope_tables(SEQ)
    expert_in_wide = w_expert_in.astype(jnp.float32)
    expert_out_wide = w_expert_out.astype(jnp.float32)
    block_units = FEXP // N_TENSOR
    expert_in_split = expert_in_wide.reshape(EXPERTS, 2, D, N_TENSOR, block_units)
    expert_out_split = expert_out_wide.reshape(EXPERTS, N_TENSOR, block_units, D)
    latent_wide = w_latent.astype(jnp.float32)
    router_wide = w_router.astype(jnp.float32)
    seq_count = tokens_in.shape[0] // SEQ

    def one_sequence(carried, items):
        seq_tokens, seq_grad, seq_routes = items
        stream = seq_tokens.astype(jnp.float32)
        normed_one, inverse_one = rms_forward(stream, attn_gain)
        normed_one = normed_one.astype(jnp.bfloat16)
        queries = mix_dot(normed_one, w_query).reshape(SEQ, H, NOPE + ROPE)
        queries = jnp.concatenate([queries[..., :NOPE], rotate(queries[..., NOPE:], cosine[:, None, :], sine_table[:, None, :])], axis=-1).astype(jnp.bfloat16)
        latent = mix_dot(normed_one, w_latent)
        compressed = latent[:, :KVR]
        comp_normed, comp_inverse = rms_forward(compressed, kv_gain)
        comp_normed = comp_normed.astype(jnp.bfloat16)
        key_rope = rotate(latent[:, KVR:], cosine, sine_table).astype(jnp.bfloat16)
        keyval = mix_dot(comp_normed, w_keyval).reshape(SEQ, H, NOPE + VD).astype(jnp.bfloat16)
        key_nope = keyval[..., :NOPE]
        values = keyval[..., NOPE:]
        attended, log_total = attend_forward(queries, key_nope, key_rope, values)
        attended_flat = attended.reshape(SEQ, H * VD)
        residual = stream + mix_dot(attended_flat, w_output)
        normed_two, inverse_two = rms_forward(residual, ffn_gain)
        normed_two = normed_two.astype(jnp.bfloat16)
        logits = mix_dot(normed_two, w_router)
        gate_weights, gate_sigmoid, gate_total, chosen = gate_values(logits, seq_routes)
        target, slot_owner = route_targets(seq_routes, CAP)
        padded_normed = jnp.concatenate([normed_two, jnp.zeros((1, D), jnp.bfloat16)], axis=0)
        expert_rows = padded_normed[slot_owner // TOP].reshape(EXPERTS, CAP, D)
        gates_up = contract('ecd,egdf->ecgf', expert_rows, expert_in_wide)
        hidden = swiglu(gates_up[..., 0, :], gates_up[..., 1, :]).astype(jnp.bfloat16)
        hidden_split = hidden.reshape(EXPERTS, CAP, N_TENSOR, block_units)
        expert_out = rounded_blocks(contract('ecnf,enfd->ecnd', hidden_split, expert_out_split))
        pair_out = expert_out.reshape(EXPERTS * CAP, D)[target].reshape(SEQ, TOP, D)
        routed = lax.optimization_barrier(jnp.sum(gate_weights[..., None] * pair_out, axis=1))
        shared_gate = mix_dot(normed_two, w_shared_in[0])
        shared_up = mix_dot(normed_two, w_shared_in[1])
        shared_hidden = swiglu(shared_gate, shared_up).astype(jnp.bfloat16)
        block_out = (residual + routed + mix_dot(shared_hidden, w_shared_out)).astype(jnp.bfloat16)
        grad_float = seq_grad.astype(jnp.float32)
        grad_gate = lax.optimization_barrier(jnp.sum(pair_out * grad_float[:, None, :], axis=-1))
        grad_pair = (gate_weights[..., None] * grad_float[:, None, :]).astype(jnp.bfloat16).reshape(SEQ * TOP, D)
        padded_grad = jnp.concatenate([grad_pair, jnp.zeros((1, D), jnp.bfloat16)], axis=0)
        grad_rows_in = padded_grad[slot_owner].reshape(EXPERTS, CAP, D)
        grad_hidden = contract('ecd,efd->ecf', grad_rows_in, expert_out_wide)
        grad_gate_up = swiglu_backward(gates_up[..., 0, :], gates_up[..., 1, :], grad_hidden)
        grad_expert_out = contract('ecf,ecd->efd', hidden, grad_rows_in)
        grad_expert_in = contract('ecd,ecgf->egdf', expert_rows, grad_gate_up)
        grad_gate_split = grad_gate_up.reshape(EXPERTS, CAP, 2, N_TENSOR, block_units)
        grad_rows_out = rounded_blocks(contract('ecgnf,egdnf->ecnd', grad_gate_split, expert_in_split))
        grad_normed = lax.optimization_barrier(jnp.sum(grad_rows_out.reshape(EXPERTS * CAP, D)[target].reshape(SEQ, TOP, D), axis=1))
        grad_logits = gate_backward(grad_gate, gate_sigmoid, gate_total, chosen)
        grad_router = exact_dot(normed_two.astype(jnp.float32).T, grad_logits)
        grad_normed = grad_normed + exact_dot(grad_logits, router_wide.T)
        grad_shared_hidden = contract('td,fd->tf', seq_grad, w_shared_out)
        grad_shared = swiglu_backward(shared_gate, shared_up, grad_shared_hidden)
        grad_shared_out = contract('tf,td->fd', shared_hidden, seq_grad)
        grad_shared_in = contract('td,tgf->gdf', normed_two, grad_shared)
        grad_normed = grad_normed + contract('tgf,gdf->td', grad_shared, w_shared_in)
        grad_res_part, grad_ffn_gain = rms_backward(residual, inverse_two, ffn_gain, grad_normed)
        grad_residual = grad_float + grad_res_part
        grad_res_low = grad_residual.astype(jnp.bfloat16)
        grad_output = contract('tv,td->vd', attended_flat, grad_res_low)
        grad_attended = contract('td,vd->tv', grad_res_low, w_output).astype(jnp.bfloat16).reshape(SEQ, H, VD)
        grad_queries, key_grads = attend_backward(queries, key_nope, key_rope, values, attended, log_total, grad_attended)
        grad_key_nope, grad_key_rope, grad_values = key_grads
        grad_query_raw = jnp.concatenate([grad_queries[..., :NOPE], unrotate(grad_queries[..., NOPE:], cosine[:, None, :], sine_table[:, None, :])], axis=-1).reshape(SEQ, H * (NOPE + ROPE)).astype(jnp.bfloat16)
        grad_query_weight = contract('td,tq->dq', normed_one, grad_query_raw)
        grad_normed_one = contract('tq,dq->td', grad_query_raw, w_query)
        grad_keyval = jnp.concatenate([grad_key_nope, grad_values], axis=-1).reshape(SEQ, H * (NOPE + VD)).astype(jnp.bfloat16)
        grad_keyval_weight = contract('tc,tk->ck', comp_normed, grad_keyval)
        grad_comp_normed = contract('tk,ck->tc', grad_keyval, w_keyval)
        grad_compressed, grad_kv_gain = rms_backward(compressed, comp_inverse, kv_gain, grad_comp_normed)
        grad_latent_out = jnp.concatenate([grad_compressed, unrotate(grad_key_rope, cosine, sine_table)], axis=-1)
        grad_latent = exact_dot(normed_one.astype(jnp.float32).T, grad_latent_out)
        grad_normed_one = grad_normed_one + exact_dot(grad_latent_out, latent_wide.T)
        grad_x_part, grad_attn_gain = rms_backward(stream, inverse_one, attn_gain, grad_normed_one)
        grad_in = grad_residual + grad_x_part
        terms = (grad_attn_gain, grad_kv_gain, grad_ffn_gain, grad_query_weight, grad_latent, grad_keyval_weight, grad_output, grad_router, grad_shared_in, grad_shared_out, grad_expert_in, grad_expert_out)
        carried = tuple((total + term for total, term in zip(carried, terms)))
        return (carried, (block_out, grad_in))
    start_sums = (jnp.zeros(attn_gain.shape, jnp.float32), jnp.zeros(kv_gain.shape, jnp.float32), jnp.zeros(ffn_gain.shape, jnp.float32), jnp.zeros(w_query.shape, jnp.float32), jnp.zeros(w_latent.shape, jnp.float32), jnp.zeros(w_keyval.shape, jnp.float32), jnp.zeros(w_output.shape, jnp.float32), jnp.zeros(w_router.shape, jnp.float32), jnp.zeros(w_shared_in.shape, jnp.float32), jnp.zeros(w_shared_out.shape, jnp.float32), jnp.zeros(w_expert_in.shape, jnp.float32), jnp.zeros(w_expert_out.shape, jnp.float32))
    items = (tokens_in.reshape(seq_count, SEQ, D), out_grad.reshape(seq_count, SEQ, D), routes.reshape(seq_count, SEQ, TOP))
    sums, (block_out, grad_in) = lax.scan(one_sequence, start_sums, items)
    return (block_out.reshape(seq_count * SEQ, D), grad_in.reshape(seq_count * SEQ, D), sums[0], sums[1], sums[2], sums[3], sums[4], sums[5], sums[6], sums[7], sums[8], sums[9], sums[10], sums[11])
```

```python
import functools
import math

import jax
import jax.numpy as jnp
from jax import lax
from jax.experimental import pallas as pl
from jax.experimental.pallas import tpu as pltpu
from jax.sharding import PartitionSpec as P

NOPE = 128
ROPE = 64
VD = 128
KVR = 512
EXPERTS = 64
TOP = 6
SLOTS = 32
SLOT_BLOCK = 256
LANES = 128

EPSILON = 1e-06
ROUTE_SCALE = 2.446
ROPE_BASE = 50000.0
BF16 = jnp.bfloat16
F32 = jnp.float32


def mix_dot(left_side, right_side):
    return jnp.dot(left_side, right_side, preferred_element_type=F32)


def contract(pattern, left_side, right_side):
    return jnp.einsum(pattern, left_side, right_side, preferred_element_type=F32)


def rms_forward(values, gain_vec):
    inverse = lax.rsqrt(jnp.mean(values * values, axis=-1, keepdims=True) + EPSILON)
    return (values * inverse * gain_vec, inverse)


def rms_backward(values, inverse, gain_vec, grad_normed):
    weighted = grad_normed * gain_vec
    grad_values = inverse * weighted - values * (inverse * inverse * inverse) * jnp.mean(
        values * weighted, axis=-1, keepdims=True
    )
    grad_gain = jnp.sum(grad_normed * values * inverse, axis=0)
    return (grad_values, grad_gain)


def rope_tables(position):
    half_rope = ROPE // 2
    frequency = jnp.exp(-jnp.log(ROPE_BASE) * jnp.arange(half_rope).astype(F32) / half_rope)
    angles = position.astype(F32)[:, None] * frequency[None, :]
    return (jnp.cos(angles), jnp.sin(angles))


def rotate(columns, cosine, sine_table):
    half_rope = columns.shape[-1] // 2
    first_half = columns[..., :half_rope]
    second_half = columns[..., half_rope:]
    return jnp.concatenate(
        [
            first_half * cosine - second_half * sine_table,
            first_half * sine_table + second_half * cosine,
        ],
        axis=-1,
    )


def low_add(first, second):
    return (first.astype(F32) + second.astype(F32)).astype(BF16)


class Grid:
    def __init__(self):
        self.experts = lax.axis_size("expert")
        self.depth = lax.axis_size("tensor")
        self.side = math.isqrt(self.experts // 2)
        assert self.side * self.side * 2 == self.experts
        self.offsets = [
            (dy, dx, dc)
            for dy in range(self.side)
            for dx in range(self.side)
            for dc in range(2)
        ]

    def neighbour(self, place, offset):
        side = self.side
        y, x, core = place // (2 * side), place // 2 % side, place % 2
        dy, dx, dc = offset
        return (((y + dy) % side) * side + (x + dx) % side) * 2 + (core + dc) % 2

    def place_of(self, offset):
        return self.neighbour(lax.axis_index("expert"), offset)

    def fetch(self, array, offset):
        pairs = [(self.neighbour(place, offset), place) for place in range(self.experts)]
        return lax.ppermute(array, "expert", pairs)

    def send(self, array, offset):
        pairs = [(place, self.neighbour(place, offset)) for place in range(self.experts)]
        return lax.ppermute(array, "expert", pairs)

    def gather(self, shard):
        if self.side != 2:
            return [shard] + [self.fetch(shard, offset) for offset in self.offsets[1:]]
        half = shard.shape[0] // 2
        along_x = self.fetch(shard, (0, 1, 0))
        along_y = self.fetch(shard, (1, 0, 0))
        pair = self.fetch(shard, (0, 0, 1))
        first = self.fetch(along_x[:half], (1, 0, 0))
        second = self.fetch(along_y[half:], (0, 1, 0))
        pair_x = self.fetch(along_x, (0, 0, 1))
        pair_y = self.fetch(along_y, (0, 0, 1))
        pair_first = self.fetch(first, (0, 0, 1))
        pair_second = self.fetch(second, (0, 0, 1))
        return [
            shard,
            pair,
            along_x,
            pair_x,
            along_y,
            pair_y,
            jnp.concatenate([first, second]),
            jnp.concatenate([pair_first, pair_second]),
        ]

    def reduce(self, chunks):
        if self.side != 2:
            total = chunks[0].astype(F32)
            for offset, chunk in zip(self.offsets[1:], chunks[1:]):
                total = total + self.send(chunk, offset).astype(F32)
            return total
        half = chunks[0].shape[0] // 2
        own = {}
        for place in (6, 2, 4, 0):
            own[place] = low_add(chunks[place], self.send(chunks[place + 1], (0, 0, 1)))
        first = self.send(own[6][:half], (0, 1, 0))
        second = self.send(own[6][half:], (1, 0, 0))
        to_y = jnp.concatenate([low_add(own[4][:half], first), own[4][half:]])
        to_x = jnp.concatenate([own[2][:half], low_add(own[2][half:], second)])
        from_x = self.send(to_x, (0, 1, 0))
        from_y = self.send(to_y, (1, 0, 0))
        return own[0].astype(F32) + from_x.astype(F32) + from_y.astype(F32)

    def gather_depth(self, shard):
        depth = self.depth
        return [shard] + [
            lax.ppermute(shard, "tensor", [((i + k) % depth, i) for i in range(depth)])
            for k in range(1, depth)
        ]

    def reduce_depth(self, chunks):
        depth = self.depth
        total = chunks[0].astype(F32)
        for k in range(1, depth):
            total = total + lax.ppermute(
                chunks[k], "tensor", [(i, (i + k) % depth) for i in range(depth)]
            ).astype(F32)
        return total

    def absolute(self, pieces, axis):
        size = pieces[0].shape[axis]
        shape = list(pieces[0].shape)
        shape[axis] = size * self.experts
        whole = jnp.zeros(shape, pieces[0].dtype)
        for offset, piece in zip(self.offsets, pieces):
            whole = lax.dynamic_update_slice_in_dim(
                whole, piece, self.place_of(offset) * size, axis
            )
        return whole

    def relative(self, whole, axis):
        size = whole.shape[axis] // self.experts
        return [
            lax.dynamic_slice_in_dim(whole, self.place_of(offset) * size, size, axis)
            for offset in self.offsets
        ]

    def absolute_depth(self, pieces, axis):
        size = pieces[0].shape[axis]
        shape = list(pieces[0].shape)
        shape[axis] = size * self.depth
        whole = jnp.zeros(shape, pieces[0].dtype)
        own = lax.axis_index("tensor")
        for k, piece in enumerate(pieces):
            whole = lax.dynamic_update_slice_in_dim(
                whole, piece, (own + k) % self.depth * size, axis
            )
        return whole

    def relative_depth(self, whole, axis):
        size = whole.shape[axis] // self.depth
        own = lax.axis_index("tensor")
        return [
            lax.dynamic_slice_in_dim(whole, (own + k) % self.depth * size, size, axis)
            for k in range(self.depth)
        ]


def split_rows(array, count):
    size = array.shape[0] // count
    return [array[i * size : (i + 1) * size] for i in range(count)]


def attention_scores(queries, key_nope, key_rope, position):
    scores = contract("qhd,khd->hqk", queries[..., :NOPE], key_nope) + contract(
        "qhr,kr->hqk", queries[..., NOPE:], key_rope
    )
    scores = scores * ((NOPE + ROPE) ** (-0.5))
    allowed = position[None, :] <= position[:, None]
    return jnp.where(allowed[None], scores, -1e30)


def dot_nn(left, right):
    return lax.dot_general(left, right, (((1,), (0,)), ((), ())), preferred_element_type=F32)


def dot_nt(left, right):
    return lax.dot_general(left, right, (((1,), (1,)), ((), ())), preferred_element_type=F32)


def dot_tn(left, right):
    return lax.dot_general(left, right, (((0,), (0,)), ((), ())), preferred_element_type=F32)


def silu_parts(gate):
    sigmoid = 1.0 / (1.0 + jnp.exp(-gate))
    return sigmoid, gate * sigmoid


def split_high(value):
    high = value.astype(BF16)
    return high, (value - high.astype(F32)).astype(BF16)


def pick_rows(routes, local):
    count = routes.shape[1]
    expert = lax.broadcasted_iota(jnp.int32, (EXPERTS, count), 0)
    chosen = expert == routes[0:1]
    for k in range(1, routes.shape[0]):
        chosen = chosen | (expert == routes[k : k + 1])
    chosen = chosen.astype(F32)
    rows = max(local, 16)
    earlier = lax.broadcasted_iota(jnp.int32, (count, count), 0) < lax.broadcasted_iota(
        jnp.int32, (count, count), 1
    )
    rank = dot_nn(chosen[:rows].astype(BF16), earlier.astype(F32).astype(BF16))
    rank = jnp.where(chosen[:rows] > 0.5, rank, -1.0)
    parts = []
    slot = lax.broadcasted_iota(jnp.int32, (SLOTS, count), 0).astype(F32)
    for j in range(local):
        parts.append((slot == rank[j : j + 1]).astype(F32))
    return jnp.concatenate(parts, axis=0), chosen


def dispatch_grads_kernel(local, routes_ref, grads_ref, shared_ref, *rest):
    slot_ref, raw_ref = rest[-2:]
    pick, _ = pick_rows(routes_ref[...], local)
    grads = grads_ref[...]
    slot_ref[...] = (
        dot_nn(pick.astype(BF16), grads).astype(BF16).reshape(local, SLOTS, grads.shape[1])
    )
    raw_ref[...] = dot_nt(shared_ref[...], grads)


def dispatch_rows_kernel(
    local, units, routes_ref, rows_ref, router_ref, shared_ref, raw_ref, *rest
):
    slot_ref, info_ref, pick_ref, gate_ref, hidden_ref, back_ref = rest[-6:]
    pick, chosen = pick_rows(routes_ref[...], local)
    rows = rows_ref[...]
    low = pick.astype(BF16)
    pick_ref[...] = low
    slot_ref[...] = dot_nn(low, rows).astype(BF16).reshape(local, SLOTS, rows.shape[1])
    sigmoid = chosen / (1.0 + jnp.exp(-dot_nt(router_ref[...], rows)))
    total = jnp.sum(sigmoid, axis=0, keepdims=True)
    gate_ref[0] = sigmoid
    gate_ref[1] = jnp.broadcast_to(total, sigmoid.shape)
    weight = ROUTE_SCALE * sigmoid / total
    scale = jnp.concatenate(
        [
            jnp.sum(pick[j * SLOTS : (j + 1) * SLOTS] * weight[j : j + 1], axis=1, keepdims=True)
            for j in range(local)
        ],
        axis=0,
    )
    high, low_part = split_high(scale)
    lane = lax.broadcasted_iota(jnp.int32, (scale.shape[0], LANES), 1)
    info = jnp.where(lane == 0, high.astype(F32), jnp.where(lane == 1, low_part.astype(F32), 0.0))
    info_ref[...] = info.astype(BF16).reshape(local, SLOTS, LANES)
    shared = dot_nt(shared_ref[...], rows)
    gate, up, raw = shared[:units], shared[units:], raw_ref[...]
    smooth, active = silu_parts(gate)
    hidden_ref[...] = (active * up).astype(BF16)
    back_ref[...] = jnp.concatenate(
        [raw * up * smooth * (1.0 + gate * (1.0 - smooth)), raw * active], axis=0
    ).astype(BF16)


def expert_kernel(
    units, rows_ref, grads_ref, info_ref, in_ref, out_ref, out_rows_ref, back_rows_ref, extra_ref,
    hidden_ref, back_ref,
):
    expert = pl.program_id(0)
    rows, grads = rows_ref[0], grads_ref[0]
    weight_in, weight_out = in_ref[0], out_ref[0]
    gates = dot_nt(weight_in, rows)
    raw = dot_nt(weight_out, grads)
    gate, up = gates[:units], gates[units:]
    lane = lax.broadcasted_iota(jnp.int32, (16, LANES), 1)
    select = (lane < 2).astype(F32).astype(BF16)
    scale = dot_nt(select, info_ref[0])[0:1]
    smooth, active = silu_parts(gate)
    hidden = active * up
    grad_gate = jnp.sum(hidden.astype(BF16).astype(F32) * raw, axis=0, keepdims=True)
    scaled = (hidden * scale).astype(BF16)
    raw = raw * scale
    back = jnp.concatenate(
        [raw * up * smooth * (1.0 + gate * (1.0 - smooth)), raw * active], axis=0
    ).astype(BF16)
    hidden_ref[0] = scaled
    back_ref[0] = back
    out_rows_ref[0] = dot_tn(scaled, weight_out).astype(BF16)
    back_rows_ref[0] = dot_tn(back, weight_in).astype(BF16)
    high, low = split_high(grad_gate)
    row = lax.broadcasted_iota(jnp.int32, (16, grad_gate.shape[1]), 0)
    pair = jnp.where(row == 0, high.astype(F32), jnp.where(row == 1, low.astype(F32), 0.0))
    row = lax.broadcasted_iota(jnp.int32, (16, LANES), 0)
    lane = lax.broadcasted_iota(jnp.int32, (16, LANES), 1)
    place = ((row < 2) & (lane == expert + row * EXPERTS)).astype(F32)
    extra_ref[0] = dot_tn(pair.astype(BF16), place.astype(BF16)).astype(BF16)


def weight_grad_kernel(rows_ref, grads_ref, hidden_ref, back_ref, in_ref, out_ref):
    @pl.when(pl.program_id(1) == 0)
    def _():
        in_ref[0] = dot_nn(back_ref[0], rows_ref[0])
        out_ref[0] = dot_nn(hidden_ref[0], grads_ref[0])

    @pl.when(pl.program_id(1) > 0)
    def _():
        in_ref[0] += dot_nn(back_ref[0], rows_ref[0])
        out_ref[0] += dot_nn(hidden_ref[0], grads_ref[0])


def combine_back_kernel(
    local, pick_ref, slots_ref, extra_ref, gate_ref, router_ref, back_ref, shared_ref,
    tokens_ref, logits_ref,
):
    pick = pick_ref[...]
    flat = local * SLOTS
    merged = dot_tn(extra_ref[...].reshape(flat, LANES), pick)
    grad_gate = merged[:EXPERTS] + merged[EXPERTS:]
    sigmoid, total = gate_ref[0], gate_ref[1]
    mixed = jnp.sum(grad_gate * sigmoid, axis=0, keepdims=True)
    logits = ROUTE_SCALE * (grad_gate / total - mixed / (total * total)) * sigmoid * (1.0 - sigmoid)
    logits = logits.astype(BF16)
    logits_ref[...] = logits
    tokens_ref[...] = (
        dot_tn(pick, slots_ref[...].reshape(flat, slots_ref.shape[2]))
        + dot_tn(back_ref[...], shared_ref[...])
        + dot_tn(logits, router_ref[...])
    ).astype(BF16)


def combine_out_kernel(local, pick_ref, slots_ref, hidden_ref, shared_ref, tokens_ref):
    tokens_ref[...] = (
        dot_tn(pick_ref[...], slots_ref[...].reshape(local * SLOTS, slots_ref.shape[2]))
        + dot_tn(hidden_ref[...], shared_ref[...])
    ).astype(BF16)


def whole(shape):
    return pl.BlockSpec(shape, lambda *_: (0,) * len(shape))


def strip(local, place, width):
    return pl.BlockSpec((local, SLOTS, width), lambda *_: (0, place, 0))


def params(*semantics):
    return pltpu.CompilerParams(
        dimension_semantics=semantics or None, vmem_limit_bytes=56 * 1024 * 1024
    )


def dispatch_grads(place, sequences, local, routes, grads, shared_out, slots):
    count, width = grads.shape
    units = shared_out.shape[0]
    first = slots is None
    operands = [routes, grads, shared_out] + ([] if first else [slots])
    return pl.pallas_call(
        functools.partial(dispatch_grads_kernel, local),
        grid=(1,),
        in_specs=[whole(a.shape) for a in operands[:3]]
        + ([] if first else [pl.BlockSpec(memory_space=pl.ANY)]),
        out_specs=[strip(local, place, width), whole((units, count))],
        out_shape=[
            jax.ShapeDtypeStruct((local, sequences * SLOTS, width), BF16),
            jax.ShapeDtypeStruct((units, count), F32),
        ],
        input_output_aliases={} if first else {3: 0},
        compiler_params=params(),
        name="dispatch_grads",
    )(*operands)


def dispatch_rows(place, sequences, local, routes, rows, router, shared_in, raw, slots, infos):
    count, width = rows.shape
    units = raw.shape[0]
    first = slots is None
    operands = [routes, rows, router, shared_in, raw] + ([] if first else [slots, infos])
    anywhere = pl.BlockSpec(memory_space=pl.ANY)
    return pl.pallas_call(
        functools.partial(dispatch_rows_kernel, local, units),
        grid=(1,),
        in_specs=[whole(a.shape) for a in operands[:5]] + ([] if first else [anywhere, anywhere]),
        out_specs=[
            strip(local, place, width),
            strip(local, place, LANES),
            whole((local * SLOTS, count)),
            whole((2, EXPERTS, count)),
            whole((units, count)),
            whole((2 * units, count)),
        ],
        out_shape=[
            jax.ShapeDtypeStruct((local, sequences * SLOTS, width), BF16),
            jax.ShapeDtypeStruct((local, sequences * SLOTS, LANES), BF16),
            jax.ShapeDtypeStruct((local * SLOTS, count), BF16),
            jax.ShapeDtypeStruct((2, EXPERTS, count), F32),
            jax.ShapeDtypeStruct((units, count), BF16),
            jax.ShapeDtypeStruct((2 * units, count), BF16),
        ],
        input_output_aliases={} if first else {5: 0, 6: 1},
        compiler_params=params(),
        name="dispatch_rows",
    )(*operands)


def tile(*shape):
    return pl.BlockSpec((1,) + shape, lambda j, b: (j, b) + (0,) * (len(shape) - 1))


def lane_tile(*shape):
    return pl.BlockSpec((1,) + shape, lambda j, b: (j, 0, b))


def one(*shape):
    return pl.BlockSpec((1,) + shape, lambda j, b: (j, 0, 0))


def expert_rows(rows, grads, infos, expert_in, expert_out):
    local, slots, width = rows.shape
    units = expert_out.shape[1]
    block = min(slots, SLOT_BLOCK)
    return pl.pallas_call(
        functools.partial(expert_kernel, units),
        grid=(local, slots // block),
        in_specs=[
            tile(block, width),
            tile(block, width),
            tile(block, LANES),
            one(2 * units, width),
            one(units, width),
        ],
        out_specs=[
            tile(block, width),
            tile(block, width),
            tile(block, LANES),
            lane_tile(units, block),
            lane_tile(2 * units, block),
        ],
        out_shape=[
            jax.ShapeDtypeStruct((local, slots, width), BF16),
            jax.ShapeDtypeStruct((local, slots, width), BF16),
            jax.ShapeDtypeStruct((local, slots, LANES), BF16),
            jax.ShapeDtypeStruct((local, units, slots), BF16),
            jax.ShapeDtypeStruct((local, 2 * units, slots), BF16),
        ],
        compiler_params=params("arbitrary", "arbitrary"),
        name="expert_rows",
    )(rows, grads, infos, expert_in, expert_out)


def weight_grads(rows, grads, hidden, back):
    local, slots, width = rows.shape
    units = hidden.shape[1]
    block = min(slots, SLOT_BLOCK)
    return pl.pallas_call(
        weight_grad_kernel,
        grid=(local, slots // block),
        in_specs=[
            tile(block, width),
            tile(block, width),
            lane_tile(units, block),
            lane_tile(2 * units, block),
        ],
        out_specs=[one(2 * units, width), one(units, width)],
        out_shape=[
            jax.ShapeDtypeStruct((local, 2 * units, width), F32),
            jax.ShapeDtypeStruct((local, units, width), F32),
        ],
        compiler_params=params("arbitrary", "arbitrary"),
        name="weight_grads",
    )(rows, grads, hidden, back)


def combine_back(place, local, pick, slots, extra, gates, router, back, shared_in):
    count, width = pick.shape[1], slots.shape[2]
    return pl.pallas_call(
        functools.partial(combine_back_kernel, local),
        grid=(1,),
        in_specs=[
            whole(pick.shape), strip(local, place, width), strip(local, place, LANES),
            whole(gates.shape), whole(router.shape), whole(back.shape), whole(shared_in.shape),
        ],
        out_specs=[whole((count, width)), whole((EXPERTS, count))],
        out_shape=[
            jax.ShapeDtypeStruct((count, width), BF16),
            jax.ShapeDtypeStruct((EXPERTS, count), BF16),
        ],
        compiler_params=params(),
        name="combine_back",
    )(pick, slots, extra, gates, router, back, shared_in)


def combine_out(place, local, pick, slots, hidden, shared_out):
    count, width = pick.shape[1], slots.shape[2]
    return pl.pallas_call(
        functools.partial(combine_out_kernel, local),
        grid=(1,),
        in_specs=[
            whole(pick.shape), strip(local, place, width), whole(hidden.shape),
            whole(shared_out.shape),
        ],
        out_specs=whole((count, width)),
        out_shape=jax.ShapeDtypeStruct((count, width), BF16),
        compiler_params=params(),
        name="combine_out",
    )(pick, slots, hidden, shared_out)


def expert_layer(rows, grads, routes, router, expert_in, expert_out, shared):
    local, units, width = expert_out.shape
    sequences = len(rows)
    shared_units = shared.shape[0] // 3
    shared_in, shared_out = shared[: 2 * shared_units], shared[2 * shared_units :]
    order = list(range(sequences))
    slot_grads, raws = None, [None] * sequences
    for s in order:
        slot_grads, raws[s] = dispatch_grads(
            s, sequences, local, routes[s], grads[s], shared_out, slot_grads
        )
    slot_rows, infos = None, None
    tables = [None] * sequences
    for s in order:
        slot_rows, infos, *tables[s] = dispatch_rows(
            s, sequences, local, routes[s], rows[s], router, shared_in, raws[s], slot_rows, infos
        )
    out_rows, back_rows, extra, hidden, back = expert_rows(
        slot_rows, slot_grads, infos, expert_in.reshape(local, 2 * units, width), expert_out
    )
    back_tokens, logits = [None] * sequences, [None] * sequences
    for s in reversed(order):
        pick, gates, _, shared_back = tables[s]
        back_tokens[s], logits[s] = combine_back(
            s, local, pick, back_rows, extra, gates, router, shared_back, shared_in
        )
    out_tokens = [None] * sequences
    for s in reversed(order):
        pick, _, shared_hidden, _ = tables[s]
        out_tokens[s] = combine_out(s, local, pick, out_rows, shared_hidden, shared_out)
    grad_in, grad_out = weight_grads(slot_rows, slot_grads, hidden, back)
    all_rows = jnp.stack(rows)
    grad_router = contract("set,std->ed", jnp.stack(logits), all_rows)
    grad_shared = jnp.concatenate(
        [
            contract("sft,std->fd", jnp.stack([table[3] for table in tables]), all_rows),
            contract("sft,std->fd", jnp.stack([table[2] for table in tables]), jnp.stack(grads)),
        ]
    )
    return (
        out_tokens,
        back_tokens,
        grad_in.reshape(local, 2, units, width),
        grad_out,
        grad_router,
        grad_shared,
    )


def per_device(
    tokens_in,
    out_grad,
    routes,
    attn_gain,
    kv_gain,
    ffn_gain,
    w_query,
    w_latent,
    w_keyval,
    w_output,
    w_router,
    w_shared_in,
    w_shared_out,
    w_expert_in,
    w_expert_out,
):
    grid = Grid()
    depth = grid.depth
    own_depth = lax.axis_index("tensor")
    own_rows, width = tokens_in.shape
    row_count = own_rows * depth
    local_experts = w_expert_in.shape[0]
    base = lax.axis_index("expert") * local_experts
    stream = jnp.concatenate(grid.gather_depth(tokens_in)).astype(F32)
    full_query = grid.absolute(grid.gather(w_query), 0)
    full_keyval = grid.absolute(grid.gather(w_keyval), 0)
    full_output = grid.absolute(grid.gather(w_output), 1)
    all_grads = grid.gather(jnp.concatenate(grid.gather_depth(out_grad)))
    routes_rel = jnp.concatenate(grid.relative_depth(routes.T, 1), axis=1)
    routes_all = [routes_rel] + [grid.fetch(routes_rel, offset) for offset in grid.offsets[1:]]
    routes_all = [(part - base) % EXPERTS for part in routes_all]
    units = w_shared_out.shape[0] // grid.experts
    padding = ((0, -units % 32), (0, 0))
    padded_units = units + padding[0][1]
    shared_parts = [
        jnp.concatenate([jnp.pad(part, padding) for part in (gate_rows, up_rows, out_rows)])
        for gate_rows, up_rows, out_rows in zip(
            grid.relative(w_shared_in[0].T, 0),
            grid.relative(w_shared_in[1].T, 0),
            grid.relative(w_shared_out, 0),
        )
    ]
    shared = grid.absolute(
        [shared_parts[0]]
        + [
            grid.send(part, offset)
            for offset, part in zip(
                [(-dy, -dx, dc) for dy, dx, dc in grid.offsets[1:]],
                [
                    shared_parts[
                        grid.offsets.index(((-dy) % grid.side, (-dx) % grid.side, dc))
                    ]
                    for dy, dx, dc in grid.offsets[1:]
                ],
            )
        ],
        1,
    )
    position = (
        (own_depth + jnp.arange(row_count) // own_rows) % depth * own_rows
        + jnp.arange(row_count) % own_rows
    )
    local_heads = full_query.shape[1] // (NOPE + ROPE)
    cosine, sine_table = rope_tables(position)
    normed_one, inverse_one = rms_forward(stream, attn_gain)
    normed_one = normed_one.astype(BF16)
    queries = mix_dot(normed_one, full_query).reshape(row_count, local_heads, NOPE + ROPE)
    queries = jnp.concatenate(
        [
            queries[..., :NOPE],
            rotate(queries[..., NOPE:], cosine[:, None, :], sine_table[:, None, :]),
        ],
        axis=-1,
    ).astype(BF16)
    latent = mix_dot(normed_one, w_latent)
    compressed = latent[:, :KVR]
    comp_normed, comp_inverse = rms_forward(compressed, kv_gain)
    comp_normed = comp_normed.astype(BF16)
    key_rope = rotate(latent[:, KVR:], cosine, sine_table).astype(BF16)
    keyval = mix_dot(comp_normed, full_keyval).reshape(row_count, local_heads, NOPE + VD).astype(BF16)
    key_nope = keyval[..., :NOPE]
    values = keyval[..., NOPE:]
    scores = attention_scores(queries, key_nope, key_rope, position)
    top_score = jnp.max(scores, axis=-1, keepdims=True)
    raised = jnp.exp(scores - top_score)
    soft = raised / jnp.sum(raised, axis=-1, keepdims=True)
    soft_low = soft.astype(BF16)
    attended = contract("hqk,khv->qhv", soft_low, values).astype(BF16)
    attended_flat = attended.reshape(row_count, local_heads * VD)
    attention_part = mix_dot(attended_flat, full_output).astype(BF16)
    stream_own = tokens_in.astype(F32)
    residual = stream_own + grid.reduce_depth(split_rows(attention_part, depth))
    normed_two, inverse_two = rms_forward(residual, ffn_gain)
    normed_two = normed_two.astype(BF16)
    all_rows = grid.gather(jnp.concatenate(grid.gather_depth(normed_two)))
    router_rel = jnp.roll(w_router.T, -base, axis=0)
    (
        out_tokens,
        back_tokens,
        grad_expert_in,
        grad_expert_out,
        grad_router_rel,
        grad_shared,
    ) = expert_layer(
        all_rows,
        all_grads,
        routes_all,
        router_rel,
        jnp.swapaxes(w_expert_in, 2, 3),
        w_expert_out,
        shared,
    )
    grad_normed = grid.reduce_depth(
        split_rows(grid.reduce(back_tokens).astype(BF16), depth)
    )
    ffn_total = grid.reduce_depth(split_rows(grid.reduce(out_tokens).astype(BF16), depth))
    block_out = (residual + ffn_total).astype(BF16)
    grad_float = out_grad.astype(F32)
    grad_res_part, grad_ffn_gain = rms_backward(residual, inverse_two, ffn_gain, grad_normed)
    grad_residual = grad_float + grad_res_part
    grad_res_low = jnp.concatenate(grid.gather_depth(grad_residual.astype(BF16)))
    grad_output = contract("tv,td->vd", attended_flat, grad_res_low).astype(BF16)
    sum_output = grid.reduce(grid.relative(grad_output, 1))
    grad_attended = (
        contract("td,vd->tv", grad_res_low, full_output)
        .astype(BF16)
        .reshape(row_count, local_heads, VD)
    )
    softmax_scale = (NOPE + ROPE) ** (-0.5)
    grad_soft = contract("qhv,khv->hqk", grad_attended, values)
    row_delta = jnp.sum(grad_attended.astype(F32) * attended.astype(F32), axis=-1).T
    grad_scores = (soft * (grad_soft - row_delta[..., None]) * softmax_scale).astype(BF16)
    grad_query_nope = contract("hqk,khd->qhd", grad_scores, key_nope)
    grad_query_rope = contract("hqk,kr->qhr", grad_scores, key_rope)
    grad_key_nope = contract("hqk,qhd->khd", grad_scores, queries[..., :NOPE])
    grad_key_rope = contract("hqk,qhr->kr", grad_scores, queries[..., NOPE:])
    grad_values = contract("hqk,qhv->khv", soft_low, grad_attended)
    grad_query_raw = (
        jnp.concatenate(
            [
                grad_query_nope,
                rotate(grad_query_rope, cosine[:, None, :], -sine_table[:, None, :]),
            ],
            axis=-1,
        )
        .reshape(row_count, local_heads * (NOPE + ROPE))
        .astype(BF16)
    )
    grad_query_weight = contract("td,tq->dq", normed_one, grad_query_raw).astype(BF16)
    grad_keyval = (
        jnp.concatenate([grad_key_nope, grad_values], axis=-1)
        .reshape(row_count, local_heads * (NOPE + VD))
        .astype(BF16)
    )
    grad_keyval_weight = contract("tc,tk->ck", comp_normed, grad_keyval).astype(BF16)
    sum_query = grid.reduce(grid.relative(grad_query_weight, 0))
    sum_keyval = grid.reduce(grid.relative(grad_keyval_weight, 0))
    grad_comp_normed = contract("tk,ck->tc", grad_keyval, full_keyval)
    grad_compressed, grad_kv_gain = rms_backward(
        compressed, comp_inverse, kv_gain, grad_comp_normed
    )
    grad_latent_out = jnp.concatenate(
        [grad_compressed, rotate(grad_key_rope, cosine, -sine_table)], axis=-1
    ).astype(BF16)
    grad_latent = contract("tk,td->kd", grad_latent_out, normed_one)
    grad_normed_one = contract("tq,dq->td", grad_query_raw, full_query) + contract(
        "tk,dk->td", grad_latent_out, w_latent
    )
    grad_normed_one = grid.reduce_depth(split_rows(grad_normed_one.astype(BF16), depth))
    inverse_own = inverse_one[:own_rows]
    grad_x_part, grad_attn_gain = rms_backward(stream_own, inverse_own, attn_gain, grad_normed_one)
    grad_in = grad_residual + grad_x_part
    grad_shared_parts = [part.astype(BF16) for part in grid.relative(grad_shared, 1)]
    returned = [grad_shared_parts[0]] + [
        grid.send(part, offset) for offset, part in zip(grid.offsets[1:], grad_shared_parts[1:])
    ]
    returned = [
        returned[grid.offsets.index(((-dy) % grid.side, (-dx) % grid.side, dc))]
        for dy, dx, dc in grid.offsets
    ]
    sum_shared_in = jnp.stack(
        [
            grid.absolute([part[:units] for part in returned], 0).T,
            grid.absolute([part[padded_units : padded_units + units] for part in returned], 0).T,
        ]
    ).astype(F32)
    sum_shared_out = grid.absolute([part[2 * padded_units : 2 * padded_units + units] for part in returned], 0).astype(F32)
    gains = jnp.stack(
        [grad_attn_gain, grad_ffn_gain, jnp.pad(grad_kv_gain, (0, width - KVR))]
    )
    replicated = jnp.concatenate([grad_latent, jnp.roll(grad_router_rel, base, axis=0), gains])
    used = replicated.shape[0]
    padded = -(-used // (16 * grid.experts)) * 16 * grid.experts
    replicated = jnp.pad(replicated, ((0, padded - used), (0, 0))).astype(BF16)
    chunk = grid.reduce(grid.relative(replicated, 0)).astype(BF16)
    part = grid.reduce_depth(grid.relative_depth(chunk, 1)).astype(BF16)
    chunk = grid.absolute_depth(grid.gather_depth(part), 1)
    whole = grid.absolute(grid.gather(chunk), 0).astype(F32)
    sum_latent = whole[: KVR + ROPE].T
    sum_router = whole[KVR + ROPE : KVR + ROPE + EXPERTS].T
    sum_attn_gain = whole[KVR + ROPE + EXPERTS]
    sum_ffn_gain = whole[KVR + ROPE + EXPERTS + 1]
    sum_kv_gain = whole[KVR + ROPE + EXPERTS + 2, :KVR]
    return (
        block_out,
        grad_in,
        sum_attn_gain,
        sum_kv_gain,
        sum_ffn_gain,
        sum_query,
        sum_latent,
        sum_keyval,
        sum_output,
        sum_router,
        sum_shared_in,
        sum_shared_out,
        jnp.swapaxes(grad_expert_in, 2, 3),
        grad_expert_out,
    )


def solution(mesh):
    placed = (
        P(("expert", "tensor"), None),
        P(("expert", "tensor"), None),
        P("expert", None),
        P(),
        P(),
        P(),
        P("expert", "tensor"),
        P(),
        P("expert", "tensor"),
        P("tensor", "expert"),
        P(),
        P(None, "expert", "tensor"),
        P("tensor", "expert"),
        P("expert", None, None, "tensor"),
        P("expert", "tensor", None),
    )
    return jax.shard_map(
        per_device,
        mesh=mesh,
        in_specs=placed,
        out_specs=(
            P(("expert", "tensor"), None),
            P(("expert", "tensor"), None),
            P(),
            P(),
            P(),
            P("expert", "tensor"),
            P(),
            P("expert", "tensor"),
            P("tensor", "expert"),
            P(),
            P(None, "expert", "tensor"),
            P("tensor", "expert"),
            P("expert", None, None, "tensor"),
            P("expert", "tensor", None),
        ),
        check_vma=False,
    )
```

```python
import functools
import math

import jax
import jax.numpy as jnp
from jax import lax
from jax.experimental import pallas as pl
from jax.experimental.pallas import tpu as pltpu
from jax.sharding import PartitionSpec as P

NOPE = 128
ROPE = 64
VD = 128
KVR = 512
EXPERTS = 64
TOP = 6
SLOTS = 32
SLOT_BLOCK = 256
LANES = 128
PARTS = 2
CHUNK_ROWS = 704

EPSILON = 1e-06
ROUTE_SCALE = 2.446
ROPE_BASE = 50000.0
BF16 = jnp.bfloat16
F32 = jnp.float32


def mix_dot(left_side, right_side):
    return jnp.dot(left_side, right_side, preferred_element_type=F32)


def contract(pattern, left_side, right_side):
    return jnp.einsum(pattern, left_side, right_side, preferred_element_type=F32)


def rms_forward(values, gain_vec):
    inverse = lax.rsqrt(jnp.mean(values * values, axis=-1, keepdims=True) + EPSILON)
    return (values * inverse * gain_vec, inverse)


def rms_backward(values, inverse, gain_vec, grad_normed):
    weighted = grad_normed * gain_vec
    grad_values = inverse * weighted - values * (inverse * inverse * inverse) * jnp.mean(
        values * weighted, axis=-1, keepdims=True
    )
    grad_gain = jnp.sum(grad_normed * values * inverse, axis=0)
    return (grad_values, grad_gain)


def rope_tables(position):
    half_rope = ROPE // 2
    frequency = jnp.exp(-jnp.log(ROPE_BASE) * jnp.arange(half_rope).astype(F32) / half_rope)
    angles = position.astype(F32)[:, None] * frequency[None, :]
    return (jnp.cos(angles), jnp.sin(angles))


def rotate(columns, cosine, sine_table):
    half_rope = columns.shape[-1] // 2
    first_half = columns[..., :half_rope]
    second_half = columns[..., half_rope:]
    return jnp.concatenate(
        [
            first_half * cosine - second_half * sine_table,
            first_half * sine_table + second_half * cosine,
        ],
        axis=-1,
    )


def low_add(first, second):
    return (first.astype(F32) + second.astype(F32)).astype(BF16)


class Grid:
    def __init__(self):
        self.experts = lax.axis_size("expert")
        self.depth = lax.axis_size("tensor")
        self.side = math.isqrt(self.experts // 2)
        assert self.side * self.side * 2 == self.experts
        self.offsets = [
            (dy, dx, dc)
            for dy in range(self.side)
            for dx in range(self.side)
            for dc in range(2)
        ]

    def neighbour(self, place, offset):
        side = self.side
        y, x, core = place // (2 * side), place // 2 % side, place % 2
        dy, dx, dc = offset
        return (((y + dy) % side) * side + (x + dx) % side) * 2 + (core + dc) % 2

    def place_of(self, offset):
        return self.neighbour(lax.axis_index("expert"), offset)

    def fetch(self, array, offset):
        pairs = [(self.neighbour(place, offset), place) for place in range(self.experts)]
        return lax.ppermute(array, "expert", pairs)

    def send(self, array, offset):
        pairs = [(place, self.neighbour(place, offset)) for place in range(self.experts)]
        return lax.ppermute(array, "expert", pairs)

    def gather(self, shard):
        if self.side != 2:
            return [shard] + [self.fetch(shard, offset) for offset in self.offsets[1:]]
        half = shard.shape[0] // 2
        along_x = self.fetch(shard, (0, 1, 0))
        along_y = self.fetch(shard, (1, 0, 0))
        pair = self.fetch(shard, (0, 0, 1))
        first = self.fetch(along_x[:half], (1, 0, 0))
        second = self.fetch(along_y[half:], (0, 1, 0))
        pair_x = self.fetch(along_x, (0, 0, 1))
        pair_y = self.fetch(along_y, (0, 0, 1))
        pair_first = self.fetch(first, (0, 0, 1))
        pair_second = self.fetch(second, (0, 0, 1))
        return [
            shard,
            pair,
            along_x,
            pair_x,
            along_y,
            pair_y,
            jnp.concatenate([first, second]),
            jnp.concatenate([pair_first, pair_second]),
        ]

    def reduce(self, chunks):
        if self.side != 2:
            total = chunks[0].astype(F32)
            for offset, chunk in zip(self.offsets[1:], chunks[1:]):
                total = total + self.send(chunk, offset).astype(F32)
            return total
        half = chunks[0].shape[0] // 2
        own = {}
        for place in (6, 2, 4, 0):
            own[place] = low_add(chunks[place], self.send(chunks[place + 1], (0, 0, 1)))
        first = self.send(own[6][:half], (0, 1, 0))
        second = self.send(own[6][half:], (1, 0, 0))
        to_y = jnp.concatenate([low_add(own[4][:half], first), own[4][half:]])
        to_x = jnp.concatenate([own[2][:half], low_add(own[2][half:], second)])
        from_x = self.send(to_x, (0, 1, 0))
        from_y = self.send(to_y, (1, 0, 0))
        return own[0].astype(F32) + from_x.astype(F32) + from_y.astype(F32)

    def gather_small(self, shard):
        along_x = self.fetch(shard, (0, 1, 0))
        along_y = self.fetch(shard, (1, 0, 0))
        near = [shard, along_x, along_y, self.fetch(along_x, (1, 0, 0))]
        return [piece for held in near for piece in (held, self.fetch(held, (0, 0, 1)))]

    def exchange(self, parts):
        pieces = [parts[0]]
        for dy, dx, dc in self.offsets[1:]:
            back = (-dy % self.side, -dx % self.side, dc)
            pieces.append(self.send(parts[self.offsets.index(back)], back))
        return pieces

    def reduce_parts(self, chunks):
        half = chunks[0].shape[0] // 2
        own = {}
        for place in (6, 2, 4, 0):
            own[place] = low_add(chunks[place], self.send(chunks[place + 1], (0, 0, 1)))
        first = self.send(own[6][:half], (0, 1, 0))
        second = self.send(own[6][half:], (1, 0, 0))
        to_y = jnp.concatenate([low_add(own[4][:half], first), own[4][half:]])
        to_x = jnp.concatenate([own[2][:half], low_add(own[2][half:], second)])
        from_x = self.send(to_x, (0, 1, 0))
        from_y = self.send(to_y, (1, 0, 0))
        return [own[0], from_x, from_y], own[6], to_x

    def gather_depth(self, shard):
        depth = self.depth
        return [shard] + [
            lax.ppermute(shard, "tensor", [((i + k) % depth, i) for i in range(depth)])
            for k in range(1, depth)
        ]

    def reduce_depth(self, chunks):
        depth = self.depth
        total = chunks[0].astype(F32)
        for k in range(1, depth):
            total = total + lax.ppermute(
                chunks[k], "tensor", [(i, (i + k) % depth) for i in range(depth)]
            ).astype(F32)
        return total

    def absolute(self, pieces, axis):
        size = pieces[0].shape[axis]
        shape = list(pieces[0].shape)
        shape[axis] = size * self.experts
        whole = jnp.zeros(shape, pieces[0].dtype)
        for offset, piece in zip(self.offsets, pieces):
            whole = lax.dynamic_update_slice_in_dim(
                whole, piece, self.place_of(offset) * size, axis
            )
        return whole

    def relative(self, whole, axis):
        size = whole.shape[axis] // self.experts
        return [
            lax.dynamic_slice_in_dim(whole, self.place_of(offset) * size, size, axis)
            for offset in self.offsets
        ]

    def absolute_depth(self, pieces, axis):
        size = pieces[0].shape[axis]
        shape = list(pieces[0].shape)
        shape[axis] = size * self.depth
        whole = jnp.zeros(shape, pieces[0].dtype)
        own = lax.axis_index("tensor")
        for k, piece in enumerate(pieces):
            whole = lax.dynamic_update_slice_in_dim(
                whole, piece, (own + k) % self.depth * size, axis
            )
        return whole

    def relative_depth(self, whole, axis):
        size = whole.shape[axis] // self.depth
        own = lax.axis_index("tensor")
        return [
            lax.dynamic_slice_in_dim(whole, (own + k) % self.depth * size, size, axis)
            for k in range(self.depth)
        ]


def split_rows(array, count):
    size = array.shape[0] // count
    return [array[i * size : (i + 1) * size] for i in range(count)]


def attention_scores(queries, key_nope, key_rope, position):
    scores = contract("qhd,khd->hqk", queries[..., :NOPE], key_nope) + contract(
        "qhr,kr->hqk", queries[..., NOPE:], key_rope
    )
    scores = scores * ((NOPE + ROPE) ** (-0.5))
    allowed = position[None, :] <= position[:, None]
    return jnp.where(allowed[None], scores, -1e30)


def dot_nn(left, right):
    return lax.dot_general(left, right, (((1,), (0,)), ((), ())), preferred_element_type=F32)


def dot_nt(left, right):
    return lax.dot_general(left, right, (((1,), (1,)), ((), ())), preferred_element_type=F32)


def dot_tn(left, right):
    return lax.dot_general(left, right, (((0,), (0,)), ((), ())), preferred_element_type=F32)


def silu_parts(gate):
    sigmoid = 1.0 / (1.0 + jnp.exp(-gate))
    return sigmoid, gate * sigmoid


def split_high(value):
    high = value.astype(BF16)
    return high, (value - high.astype(F32)).astype(BF16)


def whole(shape):
    return pl.BlockSpec(shape, lambda *_: (0,) * len(shape))


def params(*semantics):
    return pltpu.CompilerParams(
        dimension_semantics=semantics or None, vmem_limit_bytes=56 * 1024 * 1024
    )


ANYWHERE = pl.BlockSpec(memory_space=pl.ANY)


def pick_rows(routes, base, local):
    count = routes.shape[1]
    expert = lax.broadcasted_iota(jnp.int32, (EXPERTS, count), 0) + base
    expert = jnp.where(expert >= EXPERTS, expert - EXPERTS, expert)
    chosen = expert == routes[0:1]
    for k in range(1, routes.shape[0]):
        chosen = chosen | (expert == routes[k : k + 1])
    chosen = chosen.astype(F32)
    rows = max(local, 16)
    earlier = lax.broadcasted_iota(jnp.int32, (count, count), 0) < lax.broadcasted_iota(
        jnp.int32, (count, count), 1
    )
    rank = dot_nn(chosen[:rows].astype(BF16), earlier.astype(F32).astype(BF16))
    rank = jnp.where(chosen[:rows] > 0.5, rank, -1.0)
    slot = lax.broadcasted_iota(jnp.int32, (SLOTS, count), 0).astype(F32)
    parts = [(slot == rank[j : j + 1]).astype(F32) for j in range(local)]
    return jnp.concatenate(parts, axis=0), chosen


def dispatch_grads_kernel(local, base_ref, *refs):
    routes, grads, shared_ref = refs[:2], refs[2:4], refs[4]
    slot_ref, raw_ref = refs[-2:]
    for i in range(2):

        @pl.when(pl.program_id(0) == i)
        def _():
            pick, _ = pick_rows(routes[i][...], base_ref[0], local)
            values = grads[i][...]
            slot_ref[...] = (
                dot_nn(pick.astype(BF16), values).astype(BF16).reshape(slot_ref.shape)
            )
            raw_ref[0] = dot_nt(shared_ref[...], values)


def dispatch_rows_kernel(local, units, base_ref, *refs):
    routes, pieces, side_ref, raw_ref = refs[:2], refs[2:4], refs[4], refs[5]
    slot_ref, info_ref, pick_ref, gate_ref, hidden_ref, back_ref = refs[-6:]
    for i in range(2):

        @pl.when(pl.program_id(0) == i)
        def _():
            pick, chosen = pick_rows(routes[i][...], base_ref[0], local)
            rows = pieces[i][...]
            low = pick.astype(BF16)
            pick_ref[0] = low
            slot_ref[...] = dot_nn(low, rows).astype(BF16).reshape(slot_ref.shape)
            side = dot_nt(side_ref[...], rows)
            gate, up, raw = side[:units], side[units : 2 * units], raw_ref[0]
            sigmoid = chosen / (1.0 + jnp.exp(-side[2 * units :]))
            total = jnp.sum(sigmoid, axis=0, keepdims=True)
            gate_ref[0, 0] = sigmoid
            gate_ref[0, 1] = jnp.broadcast_to(total, sigmoid.shape)
            weight = ROUTE_SCALE * sigmoid / total
            scale = jnp.concatenate(
                [
                    jnp.sum(
                        pick[j * SLOTS : (j + 1) * SLOTS] * weight[j : j + 1],
                        axis=1,
                        keepdims=True,
                    )
                    for j in range(local)
                ],
                axis=0,
            )
            high, low_part = split_high(scale)
            lane = lax.broadcasted_iota(jnp.int32, (scale.shape[0], LANES), 1)
            info = jnp.where(
                lane == 0, high.astype(F32), jnp.where(lane == 1, low_part.astype(F32), 0.0)
            )
            info_ref[...] = info.astype(BF16).reshape(info_ref.shape)
            smooth, active = silu_parts(gate)
            hidden_ref[0] = (active * up).astype(BF16)
            back_ref[0] = jnp.concatenate(
                [raw * up * smooth * (1.0 + gate * (1.0 - smooth)), raw * active], axis=0
            ).astype(BF16)


def expert_raw_kernel(grads_ref, out_ref, raw_ref):
    raw_ref[0] = dot_nt(out_ref[0], grads_ref[0])


def expert_kernel(
    units, rows_ref, info_ref, in_ref, raw_ref, back_rows_ref, extra_ref, hidden_ref, back_ref
):
    expert = pl.program_id(0)
    weight_in = in_ref[0]
    gates = dot_nt(weight_in, rows_ref[0])
    raw = raw_ref[0]
    gate, up = gates[:units], gates[units:]
    lane = lax.broadcasted_iota(jnp.int32, (16, LANES), 1)
    select = (lane < 2).astype(F32).astype(BF16)
    scale = dot_nt(select, info_ref[0])[0:1]
    smooth, active = silu_parts(gate)
    hidden = active * up
    grad_gate = jnp.sum(hidden.astype(BF16).astype(F32) * raw, axis=0, keepdims=True)
    hidden_ref[0] = (hidden * scale).astype(BF16)
    raw = raw * scale
    back = jnp.concatenate(
        [raw * up * smooth * (1.0 + gate * (1.0 - smooth)), raw * active], axis=0
    ).astype(BF16)
    back_ref[0] = back
    back_rows_ref[0] = dot_tn(back, weight_in).astype(BF16)
    high, low = split_high(grad_gate)
    row = lax.broadcasted_iota(jnp.int32, (16, grad_gate.shape[1]), 0)
    pair = jnp.where(row == 0, high.astype(F32), jnp.where(row == 1, low.astype(F32), 0.0))
    row = lax.broadcasted_iota(jnp.int32, (16, LANES), 0)
    lane = lax.broadcasted_iota(jnp.int32, (16, LANES), 1)
    place = ((row < 2) & (lane == expert + row * EXPERTS)).astype(F32)
    extra_ref[0] = dot_tn(pair.astype(BF16), place.astype(BF16)).astype(BF16)


def expert_out_kernel(hidden_ref, out_ref, rows_ref):
    rows_ref[0] = dot_tn(hidden_ref[0], out_ref[0]).astype(BF16)


def weight_grad_kernel(rows_ref, grads_ref, hidden_ref, back_ref, *rest):
    in_ref, out_ref = rest[-2:]

    @pl.when(pl.program_id(1) == 0)
    def _():
        in_ref[0] = dot_nn(back_ref[0], rows_ref[0])
        out_ref[0] = dot_nn(hidden_ref[0], grads_ref[0])

    @pl.when(pl.program_id(1) > 0)
    def _():
        in_ref[0] += dot_nn(back_ref[0], rows_ref[0])
        out_ref[0] += dot_nn(hidden_ref[0], grads_ref[0])


def combine_back_kernel(
    pick_ref, slots_ref, extra_ref, gate_ref, back_ref, side_ref, *rest
):
    first_ref, second_ref, logits_ref, left_ref = rest[-4:]
    piece, part = pl.program_id(0), pl.program_id(1)
    flat = pick_ref.shape[1]
    units = back_ref.shape[1]

    @pl.when(part == 0)
    def _():
        merged = dot_tn(extra_ref[...].reshape(flat, LANES), pick_ref[0])
        grad_gate = merged[:EXPERTS] + merged[EXPERTS:]
        sigmoid, total = gate_ref[0, 0], gate_ref[0, 1]
        mixed = jnp.sum(grad_gate * sigmoid, axis=0, keepdims=True)
        logits = (
            ROUTE_SCALE
            * (grad_gate / total - mixed / (total * total))
            * sigmoid
            * (1.0 - sigmoid)
        ).astype(BF16)
        logits_ref[0] = logits
        left_ref[:units] = back_ref[0]
        left_ref[units:] = logits

    value = (
        dot_tn(pick_ref[0], slots_ref[...].reshape(flat, slots_ref.shape[2]))
        + dot_tn(left_ref[...], side_ref[...])
    ).astype(BF16)

    @pl.when(piece == 0)
    def _():
        first_ref[...] = value

    @pl.when(piece == 1)
    def _():
        second_ref[...] = value


def combine_out_kernel(pick_ref, slots_ref, hidden_ref, shared_ref, first_ref, second_ref):
    value = (
        dot_tn(pick_ref[0], slots_ref[...].reshape(pick_ref.shape[1], slots_ref.shape[2]))
        + dot_tn(hidden_ref[0], shared_ref[...])
    ).astype(BF16)

    @pl.when(pl.program_id(0) == 0)
    def _():
        first_ref[...] = value

    @pl.when(pl.program_id(0) == 1)
    def _():
        second_ref[...] = value


def chain_call(kernel, name, grid, prefetch, operands, in_specs, held, out_specs, out_shape, scratch=()):
    chained = [a for a in held if a is not None]
    at = len(prefetch) + len(operands)
    return pl.pallas_call(
        kernel,
        grid_spec=pltpu.PrefetchScalarGridSpec(
            num_scalar_prefetch=len(prefetch),
            grid=grid,
            in_specs=in_specs + [ANYWHERE] * len(chained),
            out_specs=out_specs,
            scratch_shapes=list(scratch),
        ),
        out_shape=out_shape,
        input_output_aliases={at + i: i for i in range(len(chained))},
        compiler_params=params(*["arbitrary"] * len(grid)),
        name=name,
    )(*prefetch, *operands, *chained)


def dispatch_grads(pair, sequences, local, base, routes, grads, shared_out, held):
    count, width = grads[0].shape
    units = shared_out.shape[0]
    operands = [*routes, *grads, shared_out]
    return chain_call(
        functools.partial(dispatch_grads_kernel, local),
        "dispatch_grads",
        (2,),
        [base],
        operands,
        [whole(a.shape) for a in operands],
        held,
        [
            pl.BlockSpec((local, SLOTS, width), lambda i, *_: (0, 2 * pair + i, 0)),
            pl.BlockSpec((1, units, count), lambda i, *_: (2 * pair + i, 0, 0)),
        ],
        [
            jax.ShapeDtypeStruct((local, sequences * SLOTS, width), BF16),
            jax.ShapeDtypeStruct((sequences, units, count), F32),
        ],
    )


def dispatch_rows(pair, sequences, local, base, routes, rows, side, raws, held):
    count, width = rows[0].shape
    units = raws.shape[1]
    operands = [*routes, *rows, side]
    shapes = [
        ((local * SLOTS, count), BF16),
        ((2, EXPERTS, count), F32),
        ((units, count), BF16),
        ((2 * units, count), BF16),
    ]

    def at(shape):
        return pl.BlockSpec((1,) + shape, lambda i, *_: (2 * pair + i,) + (0,) * len(shape))

    return chain_call(
        functools.partial(dispatch_rows_kernel, local, units),
        "dispatch_rows",
        (2,),
        [base],
        operands + [raws],
        [whole(a.shape) for a in operands] + [at((units, count))],
        held,
        [
            pl.BlockSpec((local, SLOTS, width), lambda i, *_: (0, 2 * pair + i, 0)),
            pl.BlockSpec((local, SLOTS, LANES), lambda i, *_: (0, 2 * pair + i, 0)),
        ]
        + [at(shape) for shape, _ in shapes],
        [
            jax.ShapeDtypeStruct((local, sequences * SLOTS, width), BF16),
            jax.ShapeDtypeStruct((local, sequences * SLOTS, LANES), BF16),
        ]
        + [jax.ShapeDtypeStruct((sequences,) + shape, dtype) for shape, dtype in shapes],
    )


def tile(*shape):
    return pl.BlockSpec((1,) + shape, lambda j, b: (j, b) + (0,) * (len(shape) - 1))


def lane_tile(*shape):
    return pl.BlockSpec((1,) + shape, lambda j, b: (j, 0, b))


def one(*shape):
    return pl.BlockSpec((1,) + shape, lambda j, b: (j, 0, 0))


def expert_raw(grads, expert_out):
    local, slots, width = grads.shape
    units = expert_out.shape[1]
    block = min(slots, SLOT_BLOCK)
    return pl.pallas_call(
        expert_raw_kernel,
        grid=(local, slots // block),
        in_specs=[tile(block, width), one(units, width)],
        out_specs=lane_tile(units, block),
        out_shape=jax.ShapeDtypeStruct((local, units, slots), F32),
        compiler_params=params("arbitrary", "arbitrary"),
        name="expert_raw",
    )(grads, expert_out)


def expert_rows(rows, infos, expert_in, raw):
    local, slots, width = rows.shape
    units = raw.shape[1]
    block = min(slots, SLOT_BLOCK)
    return pl.pallas_call(
        functools.partial(expert_kernel, units),
        grid=(local, slots // block),
        in_specs=[
            tile(block, width),
            tile(block, LANES),
            one(2 * units, width),
            lane_tile(units, block),
        ],
        out_specs=[
            tile(block, width),
            tile(block, LANES),
            lane_tile(units, block),
            lane_tile(2 * units, block),
        ],
        out_shape=[
            jax.ShapeDtypeStruct((local, slots, width), BF16),
            jax.ShapeDtypeStruct((local, slots, LANES), BF16),
            jax.ShapeDtypeStruct((local, units, slots), BF16),
            jax.ShapeDtypeStruct((local, 2 * units, slots), BF16),
        ],
        compiler_params=params("arbitrary", "arbitrary"),
        name="expert_rows",
    )(rows, infos, expert_in, raw)


def expert_out_rows(hidden, expert_out):
    local, units, slots = hidden.shape
    width = expert_out.shape[2]
    block = min(slots, SLOT_BLOCK)
    return pl.pallas_call(
        expert_out_kernel,
        grid=(local, slots // block),
        in_specs=[lane_tile(units, block), one(units, width)],
        out_specs=tile(block, width),
        out_shape=jax.ShapeDtypeStruct((local, slots, width), BF16),
        compiler_params=params("arbitrary", "arbitrary"),
        name="expert_out_rows",
    )(hidden, expert_out)


def weight_grads(start, stop, rows, grads, hidden, back, held):
    local, slots, width = rows.shape
    units = hidden.shape[1]
    block = min(slots, SLOT_BLOCK)

    def moved(spec):
        return pl.BlockSpec(
            spec.block_shape, lambda j, b: (lambda at: (at[0] + start,) + at[1:])(spec.index_map(j, b))
        )

    return chain_call(
        weight_grad_kernel,
        "weight_grads",
        (stop - start, slots // block),
        [],
        [rows, grads, hidden, back],
        [
            moved(spec)
            for spec in (
                tile(block, width),
                tile(block, width),
                lane_tile(units, block),
                lane_tile(2 * units, block),
            )
        ],
        held,
        [moved(one(2 * units, width)), moved(one(units, width))],
        [
            jax.ShapeDtypeStruct((local, 2 * units, width), F32),
            jax.ShapeDtypeStruct((local, units, width), F32),
        ],
    )


def piece_specs(width, part):
    return [
        pl.BlockSpec((width[0], part), lambda i, h: (0, jnp.where(i == 0, h, width[1] - 1))),
        pl.BlockSpec((width[0], part), lambda i, h: (0, jnp.where(i == 0, 0, h))),
    ]


def combine_back(pair, picks, slots, extra, gates, backs, side, held):
    sequences, flat, count = picks.shape
    local, _, width = slots.shape
    part = width // PARTS

    def at(array):
        shape = array.shape[1:]
        return pl.BlockSpec((1,) + shape, lambda i, h: (2 * pair + i,) + (0,) * len(shape))

    def strip(size):
        return pl.BlockSpec((local, SLOTS, size), lambda i, h: (0, 2 * pair + i, 0))

    outs = chain_call(
        lambda *refs: combine_back_kernel(*refs[:6], *refs[-3:-1], refs[-4], refs[-1]),
        "combine_back",
        (2, PARTS),
        [],
        [picks, slots, extra, gates, backs, side],
        [
            at(picks),
            pl.BlockSpec((local, SLOTS, part), lambda i, h: (0, 2 * pair + i, h)),
            strip(LANES),
            at(gates),
            at(backs),
            pl.BlockSpec((side.shape[0], part), lambda i, h: (0, h)),
        ],
        held,
        [pl.BlockSpec((1, EXPERTS, count), lambda i, h: (2 * pair + i, 0, 0))]
        + piece_specs((count, PARTS), part),
        [jax.ShapeDtypeStruct((sequences, EXPERTS, count), BF16)]
        + [jax.ShapeDtypeStruct((count, width), BF16)] * 2,
        [pltpu.VMEM((side.shape[0], count), BF16)],
    )
    return outs[1:], outs[:1]


def combine_out(pair, picks, slots, hiddens, shared_out):
    _, flat, count = picks.shape
    local, _, width = slots.shape
    part = width // PARTS
    units = hiddens.shape[1]
    return pl.pallas_call(
        combine_out_kernel,
        grid=(2, PARTS),
        in_specs=[
            pl.BlockSpec((1, flat, count), lambda i, h: (2 * pair + i, 0, 0)),
            pl.BlockSpec((local, SLOTS, part), lambda i, h: (0, 2 * pair + i, h)),
            pl.BlockSpec((1, units, count), lambda i, h: (2 * pair + i, 0, 0)),
            pl.BlockSpec((units, part), lambda i, h: (0, h)),
        ],
        out_specs=piece_specs((count, PARTS), part),
        out_shape=[jax.ShapeDtypeStruct((count, width), BF16)] * 2,
        compiler_params=params("arbitrary", "arbitrary"),
        name="combine_out",
    )(picks, slots, hiddens, shared_out)


def side_grads_kernel(sequences, block_ref, *refs):
    rows, grads, rest = refs[:sequences], refs[sequences : 2 * sequences], refs[2 * sequences :]
    logits_ref, hidden_ref, back_ref, first_ref, *parts, router_ref, left_ref, in_ref, out_ref = rest
    units = hidden_ref.shape[1]
    for s in range(sequences):
        left_ref[: 2 * units] = back_ref[s]
        left_ref[2 * units :] = logits_ref[s]
        value = dot_nn(left_ref[...], rows[s][...])
        other = dot_nn(hidden_ref[s], grads[s][...])
        if s == 0:
            in_ref[...] = value
            out_ref[...] = other
        else:
            in_ref[...] += value
            out_ref[...] += other
    shards, columns = len(parts), parts[0].shape[1]
    for k in range(shards):
        at = pl.ds(pl.multiple_of(block_ref[k] * columns, columns), columns)
        parts[k][: 2 * units] = in_ref[: 2 * units, at].astype(BF16)
        parts[k][2 * units :] = out_ref[:, at].astype(BF16)
    local = EXPERTS // shards
    for k in range(shards):
        start = first_ref[0] + k * local
        start = jnp.where(start >= EXPERTS, start - EXPERTS, start)
        router_ref[pl.ds(pl.multiple_of(start, local), local)] = in_ref[
            2 * units + k * local : 2 * units + (k + 1) * local
        ]


def side_grads(blocks, base, rows, grads, logits, hiddens, backs):
    sequences = len(rows)
    count, width = rows[0].shape
    units = hiddens.shape[1]
    shards = blocks.shape[0]
    operands = [*rows, *grads, logits, hiddens, backs]
    return pl.pallas_call(
        functools.partial(side_grads_kernel, sequences),
        grid_spec=pltpu.PrefetchScalarGridSpec(
            num_scalar_prefetch=1,
            grid=(1,),
            in_specs=[whole(a.shape) for a in operands]
            + [pl.BlockSpec(memory_space=pltpu.SMEM)],
            out_specs=[whole((3 * units, width // shards))] * shards + [whole((EXPERTS, width))],
            scratch_shapes=[
                pltpu.VMEM((2 * units + EXPERTS, count), BF16),
                pltpu.VMEM((2 * units + EXPERTS, width), F32),
                pltpu.VMEM((units, width), F32),
            ],
        ),
        out_shape=[jax.ShapeDtypeStruct((3 * units, width // shards), BF16)] * shards
        + [jax.ShapeDtypeStruct((EXPERTS, width), F32)],
        compiler_params=params("arbitrary"),
        name="side_grads",
    )(blocks, *operands, base)


def join_columns_kernel(block_ref, *refs):
    pieces, router_ref, side_ref, out_ref = refs[:-3], refs[-3], refs[-2], refs[-1]
    units = out_ref.shape[0]
    columns = pieces[0].shape[1]
    for k, piece in enumerate(pieces):
        at = pl.ds(pl.multiple_of(block_ref[k] * columns, columns), columns)
        side_ref[: 2 * units, at] = piece[: 2 * units]
        out_ref[:, at] = piece[2 * units :]
    side_ref[2 * units :] = router_ref[...]


def join_rows_kernel(units, block_ref, *refs):
    parts, in_ref, out_ref = refs[:-2], refs[-2], refs[-1]
    padded = parts[0].shape[0] // 3
    for k, part in enumerate(parts):
        at = pl.ds(pl.multiple_of(block_ref[k] * units, 8), units)
        value = part[...].astype(F32)
        in_ref[0, at] = value[:units]
        in_ref[1, at] = value[padded : padded + units]
        out_ref[at] = value[2 * padded : 2 * padded + units]


def sum_split_kernel(depth_ref, own_ref, x_ref, y_ref, *outs):
    size = outs[0].shape[0]
    for k, out in enumerate(outs):
        at = pl.ds(pl.multiple_of(depth_ref[k] * size, size), size)
        out[...] = (
            own_ref[at].astype(F32) + x_ref[at].astype(F32) + y_ref[at].astype(F32)
        ).astype(BF16)


def join_depth_kernel(depth_ref, *refs):
    pieces, out_ref = refs[:-1], refs[-1]
    size = pieces[0].shape[0]
    for k, piece in enumerate(pieces):
        out_ref[pl.ds(pl.multiple_of(depth_ref[k] * size, size), size)] = piece[...]


def replicated_kernel(used, block_ref, *refs):
    chunks, latent_ref, router_ref, gains_ref = refs[:-3], refs[-3], refs[-2], refs[-1]
    columns = chunks[0].shape[1]
    for k, chunk in enumerate(chunks):
        at = pl.ds(pl.multiple_of(block_ref[k] * columns, columns), columns)
        latent_ref[:, at] = chunk[:used].astype(F32)
        router_ref[:, at] = chunk[used : used + EXPERTS].astype(F32)
        gains_ref[:, at] = chunk[used + EXPERTS : used + EXPERTS + 16].astype(F32)


def rope_turn(first, second, cosine, sine):
    return first * cosine - second * sine, first * sine + second * cosine


def unit_rows(pieces):
    values = jnp.concatenate([piece[...] for piece in pieces], axis=0).astype(F32)
    inverse = lax.rsqrt(jnp.mean(values * values, axis=-1, keepdims=True) + EPSILON)
    return values * inverse


def latent_kernel(depth, *refs):
    pieces = refs[:depth]
    gain_ref, weight_ref, kv_gain_ref, cosine_ref, sine_ref = refs[depth : depth + 5]
    normed_ref, comp_ref, low_ref, key_ref = refs[depth + 5 :]
    normed = (unit_rows(pieces) * gain_ref[...]).astype(BF16)
    normed_ref[...] = normed
    latent = dot_nt(normed, weight_ref[...])
    compressed = latent[:, :KVR]
    comp_ref[...] = compressed
    inverse = lax.rsqrt(jnp.mean(compressed * compressed, axis=-1, keepdims=True) + EPSILON)
    low_ref[...] = (compressed * inverse * kv_gain_ref[...]).astype(BF16)
    first, second = rope_turn(
        latent[:, KVR : KVR + LANES], latent[:, KVR + LANES :], cosine_ref[...], sine_ref[...]
    )
    key_ref[...] = jnp.concatenate([first, second], axis=1).astype(BF16)


def head_mask(head):
    lane = lax.broadcasted_iota(jnp.int32, (1, LANES), 1)
    return ((lane // (ROPE // 2)) == head).astype(F32)


def keyval_weight(block_ref, packs, whole_ref, queries):
    share = KVR // len(packs)
    count = packs[0].shape[0] // share
    columns = whole_ref.shape[1] // count
    for k, pack in enumerate(packs):
        start = pl.multiple_of(block_ref[k] * share, share)
        for i in range(count):
            whole_ref[pl.ds(start, share), i * columns : (i + 1) * columns] = pack[
                i * share : (i + 1) * share, queries : queries + columns
            ]


def attention_kernel(heads, block_ref, *refs):
    shards = len(refs) - 13
    packs = refs[:shards]
    normed_ref, low_ref, key_ref, bias_ref, cosine_ref, sine_ref = refs[shards : shards + 6]
    query_ref, keyval_ref, soft_ref, attended_ref, part_ref, total_ref, weight_ref = refs[
        shards + 6 :
    ]
    share = packs[0].shape[0]
    nope = heads * NOPE
    queries = heads * (NOPE + ROPE)
    keyval_columns = keyval_ref.shape[1] * (KVR // shards) // share
    keyval_weight(block_ref, packs, weight_ref, queries)
    for k, pack in enumerate(packs):
        start = pl.multiple_of(block_ref[k] * share, share)
        value = dot_nn(normed_ref[:, pl.ds(start, share)], pack[:, :queries])
        if k == 0:
            total_ref[...] = value
        else:
            total_ref[...] += value
    keyval_ref[...] = dot_nn(low_ref[...], weight_ref[...]).astype(BF16)
    first, second = rope_turn(
        total_ref[:, nope : nope + LANES], total_ref[:, nope + LANES :], cosine_ref[...], sine_ref[...]
    )
    query_ref[:, :nope] = total_ref[:, :nope].astype(BF16)
    query_ref[:, nope : nope + LANES] = first.astype(BF16)
    query_ref[:, nope + LANES :] = second.astype(BF16)
    for head in range(heads):
        mask = head_mask(head)
        at = head * (NOPE + VD)
        turned = jnp.concatenate([first * mask, second * mask], axis=1).astype(BF16)
        scores = dot_nt(
            query_ref[:, head * NOPE : (head + 1) * NOPE], keyval_ref[:, at : at + NOPE]
        ) + dot_nt(turned, key_ref[...])
        scores = scores * ((NOPE + ROPE) ** (-0.5)) + bias_ref[...]
        raised = jnp.exp(scores - jnp.max(scores, axis=-1, keepdims=True))
        soft = raised / jnp.sum(raised, axis=-1, keepdims=True)
        soft_ref[head] = soft
        attended_ref[:, head * VD : (head + 1) * VD] = dot_nn(
            soft.astype(BF16), keyval_ref[:, at + NOPE : at + NOPE + VD]
        ).astype(BF16)
    output = queries + keyval_columns
    columns = part_ref.shape[1] // shards
    for k, pack in enumerate(packs):
        start = pl.multiple_of(block_ref[k] * columns, columns)
        value = dot_nn(attended_ref[:, :share], pack[:, output : output + columns])
        for i in range(1, heads * VD // share):
            value += dot_nn(
                attended_ref[:, i * share : (i + 1) * share],
                pack[:, output + i * columns : output + (i + 1) * columns],
            )
        part_ref[:, pl.ds(start, columns)] = value.astype(BF16)


def attention_back_kernel(heads, depth, block_ref, *refs):
    shards = (len(refs) - 2 * depth - 22) // 2
    packs, refs = refs[:shards], refs[shards:]
    tokens, refs = refs[:depth], refs[depth:]
    grads, refs = refs[:depth], refs[depth:]
    (
        query_ref, keyval_ref, key_ref, soft_ref, attended_ref, comp_ref, low_ref, normed_ref,
        latent_ref, kv_gain_ref, cosine_ref, sine_ref, router_ref, ffn_gain_ref,
        grad_query_ref, grad_keyval_ref, grad_normed_ref, *chunk_refs,
        gains_ref, grad_attended_ref, weight_ref, back_ref, stage_ref,
    ) = refs
    share = packs[0].shape[0]
    own = tokens[0].shape[0]
    nope = heads * NOPE
    queries = heads * (NOPE + ROPE)
    keyval_columns = keyval_ref.shape[1] * (KVR // shards) // share
    output = queries + keyval_columns
    columns = normed_ref.shape[1] // shards
    scale = (NOPE + ROPE) ** (-0.5)
    for z, piece in enumerate(grads):
        stage_ref[z * own : (z + 1) * own] = piece[...]
    blocks = heads * VD // share
    for i in range(blocks):
        value = None
        for k, pack in enumerate(packs):
            start = pl.multiple_of(block_ref[k] * columns, columns)
            part = dot_nt(
                stage_ref[:, pl.ds(start, columns)],
                pack[:, output + i * columns : output + (i + 1) * columns],
            )
            value = part if value is None else value + part
        grad_attended_ref[:, i * share : (i + 1) * share] = value.astype(BF16)
    cosine, sine = cosine_ref[...], sine_ref[...]
    turn_first, turn_second = None, None
    key_turn = None
    for head in range(heads):
        mask = head_mask(head)
        at = head * (NOPE + VD)
        soft = soft_ref[head]
        attended = attended_ref[:, head * VD : (head + 1) * VD]
        grad = grad_attended_ref[:, head * VD : (head + 1) * VD]
        delta = jnp.sum(grad.astype(F32) * attended.astype(F32), axis=-1, keepdims=True)
        grad_soft = dot_nt(grad, keyval_ref[:, at + NOPE : at + NOPE + VD])
        scores = (soft * (grad_soft - delta) * scale).astype(BF16)
        query = query_ref[:, head * NOPE : (head + 1) * NOPE]
        grad_query_ref[:, head * NOPE : (head + 1) * NOPE] = dot_nn(
            scores, keyval_ref[:, at : at + NOPE]
        ).astype(BF16)
        turned = dot_nn(scores, key_ref[...])
        first, second = turned[:, :LANES] * mask, turned[:, LANES:] * mask
        turn_first = first if turn_first is None else turn_first + first
        turn_second = second if turn_second is None else turn_second + second
        wide = jnp.concatenate([mask, mask], axis=1)
        masked = (query_ref[:, nope:].astype(F32) * wide).astype(BF16)
        part = dot_tn(scores, masked)
        key_turn = part if key_turn is None else key_turn + part
        grad_keyval_ref[:, at : at + NOPE] = dot_tn(scores, query).astype(BF16)
        grad_keyval_ref[:, at + NOPE : at + NOPE + VD] = dot_tn(soft.astype(BF16), grad).astype(BF16)
    first, second = rope_turn(turn_first, turn_second, cosine, -sine)
    grad_query_ref[:, nope : nope + LANES] = first.astype(BF16)
    grad_query_ref[:, nope + LANES :] = second.astype(BF16)
    keyval_weight(block_ref, packs, weight_ref, queries)
    grad_comp = dot_nt(grad_keyval_ref[...], weight_ref[...])
    compressed = comp_ref[...]
    inverse = lax.rsqrt(jnp.mean(compressed * compressed, axis=-1, keepdims=True) + EPSILON)
    weighted = grad_comp * kv_gain_ref[...]
    grad_compressed = inverse * weighted - compressed * (inverse * inverse * inverse) * jnp.mean(
        compressed * weighted, axis=-1, keepdims=True
    )
    gains_ref[...] = jnp.zeros_like(gains_ref)
    gains_ref[2:3, :KVR] = jnp.sum(grad_comp * compressed * inverse, axis=0, keepdims=True)
    back_ref[:, :KVR] = grad_compressed.astype(BF16)
    first, second = rope_turn(key_turn[:, :LANES], key_turn[:, LANES:], cosine, -sine)
    back_ref[:, KVR : KVR + LANES] = first.astype(BF16)
    back_ref[:, KVR + LANES :] = second.astype(BF16)
    unit = unit_rows(tokens)
    half = ROPE // 2
    for k, pack in enumerate(packs):
        start = pl.multiple_of(block_ref[k] * columns, columns)
        value = dot_nt(grad_query_ref[...], pack[:, :queries])
        value += dot_nn(back_ref[...], latent_ref[:, pl.ds(start, columns)])
        grad_normed_ref[:, pl.ds(start, columns)] = value.astype(BF16)
        weight = dot_tn(back_ref[...], normed_ref[:, pl.ds(start, columns)])
        turns = [
            sum(weight[KVR + i * LANES + j * half : KVR + i * LANES + (j + 1) * half] for j in range(heads))
            for i in range(2)
        ]
        chunk_refs[k][: KVR + ROPE] = jnp.concatenate([weight[:KVR]] + turns, axis=0).astype(BF16)
    gains_ref[0:1, :] = jnp.sum(grad_normed_ref[...].astype(F32) * unit, axis=0, keepdims=True)
    gains_ref[1:2, :] = ffn_gain_ref[...]
    used = KVR + ROPE
    for k in range(shards):
        at = pl.ds(pl.multiple_of(block_ref[k] * columns, columns), columns)
        chunk_refs[k][used : used + EXPERTS] = router_ref[:, at].astype(BF16)
        rows = [gains_ref[:2, at]]
        rows += [gains_ref[2:3, i * columns : (i + 1) * columns] for i in range(KVR // columns)]
        filled = 2 + KVR // columns
        rows.append(jnp.zeros((CHUNK_ROWS - used - EXPERTS - filled, columns), F32))
        chunk_refs[k][used + EXPERTS :] = jnp.concatenate(rows, axis=0).astype(BF16)


def attention_weights_kernel(heads, depth, block_ref, *refs):
    grads, refs = refs[:depth], refs[depth:]
    normed_ref, low_ref, attended_ref, query_ref, keyval_ref, *packs, stage_ref, whole_ref = refs
    own = grads[0].shape[0]
    shards, share = len(packs), packs[0].shape[0]
    queries = heads * (NOPE + ROPE)
    columns = normed_ref.shape[1] // shards
    part = KVR // shards
    count = share // part
    keyval_columns = keyval_ref.shape[1] // count
    output = queries + keyval_columns
    for z, piece in enumerate(grads):
        stage_ref[z * own : (z + 1) * own] = piece[...]
    whole_ref[...] = dot_tn(low_ref[...], keyval_ref[...]).astype(BF16)
    for k in range(shards):
        start = pl.multiple_of(block_ref[k] * columns, columns)
        packs[k][:, :queries] = dot_tn(
            normed_ref[:, pl.ds(start, columns)], query_ref[...]
        ).astype(BF16)
        rows = pl.ds(pl.multiple_of(block_ref[k] * part, part), part)
        for i in range(count):
            packs[k][i * part : (i + 1) * part, queries:output] = whole_ref[
                rows, i * keyval_columns : (i + 1) * keyval_columns
            ]
        value = dot_tn(attended_ref[...], stage_ref[:, pl.ds(start, columns)]).astype(BF16)
        for i in range(heads * VD // share):
            packs[k][:, output + i * columns : output + (i + 1) * columns] = value[
                i * share : (i + 1) * share
            ]


def vmem_call(kernel, name, blocks, operands, out_shape, scratch):
    if blocks is None:
        return pl.pallas_call(
            kernel,
            out_shape=out_shape,
            scratch_shapes=scratch,
            compiler_params=params(),
            name=name,
        )(*operands)
    return pl.pallas_call(
        kernel,
        grid_spec=pltpu.PrefetchScalarGridSpec(
            num_scalar_prefetch=1,
            grid=(1,),
            in_specs=[whole(a.shape) for a in operands],
            out_specs=[whole(a.shape) for a in out_shape],
            scratch_shapes=scratch,
        ),
        out_shape=out_shape,
        compiler_params=params("arbitrary"),
        name=name,
    )(blocks, *operands)


def latent_rows(pieces, gain, weight, kv_gain, cosine, sine):
    count = pieces[0].shape[0] * len(pieces)
    width = pieces[0].shape[1]
    return vmem_call(
        functools.partial(latent_kernel, len(pieces)),
        "latent_rows",
        None,
        [*pieces, gain[None], weight, kv_gain[None], cosine, sine],
        [
            jax.ShapeDtypeStruct((count, width), BF16),
            jax.ShapeDtypeStruct((count, KVR), F32),
            jax.ShapeDtypeStruct((count, KVR), BF16),
            jax.ShapeDtypeStruct((count, 2 * LANES), BF16),
        ],
        [],
    )


def attention_forward(heads, blocks, packs, normed, low, key, bias, cosine, sine):
    count, width = normed.shape
    queries = heads * (NOPE + ROPE)
    keyval = heads * (NOPE + VD)
    return vmem_call(
        functools.partial(attention_kernel, heads),
        "attention_forward",
        blocks,
        [*packs, normed, low, key, bias, cosine, sine],
        [
            jax.ShapeDtypeStruct((count, queries), BF16),
            jax.ShapeDtypeStruct((count, keyval), BF16),
            jax.ShapeDtypeStruct((heads, count, count), F32),
            jax.ShapeDtypeStruct((count, heads * VD), BF16),
            jax.ShapeDtypeStruct((count, width), BF16),
        ],
        [pltpu.VMEM((count, queries), F32), pltpu.VMEM((KVR, keyval), BF16)],
    )


def attention_backward(
    heads, blocks, packs, tokens, grads, saved, latent, kv_gain, cosine, sine, router, ffn_gain
):
    query, keyval, key, soft, attended, compressed, low, normed = saved
    count, width = normed.shape
    shards = len(packs)
    return vmem_call(
        functools.partial(attention_back_kernel, heads, len(tokens)),
        "attention_backward",
        blocks,
        [
            *packs, *tokens, *grads, query, keyval, key, soft, attended, compressed, low, normed,
            latent, kv_gain[None], cosine, sine, router, ffn_gain[None],
        ],
        [
            jax.ShapeDtypeStruct(query.shape, BF16),
            jax.ShapeDtypeStruct(keyval.shape, BF16),
            jax.ShapeDtypeStruct((count, width), BF16),
        ]
        + [jax.ShapeDtypeStruct((CHUNK_ROWS, width // shards), BF16)] * shards,
        [
            pltpu.VMEM((8, width), F32),
            pltpu.VMEM((count, heads * VD), BF16),
            pltpu.VMEM((KVR, keyval.shape[1]), BF16),
            pltpu.VMEM((count, latent.shape[0]), BF16),
            pltpu.VMEM((count, width), BF16),
        ],
    )


def attention_weights(heads, blocks, shape, grads, normed, low, attended, grad_query, grad_keyval):
    count, width = normed.shape
    shards = blocks.shape[0]
    return vmem_call(
        functools.partial(attention_weights_kernel, heads, len(grads)),
        "attention_weights",
        blocks,
        [*grads, normed, low, attended, grad_query, grad_keyval],
        [jax.ShapeDtypeStruct(shape, BF16)] * shards,
        [pltpu.VMEM((count, width), BF16), pltpu.VMEM((KVR, grad_keyval.shape[1]), BF16)],
    )


def query_order(heads):
    size, half = NOPE + ROPE, ROPE // 2
    pieces = []
    for start, stop in ((0, NOPE), (NOPE, NOPE + half), (NOPE + half, size)):
        pieces += [(head * size + start, head * size + stop) for head in range(heads)]
    return pieces


def pack_weights(query, keyval, output, heads):
    share, columns = query.shape[0], output.shape[1]
    part = keyval.shape[0]
    count = share // part
    wide = keyval.shape[1] // count
    return jnp.concatenate(
        [query[:, start:stop] for start, stop in query_order(heads)]
        + [
            jnp.concatenate([keyval[:, i * wide : (i + 1) * wide] for i in range(count)], axis=0)
        ]
        + [output[i * share : (i + 1) * share] for i in range(output.shape[0] // share)],
        axis=1,
    )


def unpack_weights(pack, keyval_shape, output_shape, heads):
    size, half = NOPE + ROPE, ROPE // 2
    queries = heads * size
    share = pack.shape[0]
    part = keyval_shape[0]
    count = share // part
    wide = keyval_shape[1] // count
    nope = heads * NOPE
    query = []
    for head in range(heads):
        query += [
            pack[:, head * NOPE : (head + 1) * NOPE],
            pack[:, nope + head * half : nope + (head + 1) * half],
            pack[:, nope + (heads + head) * half : nope + (heads + head + 1) * half],
        ]
    keyval = jnp.concatenate(
        [pack[i * part : (i + 1) * part, queries : queries + wide] for i in range(count)], axis=1
    )
    at, columns = queries + wide, output_shape[1]
    output = jnp.concatenate(
        [
            pack[:, at + i * columns : at + (i + 1) * columns]
            for i in range(output_shape[0] // share)
        ],
        axis=0,
    )
    return jnp.concatenate(query, axis=1), keyval, output


def expert_layer(base, rows, grads, routes, router, expert_in, expert_out, shared):
    local, units, width = expert_out.shape
    sequences = len(rows)
    pairs = range(sequences // 2)
    shared_units = shared.shape[0] // 3
    side = jnp.concatenate([shared[: 2 * shared_units], router])
    shared_out = shared[2 * shared_units :]
    held = [None, None]
    for m in pairs:
        at = slice(2 * m, 2 * m + 2)
        held = dispatch_grads(
            m, sequences, local, base, routes[at], grads[at], shared_out, held
        )
    slot_grads, shared_raw = held
    raw = expert_raw(slot_grads, expert_out)
    held = [None] * 6
    for m in pairs:
        at = slice(2 * m, 2 * m + 2)
        held = dispatch_rows(
            m, sequences, local, base, routes[at], rows[at], side, shared_raw, held
        )
    slot_rows, infos, picks, gates, shared_hidden, shared_back = held
    back_rows, extra, hidden, back = expert_rows(
        slot_rows, infos, expert_in.reshape(local, 2 * units, width), raw
    )
    back_tokens, logits = [], [None]
    for m in pairs:
        tokens, logits = combine_back(
            m, picks, back_rows, extra, gates, shared_back, side, logits
        )
        back_tokens += tokens
    out_rows = expert_out_rows(hidden, expert_out)
    out_tokens = []
    for m in pairs:
        out_tokens += combine_out(m, picks, out_rows, shared_hidden, shared_out)
    grad_in, grad_out = weight_grads(
        0, local, slot_rows, slot_grads, hidden, back, [None, None]
    )
    all_rows = jnp.stack(rows)
    grad_router = contract("set,std->ed", logits[0], all_rows)
    grad_shared = jnp.concatenate(
        [
            contract("sft,std->fd", shared_back, all_rows),
            contract("sft,std->fd", shared_hidden, jnp.stack(grads)),
        ]
    )
    return (
        out_tokens,
        back_tokens,
        grad_in.reshape(local, 2, units, width),
        grad_out,
        grad_router,
        grad_shared,
    )


def general_device(
    tokens_in,
    out_grad,
    routes,
    attn_gain,
    kv_gain,
    ffn_gain,
    w_query,
    w_latent,
    w_keyval,
    w_output,
    w_router,
    w_shared_in,
    w_shared_out,
    w_expert_in,
    w_expert_out,
):
    grid = Grid()
    depth = grid.depth
    own_depth = lax.axis_index("tensor")
    own_rows, width = tokens_in.shape
    row_count = own_rows * depth
    local_experts = w_expert_in.shape[0]
    base = lax.axis_index("expert") * local_experts
    stream = jnp.concatenate(grid.gather_depth(tokens_in)).astype(F32)
    full_query = grid.absolute(grid.gather(w_query), 0)
    full_keyval = grid.absolute(grid.gather(w_keyval), 0)
    full_output = grid.absolute(grid.gather(w_output), 1)
    all_grads = grid.gather(jnp.concatenate(grid.gather_depth(out_grad)))
    routes_rel = jnp.concatenate(grid.relative_depth(routes.T, 1), axis=1)
    routes_all = [routes_rel] + [grid.fetch(routes_rel, offset) for offset in grid.offsets[1:]]
    units = w_shared_out.shape[0] // grid.experts
    padding = ((0, -units % 32), (0, 0))
    padded_units = units + padding[0][1]
    shared_parts = [
        jnp.concatenate([jnp.pad(part, padding) for part in parts])
        for parts in zip(
            grid.relative(w_shared_in[0].T, 0),
            grid.relative(w_shared_in[1].T, 0),
            grid.relative(w_shared_out, 0),
        )
    ]
    shared = grid.absolute(grid.exchange(shared_parts), 1)
    position = (
        (own_depth + jnp.arange(row_count) // own_rows) % depth * own_rows
        + jnp.arange(row_count) % own_rows
    )
    local_heads = full_query.shape[1] // (NOPE + ROPE)
    cosine, sine_table = rope_tables(position)
    normed_one, inverse_one = rms_forward(stream, attn_gain)
    normed_one = normed_one.astype(BF16)
    queries = mix_dot(normed_one, full_query).reshape(row_count, local_heads, NOPE + ROPE)
    queries = jnp.concatenate(
        [
            queries[..., :NOPE],
            rotate(queries[..., NOPE:], cosine[:, None, :], sine_table[:, None, :]),
        ],
        axis=-1,
    ).astype(BF16)
    latent = mix_dot(normed_one, w_latent)
    compressed = latent[:, :KVR]
    comp_normed, comp_inverse = rms_forward(compressed, kv_gain)
    comp_normed = comp_normed.astype(BF16)
    key_rope = rotate(latent[:, KVR:], cosine, sine_table).astype(BF16)
    keyval = mix_dot(comp_normed, full_keyval).reshape(row_count, local_heads, NOPE + VD).astype(BF16)
    key_nope = keyval[..., :NOPE]
    values = keyval[..., NOPE:]
    scores = attention_scores(queries, key_nope, key_rope, position)
    top_score = jnp.max(scores, axis=-1, keepdims=True)
    raised = jnp.exp(scores - top_score)
    soft = raised / jnp.sum(raised, axis=-1, keepdims=True)
    soft_low = soft.astype(BF16)
    attended = contract("hqk,khv->qhv", soft_low, values).astype(BF16)
    attended_flat = attended.reshape(row_count, local_heads * VD)
    attention_part = mix_dot(attended_flat, full_output).astype(BF16)
    stream_own = tokens_in.astype(F32)
    residual = stream_own + grid.reduce_depth(split_rows(attention_part, depth))
    normed_two, inverse_two = rms_forward(residual, ffn_gain)
    normed_two = normed_two.astype(BF16)
    all_rows = grid.gather(jnp.concatenate(grid.gather_depth(normed_two)))
    router_rel = jnp.roll(w_router.T, -base, axis=0)
    (
        out_tokens,
        back_tokens,
        grad_expert_in,
        grad_expert_out,
        grad_router_rel,
        grad_shared,
    ) = expert_layer(
        base.astype(jnp.int32)[None],
        all_rows,
        all_grads,
        routes_all,
        router_rel,
        jnp.swapaxes(w_expert_in, 2, 3),
        w_expert_out,
        shared,
    )
    grad_normed = grid.reduce_depth(
        split_rows(grid.reduce(back_tokens).astype(BF16), depth)
    )
    ffn_total = grid.reduce_depth(split_rows(grid.reduce(out_tokens).astype(BF16), depth))
    block_out = (residual + ffn_total).astype(BF16)
    grad_float = out_grad.astype(F32)
    grad_res_part, grad_ffn_gain = rms_backward(residual, inverse_two, ffn_gain, grad_normed)
    grad_residual = grad_float + grad_res_part
    grad_res_low = jnp.concatenate(grid.gather_depth(grad_residual.astype(BF16)))
    grad_output = contract("tv,td->vd", attended_flat, grad_res_low).astype(BF16)
    sum_output = grid.reduce(grid.relative(grad_output, 1))
    grad_attended = (
        contract("td,vd->tv", grad_res_low, full_output)
        .astype(BF16)
        .reshape(row_count, local_heads, VD)
    )
    softmax_scale = (NOPE + ROPE) ** (-0.5)
    grad_soft = contract("qhv,khv->hqk", grad_attended, values)
    row_delta = jnp.sum(grad_attended.astype(F32) * attended.astype(F32), axis=-1).T
    grad_scores = (soft * (grad_soft - row_delta[..., None]) * softmax_scale).astype(BF16)
    grad_query_nope = contract("hqk,khd->qhd", grad_scores, key_nope)
    grad_query_rope = contract("hqk,kr->qhr", grad_scores, key_rope)
    grad_key_nope = contract("hqk,qhd->khd", grad_scores, queries[..., :NOPE])
    grad_key_rope = contract("hqk,qhr->kr", grad_scores, queries[..., NOPE:])
    grad_values = contract("hqk,qhv->khv", soft_low, grad_attended)
    grad_query_raw = (
        jnp.concatenate(
            [
                grad_query_nope,
                rotate(grad_query_rope, cosine[:, None, :], -sine_table[:, None, :]),
            ],
            axis=-1,
        )
        .reshape(row_count, local_heads * (NOPE + ROPE))
        .astype(BF16)
    )
    grad_query_weight = contract("td,tq->dq", normed_one, grad_query_raw).astype(BF16)
    grad_keyval = (
        jnp.concatenate([grad_key_nope, grad_values], axis=-1)
        .reshape(row_count, local_heads * (NOPE + VD))
        .astype(BF16)
    )
    grad_keyval_weight = contract("tc,tk->ck", comp_normed, grad_keyval).astype(BF16)
    sum_query = grid.reduce(grid.relative(grad_query_weight, 0))
    sum_keyval = grid.reduce(grid.relative(grad_keyval_weight, 0))
    grad_comp_normed = contract("tk,ck->tc", grad_keyval, full_keyval)
    grad_compressed, grad_kv_gain = rms_backward(
        compressed, comp_inverse, kv_gain, grad_comp_normed
    )
    grad_latent_out = jnp.concatenate(
        [grad_compressed, rotate(grad_key_rope, cosine, -sine_table)], axis=-1
    ).astype(BF16)
    grad_latent = contract("tk,td->kd", grad_latent_out, normed_one)
    grad_normed_one = contract("tq,dq->td", grad_query_raw, full_query) + contract(
        "tk,dk->td", grad_latent_out, w_latent
    )
    grad_normed_one = grid.reduce_depth(split_rows(grad_normed_one.astype(BF16), depth))
    inverse_own = inverse_one[:own_rows]
    grad_x_part, grad_attn_gain = rms_backward(stream_own, inverse_own, attn_gain, grad_normed_one)
    grad_in = grad_residual + grad_x_part
    grad_shared_parts = [part.astype(BF16) for part in grid.relative(grad_shared, 1)]
    returned = grid.exchange(grad_shared_parts)
    sum_shared_in = jnp.stack(
        [
            grid.absolute([part[:units] for part in returned], 0).T,
            grid.absolute([part[padded_units : padded_units + units] for part in returned], 0).T,
        ]
    ).astype(F32)
    sum_shared_out = grid.absolute([part[2 * padded_units : 2 * padded_units + units] for part in returned], 0).astype(F32)
    gains = jnp.stack(
        [grad_attn_gain, grad_ffn_gain, jnp.pad(grad_kv_gain, (0, width - KVR))]
    )
    replicated = jnp.concatenate([grad_latent, jnp.roll(grad_router_rel, base, axis=0), gains])
    used = replicated.shape[0]
    padded = -(-used // (16 * grid.experts)) * 16 * grid.experts
    replicated = jnp.pad(replicated, ((0, padded - used), (0, 0))).astype(BF16)
    chunk = grid.reduce(grid.relative(replicated, 0)).astype(BF16)
    part = grid.reduce_depth(grid.relative_depth(chunk, 1)).astype(BF16)
    chunk = grid.absolute_depth(grid.gather_depth(part), 1)
    whole = grid.absolute(grid.gather(chunk), 0).astype(F32)
    sum_latent = whole[: KVR + ROPE].T
    sum_router = whole[KVR + ROPE : KVR + ROPE + EXPERTS].T
    sum_attn_gain = whole[KVR + ROPE + EXPERTS]
    sum_ffn_gain = whole[KVR + ROPE + EXPERTS + 1]
    sum_kv_gain = whole[KVR + ROPE + EXPERTS + 2, :KVR]
    return (
        block_out,
        grad_in,
        sum_attn_gain,
        sum_kv_gain,
        sum_ffn_gain,
        sum_query,
        sum_latent,
        sum_keyval,
        sum_output,
        sum_router,
        sum_shared_in,
        sum_shared_out,
        jnp.swapaxes(grad_expert_in, 2, 3),
        grad_expert_out,
    )


def after(array, *earlier):
    return lax.optimization_barrier((array, *earlier))[0]


def square_device(
    tokens_in,
    out_grad,
    routes,
    attn_gain,
    kv_gain,
    ffn_gain,
    w_query,
    w_latent,
    w_keyval,
    w_output,
    w_router,
    w_shared_in,
    w_shared_out,
    w_expert_in,
    w_expert_out,
):
    grid = Grid()
    depth = grid.depth
    sequences = grid.experts
    pairs = range(sequences // 2)
    own_rows, width = tokens_in.shape
    row_count = own_rows * depth
    local = w_expert_in.shape[0]
    hidden_units = w_expert_out.shape[1]
    heads = w_query.shape[1] // (NOPE + ROPE)
    own_depth = lax.axis_index("tensor")
    blocks = jnp.stack([grid.place_of(offset) for offset in grid.offsets]).astype(jnp.int32)
    depths = ((own_depth + jnp.arange(depth)) % depth).astype(jnp.int32)
    base = (lax.axis_index("expert") * local).astype(jnp.int32)[None]

    tokens = grid.gather_depth(tokens_in)
    packs = grid.gather(pack_weights(w_query, w_keyval, w_output, heads))
    position = (
        (own_depth + jnp.arange(row_count) // own_rows) % depth * own_rows
        + jnp.arange(row_count) % own_rows
    )
    cosine, sine = (jnp.tile(table, (1, heads)) for table in rope_tables(position))
    bias = jnp.where(position[None, :] <= position[:, None], 0.0, -1e30).astype(F32)
    half = ROPE // 2
    latent_t = w_latent.T
    latent_t = jnp.concatenate(
        [latent_t[:KVR]] + [latent_t[KVR : KVR + half]] * heads + [latent_t[KVR + half :]] * heads
    )
    normed, compressed, low, key = latent_rows(tokens, attn_gain, latent_t, kv_gain, cosine, sine)

    group_grads = jnp.concatenate(grid.gather_depth(after(out_grad, *tokens)))
    all_grads = grid.gather(after(group_grads, *packs))
    routes_t = after(routes, normed).T
    routes_t = jnp.concatenate(grid.relative_depth(routes_t, 1), axis=1)
    routes_all = grid.gather_small(routes_t)
    units = w_shared_out.shape[0] // grid.experts
    padding = ((0, -units % 32), (0, 0))
    shared_in, shared_out = after(w_shared_in, normed), after(w_shared_out, normed)
    shared_parts = [
        jnp.concatenate([jnp.pad(part, padding) for part in parts])
        for parts in zip(
            grid.relative(shared_in[0].T, 0),
            grid.relative(shared_in[1].T, 0),
            grid.relative(shared_out, 0),
        )
    ]
    pieces = grid.exchange(shared_parts)
    router = jnp.roll(w_router.T, -base[0], axis=0)
    padded_units = units + padding[0][1]
    side, shared_out = vmem_call(
        join_columns_kernel,
        "join_columns",
        blocks,
        [*pieces, router],
        [
            jax.ShapeDtypeStruct((2 * padded_units + EXPERTS, width), BF16),
            jax.ShapeDtypeStruct((padded_units, width), BF16),
        ],
        [],
    )

    query, keyval, soft, attended, part = attention_forward(
        heads, blocks, packs, normed, low, key, bias, cosine, sine
    )
    stream = tokens_in.astype(F32)
    residual = stream + grid.reduce_depth(split_rows(part, depth))
    normed_two, inverse_two = rms_forward(residual, ffn_gain)
    normed_two = normed_two.astype(BF16)

    held = [None, None]
    for m in pairs:
        held = dispatch_grads(
            m,
            sequences,
            local,
            base,
            routes_all[2 * m : 2 * m + 2],
            all_grads[2 * m : 2 * m + 2],
            shared_out,
            held,
        )
    slot_grads, shared_raw = held
    raw = expert_raw(slot_grads, w_expert_out)

    rows = grid.gather(jnp.concatenate(grid.gather_depth(normed_two)))
    held = [None] * 6
    for m in pairs:
        held = dispatch_rows(
            m,
            sequences,
            local,
            base,
            routes_all[2 * m : 2 * m + 2],
            rows[2 * m : 2 * m + 2],
            side,
            shared_raw,
            held,
        )
    slot_rows, infos, picks, gates, shared_hidden, shared_back = held
    expert_in = jnp.swapaxes(w_expert_in, 2, 3).reshape(local, 2 * hidden_units, width)
    back_rows, extra, hidden, back = expert_rows(slot_rows, infos, expert_in, raw)
    back_tokens, logits = [None] * sequences, [None]
    for m in reversed(pairs):
        back_tokens[2 * m : 2 * m + 2], logits = combine_back(
            m, picks, back_rows, extra, gates, shared_back, side, logits
        )
    sums, first_mark, second_mark = grid.reduce_parts(back_tokens)
    grad_group = sum(array.astype(F32) for array in sums).astype(BF16)
    grad_normed = grid.reduce_depth(split_rows(grad_group, depth))

    half_experts = local // 2
    held = weight_grads(
        0, half_experts, after(slot_rows, first_mark), slot_grads, hidden, back, [None, None]
    )
    grad_expert_in, grad_expert_out = weight_grads(
        half_experts, local, after(slot_rows, second_mark), slot_grads, hidden, back, held
    )
    out_rows = expert_out_rows(after(hidden, second_mark), w_expert_out)
    out_tokens = []
    for m in pairs:
        out_tokens += combine_out(
            m, picks, after(out_rows, grad_group), shared_hidden, shared_out
        )
    *grad_parts, grad_router = side_grads(
        blocks, base, rows, all_grads, after(logits[0], grad_group), shared_hidden, shared_back
    )
    out_sums, _, _ = grid.reduce_parts(out_tokens)
    out_group = sum(array.astype(F32) for array in out_sums).astype(BF16)

    grad_res_part, grad_ffn_gain = rms_backward(residual, inverse_two, ffn_gain, grad_normed)
    grad_residual = out_grad.astype(F32) + grad_res_part
    grads = grid.gather_depth(grad_residual.astype(BF16))

    ffn_total = grid.reduce_depth(split_rows(after(out_group, *grads), depth))
    block_out = (residual + ffn_total).astype(BF16)
    returned = grid.exchange([after(part, grad_group) for part in grad_parts])
    sum_shared_in, sum_shared_out = vmem_call(
        functools.partial(join_rows_kernel, units),
        "join_rows",
        blocks,
        returned,
        [
            jax.ShapeDtypeStruct((2, units * grid.experts, width // grid.experts), F32),
            jax.ShapeDtypeStruct((units * grid.experts, width // grid.experts), F32),
        ],
        [],
    )

    grad_query, grad_keyval, grad_normed_one, *chunks = attention_backward(
        heads,
        blocks,
        packs,
        tokens,
        grads,
        (query, keyval, key, soft, attended, compressed, low, normed),
        latent_t,
        kv_gain,
        cosine,
        sine,
        grad_router,
        grad_ffn_gain,
    )
    grad_packs = attention_weights(
        heads, blocks, packs[0].shape, grads, normed, low, attended, grad_query, grad_keyval
    )
    sums, _, _ = grid.reduce_parts(chunks)
    size = CHUNK_ROWS // depth
    columns = width // grid.experts
    parts = vmem_call(
        sum_split_kernel,
        "sum_split",
        depths,
        sums,
        [jax.ShapeDtypeStruct((size, columns), BF16)] * depth,
        [],
    )
    parts = grid.gather_depth(grid.reduce_depth(parts).astype(BF16))
    (chunk,) = vmem_call(
        join_depth_kernel,
        "join_depth",
        depths,
        parts,
        [jax.ShapeDtypeStruct((CHUNK_ROWS, columns), BF16)],
        [],
    )
    sum_latent, sum_router, sum_gains = vmem_call(
        functools.partial(replicated_kernel, KVR + ROPE),
        "replicated",
        blocks,
        grid.gather(chunk),
        [
            jax.ShapeDtypeStruct((KVR + ROPE, width), F32),
            jax.ShapeDtypeStruct((EXPERTS, width), F32),
            jax.ShapeDtypeStruct((16, width), F32),
        ],
        [],
    )
    sum_kv_gain = sum_gains[2 : 2 + KVR // columns, :columns].reshape(KVR)

    grad_normed_one = grid.reduce_depth(split_rows(grad_normed_one, depth))
    inverse_one = lax.rsqrt(jnp.mean(stream * stream, axis=-1, keepdims=True) + EPSILON)
    grad_in = grad_residual + rms_backward(stream, inverse_one, attn_gain, grad_normed_one)[0]
    sums, _, _ = grid.reduce_parts(grad_packs)
    sum_query, sum_keyval, sum_output = unpack_weights(
        sum(array.astype(F32) for array in sums), w_keyval.shape, w_output.shape, heads
    )
    return (
        block_out,
        grad_in,
        sum_gains[0],
        sum_kv_gain,
        sum_gains[1],
        sum_query,
        sum_latent.T,
        sum_keyval,
        sum_output,
        sum_router.T,
        jnp.swapaxes(sum_shared_in, 1, 2),
        sum_shared_out,
        jnp.swapaxes(grad_expert_in.reshape(local, 2, hidden_units, width), 2, 3),
        grad_expert_out,
    )


def solution(mesh):
    placed = (
        P(("expert", "tensor"), None),
        P(("expert", "tensor"), None),
        P("expert", None),
        P(),
        P(),
        P(),
        P("expert", "tensor"),
        P(),
        P("expert", "tensor"),
        P("tensor", "expert"),
        P(),
        P(None, "expert", "tensor"),
        P("tensor", "expert"),
        P("expert", None, None, "tensor"),
        P("expert", "tensor", None),
    )
    square = mesh.shape["expert"] == 8
    return jax.shard_map(
        square_device if square else general_device,
        mesh=mesh,
        in_specs=placed,
        out_specs=(
            P(("expert", "tensor"), None),
            P(("expert", "tensor"), None),
            P(),
            P(),
            P(),
            P("expert", "tensor"),
            P(),
            P("expert", "tensor"),
            P("tensor", "expert"),
            P(),
            P(None, "expert", "tensor"),
            P("tensor", "expert"),
            P("expert", None, None, "tensor"),
            P("expert", "tensor", None),
        ),
        check_vma=False,
    )
```

```python
import functools
import math

import jax
import jax.numpy as jnp
from jax import lax
from jax.experimental import pallas as pl
from jax.experimental.pallas import tpu as pltpu
from jax.sharding import PartitionSpec as P

NOPE = 128
ROPE = 64
VD = 128
KVR = 512
EXPERTS = 64
TOP = 6
SLOTS = 32
SLOT_BLOCK = 256
LANES = 128
PARTS = 2
CHUNK_ROWS = 704

EPSILON = 1e-06
ROUTE_SCALE = 2.446
ROPE_BASE = 50000.0
BF16 = jnp.bfloat16
F32 = jnp.float32


def mix_dot(left_side, right_side):
    return jnp.dot(left_side, right_side, preferred_element_type=F32)


def contract(pattern, left_side, right_side):
    return jnp.einsum(pattern, left_side, right_side, preferred_element_type=F32)


def rms_forward(values, gain_vec):
    inverse = lax.rsqrt(jnp.mean(values * values, axis=-1, keepdims=True) + EPSILON)
    return (values * inverse * gain_vec, inverse)


def rms_backward(values, inverse, gain_vec, grad_normed):
    weighted = grad_normed * gain_vec
    grad_values = inverse * weighted - values * (inverse * inverse * inverse) * jnp.mean(
        values * weighted, axis=-1, keepdims=True
    )
    grad_gain = jnp.sum(grad_normed * values * inverse, axis=0)
    return (grad_values, grad_gain)


def rope_tables(position):
    half_rope = ROPE // 2
    frequency = jnp.exp(-jnp.log(ROPE_BASE) * jnp.arange(half_rope).astype(F32) / half_rope)
    angles = position.astype(F32)[:, None] * frequency[None, :]
    return (jnp.cos(angles), jnp.sin(angles))


def rotate(columns, cosine, sine_table):
    half_rope = columns.shape[-1] // 2
    first_half = columns[..., :half_rope]
    second_half = columns[..., half_rope:]
    return jnp.concatenate(
        [
            first_half * cosine - second_half * sine_table,
            first_half * sine_table + second_half * cosine,
        ],
        axis=-1,
    )


def low_add(first, second):
    return (first.astype(F32) + second.astype(F32)).astype(BF16)


class Grid:
    def __init__(self):
        self.experts = lax.axis_size("expert")
        self.depth = lax.axis_size("tensor")
        self.side = math.isqrt(self.experts // 2)
        assert self.side * self.side * 2 == self.experts
        self.offsets = [
            (dy, dx, dc)
            for dy in range(self.side)
            for dx in range(self.side)
            for dc in range(2)
        ]

    def neighbour(self, place, offset):
        side = self.side
        y, x, core = place // (2 * side), place // 2 % side, place % 2
        dy, dx, dc = offset
        return (((y + dy) % side) * side + (x + dx) % side) * 2 + (core + dc) % 2

    def place_of(self, offset):
        return self.neighbour(lax.axis_index("expert"), offset)

    def fetch(self, array, offset):
        pairs = [(self.neighbour(place, offset), place) for place in range(self.experts)]
        return lax.ppermute(array, "expert", pairs)

    def send(self, array, offset):
        pairs = [(place, self.neighbour(place, offset)) for place in range(self.experts)]
        return lax.ppermute(array, "expert", pairs)

    def gather(self, shard):
        if self.side != 2:
            return [shard] + [self.fetch(shard, offset) for offset in self.offsets[1:]]
        half = shard.shape[0] // 2
        along_x = self.fetch(shard, (0, 1, 0))
        along_y = self.fetch(shard, (1, 0, 0))
        pair = self.fetch(shard, (0, 0, 1))
        first = self.fetch(along_x[:half], (1, 0, 0))
        second = self.fetch(along_y[half:], (0, 1, 0))
        pair_x = self.fetch(along_x, (0, 0, 1))
        pair_y = self.fetch(along_y, (0, 0, 1))
        pair_first = self.fetch(first, (0, 0, 1))
        pair_second = self.fetch(second, (0, 0, 1))
        return [
            shard,
            pair,
            along_x,
            pair_x,
            along_y,
            pair_y,
            jnp.concatenate([first, second]),
            jnp.concatenate([pair_first, pair_second]),
        ]

    def reduce(self, chunks):
        if self.side != 2:
            total = chunks[0].astype(F32)
            for offset, chunk in zip(self.offsets[1:], chunks[1:]):
                total = total + self.send(chunk, offset).astype(F32)
            return total
        half = chunks[0].shape[0] // 2
        own = {}
        for place in (6, 2, 4, 0):
            own[place] = low_add(chunks[place], self.send(chunks[place + 1], (0, 0, 1)))
        first = self.send(own[6][:half], (0, 1, 0))
        second = self.send(own[6][half:], (1, 0, 0))
        to_y = jnp.concatenate([low_add(own[4][:half], first), own[4][half:]])
        to_x = jnp.concatenate([own[2][:half], low_add(own[2][half:], second)])
        from_x = self.send(to_x, (0, 1, 0))
        from_y = self.send(to_y, (1, 0, 0))
        return own[0].astype(F32) + from_x.astype(F32) + from_y.astype(F32)

    def gather_small(self, shard):
        along_x = self.fetch(shard, (0, 1, 0))
        along_y = self.fetch(shard, (1, 0, 0))
        near = [shard, along_x, along_y, self.fetch(along_x, (1, 0, 0))]
        return [piece for held in near for piece in (held, self.fetch(held, (0, 0, 1)))]

    def exchange(self, parts):
        pieces = [parts[0]]
        for dy, dx, dc in self.offsets[1:]:
            back = (-dy % self.side, -dx % self.side, dc)
            pieces.append(self.send(parts[self.offsets.index(back)], back))
        return pieces

    def reduce_parts(self, chunks):
        half = chunks[0].shape[0] // 2
        own = {}
        for place in (6, 2, 4, 0):
            own[place] = low_add(chunks[place], self.send(chunks[place + 1], (0, 0, 1)))
        first = self.send(own[6][:half], (0, 1, 0))
        second = self.send(own[6][half:], (1, 0, 0))
        to_y = jnp.concatenate([low_add(own[4][:half], first), own[4][half:]])
        to_x = jnp.concatenate([own[2][:half], low_add(own[2][half:], second)])
        from_x = self.send(to_x, (0, 1, 0))
        from_y = self.send(to_y, (1, 0, 0))
        return [own[0], from_x, from_y], own[6], (to_x, to_y)

    def ring(self, array, step):
        depth = self.depth
        return lax.ppermute(array, "tensor", [(i, (i + step) % depth) for i in range(depth)])

    def ring_near(self, shard):
        return self.ring(shard, -1), self.ring(shard, 1)

    def ring_far(self, ahead, behind):
        half = ahead.shape[0] // 2
        return self.ring(ahead[:half], -1), self.ring(behind[half:], 1)

    def ring_gather(self, shard):
        ahead, behind = self.ring_near(shard)
        return [shard, ahead, *self.ring_far(ahead, behind), behind]

    def ring_start(self, chunks):
        half = chunks[2].shape[0] // 2
        first = self.ring(chunks[2][:half], 1)
        second = self.ring(chunks[2][half:], -1)
        return first, second

    def ring_finish(self, chunks, first, second):
        half = chunks[2].shape[0] // 2
        to_ahead = jnp.concatenate([low_add(chunks[1][:half], first), chunks[1][half:]])
        to_behind = jnp.concatenate([chunks[3][:half], low_add(chunks[3][half:], second)])
        return self.ring(to_ahead, 1), self.ring(to_behind, -1), (to_ahead, to_behind)

    def ring_reduce(self, chunks):
        ahead, behind, _ = self.ring_finish(chunks, *self.ring_start(chunks))
        return chunks[0].astype(F32) + ahead.astype(F32) + behind.astype(F32)

    def gather_depth(self, shard):
        depth = self.depth
        return [shard] + [
            lax.ppermute(shard, "tensor", [((i + k) % depth, i) for i in range(depth)])
            for k in range(1, depth)
        ]

    def reduce_depth(self, chunks):
        depth = self.depth
        total = chunks[0].astype(F32)
        for k in range(1, depth):
            total = total + lax.ppermute(
                chunks[k], "tensor", [(i, (i + k) % depth) for i in range(depth)]
            ).astype(F32)
        return total

    def absolute(self, pieces, axis):
        size = pieces[0].shape[axis]
        shape = list(pieces[0].shape)
        shape[axis] = size * self.experts
        whole = jnp.zeros(shape, pieces[0].dtype)
        for offset, piece in zip(self.offsets, pieces):
            whole = lax.dynamic_update_slice_in_dim(
                whole, piece, self.place_of(offset) * size, axis
            )
        return whole

    def relative(self, whole, axis):
        size = whole.shape[axis] // self.experts
        return [
            lax.dynamic_slice_in_dim(whole, self.place_of(offset) * size, size, axis)
            for offset in self.offsets
        ]

    def absolute_depth(self, pieces, axis):
        size = pieces[0].shape[axis]
        shape = list(pieces[0].shape)
        shape[axis] = size * self.depth
        whole = jnp.zeros(shape, pieces[0].dtype)
        own = lax.axis_index("tensor")
        for k, piece in enumerate(pieces):
            whole = lax.dynamic_update_slice_in_dim(
                whole, piece, (own + k) % self.depth * size, axis
            )
        return whole

    def relative_depth(self, whole, axis):
        size = whole.shape[axis] // self.depth
        own = lax.axis_index("tensor")
        return [
            lax.dynamic_slice_in_dim(whole, (own + k) % self.depth * size, size, axis)
            for k in range(self.depth)
        ]


def split_rows(array, count):
    size = array.shape[0] // count
    return [array[i * size : (i + 1) * size] for i in range(count)]


def attention_scores(queries, key_nope, key_rope, position):
    scores = contract("qhd,khd->hqk", queries[..., :NOPE], key_nope) + contract(
        "qhr,kr->hqk", queries[..., NOPE:], key_rope
    )
    scores = scores * ((NOPE + ROPE) ** (-0.5))
    allowed = position[None, :] <= position[:, None]
    return jnp.where(allowed[None], scores, -1e30)


def dot_nn(left, right):
    return lax.dot_general(left, right, (((1,), (0,)), ((), ())), preferred_element_type=F32)


def dot_nt(left, right):
    return lax.dot_general(left, right, (((1,), (1,)), ((), ())), preferred_element_type=F32)


def dot_tn(left, right):
    return lax.dot_general(left, right, (((0,), (0,)), ((), ())), preferred_element_type=F32)


def silu_parts(gate):
    sigmoid = 1.0 / (1.0 + jnp.exp(-gate))
    return sigmoid, gate * sigmoid


def split_high(value):
    high = value.astype(BF16)
    return high, (value - high.astype(F32)).astype(BF16)


def whole(shape):
    return pl.BlockSpec(shape, lambda *_: (0,) * len(shape))


def params(*semantics):
    return pltpu.CompilerParams(
        dimension_semantics=semantics or None, vmem_limit_bytes=56 * 1024 * 1024
    )


ANYWHERE = pl.BlockSpec(memory_space=pl.ANY)


def pick_rows(routes, base, local):
    count = routes.shape[1]
    expert = lax.broadcasted_iota(jnp.int32, (EXPERTS, count), 0) + base
    expert = jnp.where(expert >= EXPERTS, expert - EXPERTS, expert)
    chosen = expert == routes[0:1]
    for k in range(1, routes.shape[0]):
        chosen = chosen | (expert == routes[k : k + 1])
    chosen = chosen.astype(F32)
    rows = max(local, 16)
    earlier = lax.broadcasted_iota(jnp.int32, (count, count), 0) < lax.broadcasted_iota(
        jnp.int32, (count, count), 1
    )
    rank = dot_nn(chosen[:rows].astype(BF16), earlier.astype(F32).astype(BF16))
    rank = jnp.where(chosen[:rows] > 0.5, rank, -1.0)
    slot = lax.broadcasted_iota(jnp.int32, (SLOTS, count), 0).astype(F32)
    parts = [(slot == rank[j : j + 1]).astype(F32) for j in range(local)]
    return jnp.concatenate(parts, axis=0), chosen


def dispatch_grads_kernel(local, base_ref, routes_ref, *refs):
    shared_ref, slot_ref, raw_ref = refs[-3:]
    pieces = refs[:-3]
    half = len(pieces) // 2
    for core in range(2):

        @pl.when(pl.program_id(0) % 2 == core)
        def _():
            pick, _ = pick_rows(routes_ref[0], base_ref[0], local)
            values = jnp.concatenate(
                [piece[...] for piece in pieces[core * half : (core + 1) * half]], axis=0
            )
            slot_ref[...] = (
                dot_nn(pick.astype(BF16), values).astype(BF16).reshape(slot_ref.shape)
            )
            raw_ref[0] = dot_nt(shared_ref[...], values)


def dispatch_rows_kernel(local, units, base_ref, *refs):
    routes, pieces, side_ref, raw_ref = refs[:2], refs[2:4], refs[4], refs[5]
    slot_ref, info_ref, pick_ref, gate_ref, hidden_ref, back_ref = refs[-6:]
    for i in range(2):

        @pl.when(pl.program_id(0) == i)
        def _():
            pick, chosen = pick_rows(routes[i][...], base_ref[0], local)
            rows = pieces[i][...]
            low = pick.astype(BF16)
            pick_ref[0] = low
            slot_ref[...] = dot_nn(low, rows).astype(BF16).reshape(slot_ref.shape)
            side = dot_nt(side_ref[...], rows)
            gate, up, raw = side[:units], side[units : 2 * units], raw_ref[0]
            sigmoid = chosen / (1.0 + jnp.exp(-side[2 * units :]))
            total = jnp.sum(sigmoid, axis=0, keepdims=True)
            gate_ref[0, 0] = sigmoid
            gate_ref[0, 1] = jnp.broadcast_to(total, sigmoid.shape)
            weight = ROUTE_SCALE * sigmoid / total
            scale = jnp.concatenate(
                [
                    jnp.sum(
                        pick[j * SLOTS : (j + 1) * SLOTS] * weight[j : j + 1],
                        axis=1,
                        keepdims=True,
                    )
                    for j in range(local)
                ],
                axis=0,
            )
            high, low_part = split_high(scale)
            lane = lax.broadcasted_iota(jnp.int32, (scale.shape[0], LANES), 1)
            info = jnp.where(
                lane == 0, high.astype(F32), jnp.where(lane == 1, low_part.astype(F32), 0.0)
            )
            info_ref[...] = info.astype(BF16).reshape(info_ref.shape)
            smooth, active = silu_parts(gate)
            hidden_ref[0] = (active * up).astype(BF16)
            back_ref[0] = jnp.concatenate(
                [raw * up * smooth * (1.0 + gate * (1.0 - smooth)), raw * active], axis=0
            ).astype(BF16)


def expert_raw_kernel(grads_ref, out_ref, raw_ref):
    raw_ref[0] = dot_nt(out_ref[0], grads_ref[0])


def expert_kernel(
    units, rows_ref, info_ref, in_ref, raw_ref, back_rows_ref, extra_ref, hidden_ref, back_ref
):
    expert = pl.program_id(0)
    weight_in = in_ref[0]
    gates = dot_nt(weight_in, rows_ref[0])
    raw = raw_ref[0]
    gate, up = gates[:units], gates[units:]
    lane = lax.broadcasted_iota(jnp.int32, (16, LANES), 1)
    select = (lane < 2).astype(F32).astype(BF16)
    scale = dot_nt(select, info_ref[0])[0:1]
    smooth, active = silu_parts(gate)
    hidden = active * up
    grad_gate = jnp.sum(hidden.astype(BF16).astype(F32) * raw, axis=0, keepdims=True)
    hidden_ref[0] = (hidden * scale).astype(BF16)
    raw = raw * scale
    back = jnp.concatenate(
        [raw * up * smooth * (1.0 + gate * (1.0 - smooth)), raw * active], axis=0
    ).astype(BF16)
    back_ref[0] = back
    back_rows_ref[0] = dot_tn(back, weight_in).astype(BF16)
    high, low = split_high(grad_gate)
    row = lax.broadcasted_iota(jnp.int32, (16, grad_gate.shape[1]), 0)
    pair = jnp.where(row == 0, high.astype(F32), jnp.where(row == 1, low.astype(F32), 0.0))
    row = lax.broadcasted_iota(jnp.int32, (16, LANES), 0)
    lane = lax.broadcasted_iota(jnp.int32, (16, LANES), 1)
    place = ((row < 2) & (lane == expert + row * EXPERTS)).astype(F32)
    extra_ref[0] = dot_tn(pair.astype(BF16), place.astype(BF16)).astype(BF16)


def expert_out_kernel(hidden_ref, out_ref, rows_ref):
    rows_ref[0] = dot_tn(hidden_ref[0], out_ref[0]).astype(BF16)


def weight_grad_kernel(rows_ref, grads_ref, hidden_ref, back_ref, *rest):
    in_ref, out_ref, mark_ref = rest[-3:]
    mark_ref[...] = jnp.zeros_like(mark_ref)

    @pl.when(pl.program_id(1) == 0)
    def _():
        in_ref[0] = dot_nn(back_ref[0], rows_ref[0])
        out_ref[0] = dot_nn(hidden_ref[0], grads_ref[0])

    @pl.when(pl.program_id(1) > 0)
    def _():
        in_ref[0] += dot_nn(back_ref[0], rows_ref[0])
        out_ref[0] += dot_nn(hidden_ref[0], grads_ref[0])


def combine_back_kernel(
    pick_ref, slots_ref, extra_ref, gate_ref, back_ref, side_ref, *rest
):
    first_ref, second_ref, logits_ref, left_ref = rest[-4:]
    piece, part = pl.program_id(0), pl.program_id(1)
    flat = pick_ref.shape[1]
    units = back_ref.shape[1]

    @pl.when(part == 0)
    def _():
        merged = dot_tn(extra_ref[...].reshape(flat, LANES), pick_ref[0])
        grad_gate = merged[:EXPERTS] + merged[EXPERTS:]
        sigmoid, total = gate_ref[0, 0], gate_ref[0, 1]
        mixed = jnp.sum(grad_gate * sigmoid, axis=0, keepdims=True)
        logits = (
            ROUTE_SCALE
            * (grad_gate / total - mixed / (total * total))
            * sigmoid
            * (1.0 - sigmoid)
        ).astype(BF16)
        logits_ref[0] = logits
        left_ref[:units] = back_ref[0]
        left_ref[units:] = logits

    value = (
        dot_tn(pick_ref[0], slots_ref[...].reshape(flat, slots_ref.shape[2]))
        + dot_tn(left_ref[...], side_ref[...])
    ).astype(BF16)

    @pl.when(piece == 0)
    def _():
        first_ref[...] = value

    @pl.when(piece == 1)
    def _():
        second_ref[...] = value


def combine_out_kernel(pick_ref, slots_ref, hidden_ref, shared_ref, first_ref, second_ref):
    value = (
        dot_tn(pick_ref[0], slots_ref[...].reshape(pick_ref.shape[1], slots_ref.shape[2]))
        + dot_tn(hidden_ref[0], shared_ref[...])
    ).astype(BF16)

    @pl.when(pl.program_id(0) == 0)
    def _():
        first_ref[...] = value

    @pl.when(pl.program_id(0) == 1)
    def _():
        second_ref[...] = value


def chain_call(kernel, name, grid, prefetch, operands, in_specs, held, out_specs, out_shape, scratch=()):
    chained = [a for a in held if a is not None]
    at = len(prefetch) + len(operands)
    return pl.pallas_call(
        kernel,
        grid_spec=pltpu.PrefetchScalarGridSpec(
            num_scalar_prefetch=len(prefetch),
            grid=grid,
            in_specs=in_specs + [ANYWHERE] * len(chained),
            out_specs=out_specs,
            scratch_shapes=list(scratch),
        ),
        out_shape=out_shape,
        input_output_aliases={at + i: i for i in range(len(chained))},
        compiler_params=params(*["arbitrary"] * len(grid)),
        name=name,
    )(*prefetch, *operands, *chained)


def dispatch_grads(local, base, routes, grads, shared_out):
    sequences, top, count = routes.shape
    width = grads[0].shape[1]
    part = count * 2 // len(grads)
    units = shared_out.shape[0]
    return pl.pallas_call(
        functools.partial(dispatch_grads_kernel, local),
        grid_spec=pltpu.PrefetchScalarGridSpec(
            num_scalar_prefetch=1,
            grid=(sequences,),
            in_specs=[pl.BlockSpec((1, top, count), lambda s, *_: (s, 0, 0))]
            + [pl.BlockSpec((part, width), lambda s, *_: (s // 2, 0))] * len(grads)
            + [whole(shared_out.shape)],
            out_specs=[
                pl.BlockSpec((local, SLOTS, width), lambda s, *_: (0, s, 0)),
                pl.BlockSpec((1, units, count), lambda s, *_: (s, 0, 0)),
            ],
        ),
        out_shape=[
            jax.ShapeDtypeStruct((local, sequences * SLOTS, width), BF16),
            jax.ShapeDtypeStruct((sequences, units, count), F32),
        ],
        compiler_params=params("arbitrary"),
        name="dispatch_grads",
    )(base, routes, *grads, shared_out)


def dispatch_rows(pair, sequences, local, base, routes, rows, side, raws, held):
    count, width = rows[0].shape
    units = raws.shape[1]
    operands = [*routes, *rows, side]
    shapes = [
        ((local * SLOTS, count), BF16),
        ((2, EXPERTS, count), F32),
        ((units, count), BF16),
        ((2 * units, count), BF16),
    ]

    def at(shape):
        return pl.BlockSpec((1,) + shape, lambda i, *_: (2 * pair + i,) + (0,) * len(shape))

    return chain_call(
        functools.partial(dispatch_rows_kernel, local, units),
        "dispatch_rows",
        (2,),
        [base],
        operands + [raws],
        [whole(a.shape) for a in operands] + [at((units, count))],
        held,
        [
            pl.BlockSpec((local, SLOTS, width), lambda i, *_: (0, 2 * pair + i, 0)),
            pl.BlockSpec((local, SLOTS, LANES), lambda i, *_: (0, 2 * pair + i, 0)),
        ]
        + [at(shape) for shape, _ in shapes],
        [
            jax.ShapeDtypeStruct((local, sequences * SLOTS, width), BF16),
            jax.ShapeDtypeStruct((local, sequences * SLOTS, LANES), BF16),
        ]
        + [jax.ShapeDtypeStruct((sequences,) + shape, dtype) for shape, dtype in shapes],
    )


def tile(*shape):
    return pl.BlockSpec((1,) + shape, lambda j, b: (j, b) + (0,) * (len(shape) - 1))


def lane_tile(*shape):
    return pl.BlockSpec((1,) + shape, lambda j, b: (j, 0, b))


def one(*shape):
    return pl.BlockSpec((1,) + shape, lambda j, b: (j, 0, 0))


def expert_raw(grads, expert_out):
    local, slots, width = grads.shape
    units = expert_out.shape[1]
    block = min(slots, SLOT_BLOCK)
    return pl.pallas_call(
        expert_raw_kernel,
        grid=(local, slots // block),
        in_specs=[tile(block, width), one(units, width)],
        out_specs=lane_tile(units, block),
        out_shape=jax.ShapeDtypeStruct((local, units, slots), F32),
        compiler_params=params("arbitrary", "arbitrary"),
        name="expert_raw",
    )(grads, expert_out)


def expert_rows(rows, infos, expert_in, raw):
    local, slots, width = rows.shape
    units = raw.shape[1]
    block = min(slots, SLOT_BLOCK)
    return pl.pallas_call(
        functools.partial(expert_kernel, units),
        grid=(local, slots // block),
        in_specs=[
            tile(block, width),
            tile(block, LANES),
            one(2 * units, width),
            lane_tile(units, block),
        ],
        out_specs=[
            tile(block, width),
            tile(block, LANES),
            lane_tile(units, block),
            lane_tile(2 * units, block),
        ],
        out_shape=[
            jax.ShapeDtypeStruct((local, slots, width), BF16),
            jax.ShapeDtypeStruct((local, slots, LANES), BF16),
            jax.ShapeDtypeStruct((local, units, slots), BF16),
            jax.ShapeDtypeStruct((local, 2 * units, slots), BF16),
        ],
        compiler_params=params("arbitrary", "arbitrary"),
        name="expert_rows",
    )(rows, infos, expert_in, raw)


def expert_out_rows(hidden, expert_out):
    local, units, slots = hidden.shape
    width = expert_out.shape[2]
    block = min(slots, SLOT_BLOCK)
    return pl.pallas_call(
        expert_out_kernel,
        grid=(local, slots // block),
        in_specs=[lane_tile(units, block), one(units, width)],
        out_specs=tile(block, width),
        out_shape=jax.ShapeDtypeStruct((local, slots, width), BF16),
        compiler_params=params("arbitrary", "arbitrary"),
        name="expert_out_rows",
    )(hidden, expert_out)


def weight_grads(start, stop, rows, grads, hidden, back, held):
    local, slots, width = rows.shape
    units = hidden.shape[1]
    block = min(slots, SLOT_BLOCK)

    def moved(spec):
        return pl.BlockSpec(
            spec.block_shape, lambda j, b: (lambda at: (at[0] + start,) + at[1:])(spec.index_map(j, b))
        )

    return chain_call(
        weight_grad_kernel,
        "weight_grads",
        (stop - start, slots // block),
        [],
        [rows, grads, hidden, back],
        [
            moved(spec)
            for spec in (
                tile(block, width),
                tile(block, width),
                lane_tile(units, block),
                lane_tile(2 * units, block),
            )
        ],
        held,
        [moved(one(2 * units, width)), moved(one(units, width)), whole((8, LANES))],
        [
            jax.ShapeDtypeStruct((local, 2 * units, width), F32),
            jax.ShapeDtypeStruct((local, units, width), F32),
            jax.ShapeDtypeStruct((8, LANES), F32),
        ],
    )


def piece_specs(width, part):
    return [
        pl.BlockSpec((width[0], part), lambda i, h: (0, jnp.where(i == 0, h, width[1] - 1))),
        pl.BlockSpec((width[0], part), lambda i, h: (0, jnp.where(i == 0, 0, h))),
    ]


def combine_back(pair, picks, slots, extra, gates, backs, side, held):
    sequences, flat, count = picks.shape
    local, _, width = slots.shape
    part = width // PARTS

    def at(array):
        shape = array.shape[1:]
        return pl.BlockSpec((1,) + shape, lambda i, h: (2 * pair + i,) + (0,) * len(shape))

    def strip(size):
        return pl.BlockSpec((local, SLOTS, size), lambda i, h: (0, 2 * pair + i, 0))

    outs = chain_call(
        lambda *refs: combine_back_kernel(*refs[:6], *refs[-3:-1], refs[-4], refs[-1]),
        "combine_back",
        (2, PARTS),
        [],
        [picks, slots, extra, gates, backs, side],
        [
            at(picks),
            pl.BlockSpec((local, SLOTS, part), lambda i, h: (0, 2 * pair + i, h)),
            strip(LANES),
            at(gates),
            at(backs),
            pl.BlockSpec((side.shape[0], part), lambda i, h: (0, h)),
        ],
        held,
        [pl.BlockSpec((1, EXPERTS, count), lambda i, h: (2 * pair + i, 0, 0))]
        + piece_specs((count, PARTS), part),
        [jax.ShapeDtypeStruct((sequences, EXPERTS, count), BF16)]
        + [jax.ShapeDtypeStruct((count, width), BF16)] * 2,
        [pltpu.VMEM((side.shape[0], count), BF16)],
    )
    return outs[1:], outs[:1]


def combine_out(pair, picks, slots, hiddens, shared_out):
    _, flat, count = picks.shape
    local, _, width = slots.shape
    part = width // PARTS
    units = hiddens.shape[1]
    return pl.pallas_call(
        combine_out_kernel,
        grid=(2, PARTS),
        in_specs=[
            pl.BlockSpec((1, flat, count), lambda i, h: (2 * pair + i, 0, 0)),
            pl.BlockSpec((local, SLOTS, part), lambda i, h: (0, 2 * pair + i, h)),
            pl.BlockSpec((1, units, count), lambda i, h: (2 * pair + i, 0, 0)),
            pl.BlockSpec((units, part), lambda i, h: (0, h)),
        ],
        out_specs=piece_specs((count, PARTS), part),
        out_shape=[jax.ShapeDtypeStruct((count, width), BF16)] * 2,
        compiler_params=params("arbitrary", "arbitrary"),
        name="combine_out",
    )(picks, slots, hiddens, shared_out)


def side_grads_kernel(sequences, block_ref, *refs):
    rows, grads, rest = refs[:sequences], refs[sequences : 2 * sequences], refs[2 * sequences :]
    half = len(grads) // 2
    part = rows[0].shape[0] // half
    logits_ref, hidden_ref, back_ref, first_ref, *parts, router_ref, left_ref, in_ref, out_ref = rest
    units = hidden_ref.shape[1]
    for s in range(sequences):
        left_ref[: 2 * units] = back_ref[s]
        left_ref[2 * units :] = logits_ref[s]
        value = dot_nn(left_ref[...], rows[s][...])
        held = grads[s % 2 * half : (s % 2 + 1) * half]
        other = dot_nn(
            hidden_ref[s],
            jnp.concatenate([piece[s // 2 * part : (s // 2 + 1) * part] for piece in held], axis=0),
        )
        if s == 0:
            in_ref[...] = value
            out_ref[...] = other
        else:
            in_ref[...] += value
            out_ref[...] += other
    shards, columns = len(parts), parts[0].shape[1]
    for k in range(shards):
        at = pl.ds(pl.multiple_of(block_ref[k] * columns, columns), columns)
        parts[k][: 2 * units] = in_ref[: 2 * units, at].astype(BF16)
        parts[k][2 * units :] = out_ref[:, at].astype(BF16)
    local = EXPERTS // shards
    for k in range(shards):
        start = first_ref[0] + k * local
        start = jnp.where(start >= EXPERTS, start - EXPERTS, start)
        router_ref[pl.ds(pl.multiple_of(start, local), local)] = in_ref[
            2 * units + k * local : 2 * units + (k + 1) * local
        ]


def side_grads(blocks, base, rows, grads, logits, hiddens, backs):
    sequences = len(rows)
    count, width = rows[0].shape
    units = hiddens.shape[1]
    shards = blocks.shape[0]
    operands = [*rows, *grads, logits, hiddens, backs]
    return pl.pallas_call(
        functools.partial(side_grads_kernel, sequences),
        grid_spec=pltpu.PrefetchScalarGridSpec(
            num_scalar_prefetch=1,
            grid=(1,),
            in_specs=[whole(a.shape) for a in operands]
            + [pl.BlockSpec(memory_space=pltpu.SMEM)],
            out_specs=[whole((3 * units, width // shards))] * shards + [whole((EXPERTS, width))],
            scratch_shapes=[
                pltpu.VMEM((2 * units + EXPERTS, count), BF16),
                pltpu.VMEM((2 * units + EXPERTS, width), F32),
                pltpu.VMEM((units, width), F32),
            ],
        ),
        out_shape=[jax.ShapeDtypeStruct((3 * units, width // shards), BF16)] * shards
        + [jax.ShapeDtypeStruct((EXPERTS, width), F32)],
        compiler_params=params("arbitrary"),
        name="side_grads",
    )(blocks, *operands, base)


def join_columns_kernel(block_ref, *refs):
    pieces, router_ref, side_ref, out_ref = refs[:-3], refs[-3], refs[-2], refs[-1]
    units = out_ref.shape[0]
    columns = pieces[0].shape[1]
    for k, piece in enumerate(pieces):
        at = pl.ds(pl.multiple_of(block_ref[k] * columns, columns), columns)
        side_ref[: 2 * units, at] = piece[: 2 * units]
        out_ref[:, at] = piece[2 * units :]
    side_ref[2 * units :] = router_ref[...]


def join_rows_kernel(units, block_ref, *refs):
    parts, in_ref, out_ref = refs[:-2], refs[-2], refs[-1]
    padded = parts[0].shape[0] // 3
    for k, part in enumerate(parts):
        at = pl.ds(pl.multiple_of(block_ref[k] * units, 8), units)
        value = part[...].astype(F32)
        in_ref[0, at] = value[:units]
        in_ref[1, at] = value[padded : padded + units]
        out_ref[at] = value[2 * padded : 2 * padded + units]


def sum_split_kernel(depth_ref, own_ref, x_ref, y_ref, *outs):
    size = outs[0].shape[0]
    for k, out in enumerate(outs):
        at = pl.ds(pl.multiple_of(depth_ref[k] * size, size), size)
        out[...] = (
            own_ref[at].astype(F32) + x_ref[at].astype(F32) + y_ref[at].astype(F32)
        ).astype(BF16)


def join_depth_kernel(depth_ref, *refs):
    pieces, out_ref = refs[:-1], refs[-1]
    size = pieces[0].shape[0]
    for k, piece in enumerate(pieces):
        out_ref[pl.ds(pl.multiple_of(depth_ref[k] * size, size), size)] = piece[...]


def replicated_kernel(used, block_ref, *refs):
    chunks, latent_ref, router_ref, gains_ref = refs[:-3], refs[-3], refs[-2], refs[-1]
    columns = chunks[0].shape[1]
    for k, chunk in enumerate(chunks):
        at = pl.ds(pl.multiple_of(block_ref[k] * columns, columns), columns)
        latent_ref[:, at] = chunk[:used].astype(F32)
        router_ref[:, at] = chunk[used : used + EXPERTS].astype(F32)
        gains_ref[:, at] = chunk[used + EXPERTS : used + EXPERTS + 16].astype(F32)


def rope_turn(first, second, cosine, sine):
    return first * cosine - second * sine, first * sine + second * cosine


def unit_rows(pieces):
    values = jnp.concatenate([piece[...] for piece in pieces], axis=0).astype(F32)
    inverse = lax.rsqrt(jnp.mean(values * values, axis=-1, keepdims=True) + EPSILON)
    return values * inverse


def latent_kernel(depth, *refs):
    pieces = refs[:depth]
    gain_ref, weight_ref, kv_gain_ref, cosine_ref, sine_ref = refs[depth : depth + 5]
    normed_ref, comp_ref, low_ref, key_ref = refs[depth + 5 :]
    normed = (unit_rows(pieces) * gain_ref[...]).astype(BF16)
    normed_ref[...] = normed
    latent = dot_nt(normed, weight_ref[...])
    compressed = latent[:, :KVR]
    comp_ref[...] = compressed
    inverse = lax.rsqrt(jnp.mean(compressed * compressed, axis=-1, keepdims=True) + EPSILON)
    low_ref[...] = (compressed * inverse * kv_gain_ref[...]).astype(BF16)
    first, second = rope_turn(
        latent[:, KVR : KVR + LANES], latent[:, KVR + LANES :], cosine_ref[...], sine_ref[...]
    )
    key_ref[...] = jnp.concatenate([first, second], axis=1).astype(BF16)


def head_mask(head):
    lane = lax.broadcasted_iota(jnp.int32, (1, LANES), 1)
    return ((lane // (ROPE // 2)) == head).astype(F32)


def keyval_weight(block_ref, packs, whole_ref, queries):
    share = KVR // len(packs)
    count = packs[0].shape[0] // share
    columns = whole_ref.shape[1] // count
    for k, pack in enumerate(packs):
        start = pl.multiple_of(block_ref[k] * share, share)
        for i in range(count):
            whole_ref[pl.ds(start, share), i * columns : (i + 1) * columns] = pack[
                i * share : (i + 1) * share, queries : queries + columns
            ]


def attention_kernel(heads, block_ref, *refs):
    shards = len(refs) - 13
    packs = refs[:shards]
    normed_ref, low_ref, key_ref, bias_ref, cosine_ref, sine_ref = refs[shards : shards + 6]
    query_ref, keyval_ref, soft_ref, attended_ref, part_ref, total_ref, weight_ref = refs[
        shards + 6 :
    ]
    share = packs[0].shape[0]
    nope = heads * NOPE
    queries = heads * (NOPE + ROPE)
    keyval_columns = keyval_ref.shape[1] * (KVR // shards) // share
    keyval_weight(block_ref, packs, weight_ref, queries)
    for k, pack in enumerate(packs):
        start = pl.multiple_of(block_ref[k] * share, share)
        value = dot_nn(normed_ref[:, pl.ds(start, share)], pack[:, :queries])
        if k == 0:
            total_ref[...] = value
        else:
            total_ref[...] += value
    keyval_ref[...] = dot_nn(low_ref[...], weight_ref[...]).astype(BF16)
    first, second = rope_turn(
        total_ref[:, nope : nope + LANES], total_ref[:, nope + LANES :], cosine_ref[...], sine_ref[...]
    )
    query_ref[:, :nope] = total_ref[:, :nope].astype(BF16)
    query_ref[:, nope : nope + LANES] = first.astype(BF16)
    query_ref[:, nope + LANES :] = second.astype(BF16)
    for head in range(heads):
        mask = head_mask(head)
        at = head * (NOPE + VD)
        turned = jnp.concatenate([first * mask, second * mask], axis=1).astype(BF16)
        scores = dot_nt(
            query_ref[:, head * NOPE : (head + 1) * NOPE], keyval_ref[:, at : at + NOPE]
        ) + dot_nt(turned, key_ref[...])
        scores = scores * ((NOPE + ROPE) ** (-0.5)) + bias_ref[...]
        raised = jnp.exp(scores - jnp.max(scores, axis=-1, keepdims=True))
        soft = raised / jnp.sum(raised, axis=-1, keepdims=True)
        soft_ref[head] = soft
        attended_ref[:, head * VD : (head + 1) * VD] = dot_nn(
            soft.astype(BF16), keyval_ref[:, at + NOPE : at + NOPE + VD]
        ).astype(BF16)
    output = queries + keyval_columns
    columns = part_ref.shape[1] // shards
    for k, pack in enumerate(packs):
        start = pl.multiple_of(block_ref[k] * columns, columns)
        value = dot_nn(attended_ref[:, :share], pack[:, output : output + columns])
        for i in range(1, heads * VD // share):
            value += dot_nn(
                attended_ref[:, i * share : (i + 1) * share],
                pack[:, output + i * columns : output + (i + 1) * columns],
            )
        part_ref[:, pl.ds(start, columns)] = value.astype(BF16)


def attention_back_kernel(heads, depth, block_ref, *refs):
    shards = (len(refs) - 2 * depth - 22) // 2
    packs, refs = refs[:shards], refs[shards:]
    tokens, refs = refs[:depth], refs[depth:]
    grads, refs = refs[:depth], refs[depth:]
    (
        query_ref, keyval_ref, key_ref, soft_ref, attended_ref, comp_ref, low_ref, normed_ref,
        latent_ref, kv_gain_ref, cosine_ref, sine_ref, router_ref, ffn_gain_ref,
        grad_query_ref, grad_keyval_ref, grad_normed_ref, *chunk_refs,
        gains_ref, grad_attended_ref, weight_ref, back_ref, stage_ref,
    ) = refs
    share = packs[0].shape[0]
    nope = heads * NOPE
    queries = heads * (NOPE + ROPE)
    keyval_columns = keyval_ref.shape[1] * (KVR // shards) // share
    output = queries + keyval_columns
    columns = normed_ref.shape[1] // shards
    scale = (NOPE + ROPE) ** (-0.5)
    stage_ref[...] = jnp.concatenate([piece[...] for piece in grads], axis=0)
    blocks = heads * VD // share
    for i in range(blocks):
        value = None
        for k, pack in enumerate(packs):
            start = pl.multiple_of(block_ref[k] * columns, columns)
            part = dot_nt(
                stage_ref[:, pl.ds(start, columns)],
                pack[:, output + i * columns : output + (i + 1) * columns],
            )
            value = part if value is None else value + part
        grad_attended_ref[:, i * share : (i + 1) * share] = value.astype(BF16)
    cosine, sine = cosine_ref[...], sine_ref[...]
    turn_first, turn_second = None, None
    key_turn = None
    for head in range(heads):
        mask = head_mask(head)
        at = head * (NOPE + VD)
        soft = soft_ref[head]
        attended = attended_ref[:, head * VD : (head + 1) * VD]
        grad = grad_attended_ref[:, head * VD : (head + 1) * VD]
        delta = jnp.sum(grad.astype(F32) * attended.astype(F32), axis=-1, keepdims=True)
        grad_soft = dot_nt(grad, keyval_ref[:, at + NOPE : at + NOPE + VD])
        scores = (soft * (grad_soft - delta) * scale).astype(BF16)
        query = query_ref[:, head * NOPE : (head + 1) * NOPE]
        grad_query_ref[:, head * NOPE : (head + 1) * NOPE] = dot_nn(
            scores, keyval_ref[:, at : at + NOPE]
        ).astype(BF16)
        turned = dot_nn(scores, key_ref[...])
        first, second = turned[:, :LANES] * mask, turned[:, LANES:] * mask
        turn_first = first if turn_first is None else turn_first + first
        turn_second = second if turn_second is None else turn_second + second
        wide = jnp.concatenate([mask, mask], axis=1)
        masked = (query_ref[:, nope:].astype(F32) * wide).astype(BF16)
        part = dot_tn(scores, masked)
        key_turn = part if key_turn is None else key_turn + part
        grad_keyval_ref[:, at : at + NOPE] = dot_tn(scores, query).astype(BF16)
        grad_keyval_ref[:, at + NOPE : at + NOPE + VD] = dot_tn(soft.astype(BF16), grad).astype(BF16)
    first, second = rope_turn(turn_first, turn_second, cosine, -sine)
    grad_query_ref[:, nope : nope + LANES] = first.astype(BF16)
    grad_query_ref[:, nope + LANES :] = second.astype(BF16)
    keyval_weight(block_ref, packs, weight_ref, queries)
    grad_comp = dot_nt(grad_keyval_ref[...], weight_ref[...])
    compressed = comp_ref[...]
    inverse = lax.rsqrt(jnp.mean(compressed * compressed, axis=-1, keepdims=True) + EPSILON)
    weighted = grad_comp * kv_gain_ref[...]
    grad_compressed = inverse * weighted - compressed * (inverse * inverse * inverse) * jnp.mean(
        compressed * weighted, axis=-1, keepdims=True
    )
    gains_ref[...] = jnp.zeros_like(gains_ref)
    gains_ref[2:3, :KVR] = jnp.sum(grad_comp * compressed * inverse, axis=0, keepdims=True)
    back_ref[:, :KVR] = grad_compressed.astype(BF16)
    first, second = rope_turn(key_turn[:, :LANES], key_turn[:, LANES:], cosine, -sine)
    back_ref[:, KVR : KVR + LANES] = first.astype(BF16)
    back_ref[:, KVR + LANES :] = second.astype(BF16)
    unit = unit_rows(tokens)
    half = ROPE // 2
    for k, pack in enumerate(packs):
        start = pl.multiple_of(block_ref[k] * columns, columns)
        value = dot_nt(grad_query_ref[...], pack[:, :queries])
        value += dot_nn(back_ref[...], latent_ref[:, pl.ds(start, columns)])
        grad_normed_ref[:, pl.ds(start, columns)] = value.astype(BF16)
        weight = dot_tn(back_ref[...], normed_ref[:, pl.ds(start, columns)])
        turns = [
            sum(weight[KVR + i * LANES + j * half : KVR + i * LANES + (j + 1) * half] for j in range(heads))
            for i in range(2)
        ]
        chunk_refs[k][: KVR + ROPE] = jnp.concatenate([weight[:KVR]] + turns, axis=0).astype(BF16)
    gains_ref[0:1, :] = jnp.sum(grad_normed_ref[...].astype(F32) * unit, axis=0, keepdims=True)
    gains_ref[1:2, :] = ffn_gain_ref[...]
    used = KVR + ROPE
    for k in range(shards):
        at = pl.ds(pl.multiple_of(block_ref[k] * columns, columns), columns)
        chunk_refs[k][used : used + EXPERTS] = router_ref[:, at].astype(BF16)
        rows = [gains_ref[:2, at]]
        rows += [gains_ref[2:3, i * columns : (i + 1) * columns] for i in range(KVR // columns)]
        filled = 2 + KVR // columns
        rows.append(jnp.zeros((CHUNK_ROWS - used - EXPERTS - filled, columns), F32))
        chunk_refs[k][used + EXPERTS :] = jnp.concatenate(rows, axis=0).astype(BF16)


def attention_weights_kernel(heads, depth, block_ref, *refs):
    grads, refs = refs[:depth], refs[depth:]
    normed_ref, low_ref, attended_ref, query_ref, keyval_ref, *packs, stage_ref, whole_ref = refs
    shards, share = len(packs), packs[0].shape[0]
    queries = heads * (NOPE + ROPE)
    columns = normed_ref.shape[1] // shards
    part = KVR // shards
    count = share // part
    keyval_columns = keyval_ref.shape[1] // count
    output = queries + keyval_columns
    stage_ref[...] = jnp.concatenate([piece[...] for piece in grads], axis=0)
    whole_ref[...] = dot_tn(low_ref[...], keyval_ref[...]).astype(BF16)
    for k in range(shards):
        start = pl.multiple_of(block_ref[k] * columns, columns)
        packs[k][:, :queries] = dot_tn(
            normed_ref[:, pl.ds(start, columns)], query_ref[...]
        ).astype(BF16)
        rows = pl.ds(pl.multiple_of(block_ref[k] * part, part), part)
        for i in range(count):
            packs[k][i * part : (i + 1) * part, queries:output] = whole_ref[
                rows, i * keyval_columns : (i + 1) * keyval_columns
            ]
        value = dot_tn(attended_ref[...], stage_ref[:, pl.ds(start, columns)]).astype(BF16)
        for i in range(heads * VD // share):
            packs[k][:, output + i * columns : output + (i + 1) * columns] = value[
                i * share : (i + 1) * share
            ]


def vmem_call(kernel, name, blocks, operands, out_shape, scratch):
    if blocks is None:
        return pl.pallas_call(
            kernel,
            out_shape=out_shape,
            scratch_shapes=scratch,
            compiler_params=params(),
            name=name,
        )(*operands)
    return pl.pallas_call(
        kernel,
        grid_spec=pltpu.PrefetchScalarGridSpec(
            num_scalar_prefetch=1,
            grid=(1,),
            in_specs=[whole(a.shape) for a in operands],
            out_specs=[whole(a.shape) for a in out_shape],
            scratch_shapes=scratch,
        ),
        out_shape=out_shape,
        compiler_params=params("arbitrary"),
        name=name,
    )(blocks, *operands)


def latent_rows(pieces, gain, weight, kv_gain, cosine, sine):
    count = sum(piece.shape[0] for piece in pieces)
    width = pieces[0].shape[1]
    return vmem_call(
        functools.partial(latent_kernel, len(pieces)),
        "latent_rows",
        None,
        [*pieces, gain[None], weight, kv_gain[None], cosine, sine],
        [
            jax.ShapeDtypeStruct((count, width), BF16),
            jax.ShapeDtypeStruct((count, KVR), F32),
            jax.ShapeDtypeStruct((count, KVR), BF16),
            jax.ShapeDtypeStruct((count, 2 * LANES), BF16),
        ],
        [],
    )


def attention_forward(heads, blocks, packs, normed, low, key, bias, cosine, sine):
    count, width = normed.shape
    queries = heads * (NOPE + ROPE)
    keyval = heads * (NOPE + VD)
    return vmem_call(
        functools.partial(attention_kernel, heads),
        "attention_forward",
        blocks,
        [*packs, normed, low, key, bias, cosine, sine],
        [
            jax.ShapeDtypeStruct((count, queries), BF16),
            jax.ShapeDtypeStruct((count, keyval), BF16),
            jax.ShapeDtypeStruct((heads, count, count), F32),
            jax.ShapeDtypeStruct((count, heads * VD), BF16),
            jax.ShapeDtypeStruct((count, width), BF16),
        ],
        [pltpu.VMEM((count, queries), F32), pltpu.VMEM((KVR, keyval), BF16)],
    )


def attention_backward(
    heads, blocks, packs, tokens, grads, saved, latent, kv_gain, cosine, sine, router, ffn_gain
):
    query, keyval, key, soft, attended, compressed, low, normed = saved
    count, width = normed.shape
    shards = len(packs)
    return vmem_call(
        functools.partial(attention_back_kernel, heads, len(tokens)),
        "attention_backward",
        blocks,
        [
            *packs, *tokens, *grads, query, keyval, key, soft, attended, compressed, low, normed,
            latent, kv_gain[None], cosine, sine, router, ffn_gain[None],
        ],
        [
            jax.ShapeDtypeStruct(query.shape, BF16),
            jax.ShapeDtypeStruct(keyval.shape, BF16),
            jax.ShapeDtypeStruct((count, width), BF16),
        ]
        + [jax.ShapeDtypeStruct((CHUNK_ROWS, width // shards), BF16)] * shards,
        [
            pltpu.VMEM((8, width), F32),
            pltpu.VMEM((count, heads * VD), BF16),
            pltpu.VMEM((KVR, keyval.shape[1]), BF16),
            pltpu.VMEM((count, latent.shape[0]), BF16),
            pltpu.VMEM((count, width), BF16),
        ],
    )


def attention_weights(heads, blocks, shape, grads, normed, low, attended, grad_query, grad_keyval):
    count, width = normed.shape
    shards = blocks.shape[0]
    return vmem_call(
        functools.partial(attention_weights_kernel, heads, len(grads)),
        "attention_weights",
        blocks,
        [*grads, normed, low, attended, grad_query, grad_keyval],
        [jax.ShapeDtypeStruct(shape, BF16)] * shards,
        [pltpu.VMEM((count, width), BF16), pltpu.VMEM((KVR, grad_keyval.shape[1]), BF16)],
    )


def query_order(heads):
    size, half = NOPE + ROPE, ROPE // 2
    pieces = []
    for start, stop in ((0, NOPE), (NOPE, NOPE + half), (NOPE + half, size)):
        pieces += [(head * size + start, head * size + stop) for head in range(heads)]
    return pieces


def pack_weights(query, keyval, output, heads):
    share, columns = query.shape[0], output.shape[1]
    part = keyval.shape[0]
    count = share // part
    wide = keyval.shape[1] // count
    return jnp.concatenate(
        [query[:, start:stop] for start, stop in query_order(heads)]
        + [
            jnp.concatenate([keyval[:, i * wide : (i + 1) * wide] for i in range(count)], axis=0)
        ]
        + [output[i * share : (i + 1) * share] for i in range(output.shape[0] // share)],
        axis=1,
    )


def unpack_weights(pack, keyval_shape, output_shape, heads):
    size, half = NOPE + ROPE, ROPE // 2
    queries = heads * size
    share = pack.shape[0]
    part = keyval_shape[0]
    count = share // part
    wide = keyval_shape[1] // count
    nope = heads * NOPE
    query = []
    for head in range(heads):
        query += [
            pack[:, head * NOPE : (head + 1) * NOPE],
            pack[:, nope + head * half : nope + (head + 1) * half],
            pack[:, nope + (heads + head) * half : nope + (heads + head + 1) * half],
        ]
    keyval = jnp.concatenate(
        [pack[i * part : (i + 1) * part, queries : queries + wide] for i in range(count)], axis=1
    )
    at, columns = queries + wide, output_shape[1]
    output = jnp.concatenate(
        [
            pack[:, at + i * columns : at + (i + 1) * columns]
            for i in range(output_shape[0] // share)
        ],
        axis=0,
    )
    return jnp.concatenate(query, axis=1), keyval, output


def expert_layer(base, rows, grads, routes, router, expert_in, expert_out, shared):
    local, units, width = expert_out.shape
    sequences = len(rows)
    pairs = range(sequences // 2)
    shared_units = shared.shape[0] // 3
    side = jnp.concatenate([shared[: 2 * shared_units], router])
    shared_out = shared[2 * shared_units :]
    by_core = [jnp.concatenate(grads[core::2]) for core in range(2)]
    slot_grads, shared_raw = dispatch_grads(local, base, jnp.stack(routes), by_core, shared_out)
    raw = expert_raw(slot_grads, expert_out)
    held = [None] * 6
    for m in pairs:
        at = slice(2 * m, 2 * m + 2)
        held = dispatch_rows(
            m, sequences, local, base, routes[at], rows[at], side, shared_raw, held
        )
    slot_rows, infos, picks, gates, shared_hidden, shared_back = held
    back_rows, extra, hidden, back = expert_rows(
        slot_rows, infos, expert_in.reshape(local, 2 * units, width), raw
    )
    back_tokens, logits = [], [None]
    for m in pairs:
        tokens, logits = combine_back(
            m, picks, back_rows, extra, gates, shared_back, side, logits
        )
        back_tokens += tokens
    out_rows = expert_out_rows(hidden, expert_out)
    out_tokens = []
    for m in pairs:
        out_tokens += combine_out(m, picks, out_rows, shared_hidden, shared_out)
    grad_in, grad_out, _ = weight_grads(
        0, local, slot_rows, slot_grads, hidden, back, [None, None]
    )
    all_rows = jnp.stack(rows)
    grad_router = contract("set,std->ed", logits[0], all_rows)
    grad_shared = jnp.concatenate(
        [
            contract("sft,std->fd", shared_back, all_rows),
            contract("sft,std->fd", shared_hidden, jnp.stack(grads)),
        ]
    )
    return (
        out_tokens,
        back_tokens,
        grad_in.reshape(local, 2, units, width),
        grad_out,
        grad_router,
        grad_shared,
    )


def general_device(
    tokens_in,
    out_grad,
    routes,
    attn_gain,
    kv_gain,
    ffn_gain,
    w_query,
    w_latent,
    w_keyval,
    w_output,
    w_router,
    w_shared_in,
    w_shared_out,
    w_expert_in,
    w_expert_out,
):
    grid = Grid()
    depth = grid.depth
    own_depth = lax.axis_index("tensor")
    own_rows, width = tokens_in.shape
    row_count = own_rows * depth
    local_experts = w_expert_in.shape[0]
    base = lax.axis_index("expert") * local_experts
    stream = jnp.concatenate(grid.gather_depth(tokens_in)).astype(F32)
    full_query = grid.absolute(grid.gather(w_query), 0)
    full_keyval = grid.absolute(grid.gather(w_keyval), 0)
    full_output = grid.absolute(grid.gather(w_output), 1)
    all_grads = grid.gather(jnp.concatenate(grid.gather_depth(out_grad)))
    routes_rel = jnp.concatenate(grid.relative_depth(routes.T, 1), axis=1)
    routes_all = [routes_rel] + [grid.fetch(routes_rel, offset) for offset in grid.offsets[1:]]
    units = w_shared_out.shape[0] // grid.experts
    padding = ((0, -units % 32), (0, 0))
    padded_units = units + padding[0][1]
    shared_parts = [
        jnp.concatenate([jnp.pad(part, padding) for part in parts])
        for parts in zip(
            grid.relative(w_shared_in[0].T, 0),
            grid.relative(w_shared_in[1].T, 0),
            grid.relative(w_shared_out, 0),
        )
    ]
    shared = grid.absolute(grid.exchange(shared_parts), 1)
    position = (
        (own_depth + jnp.arange(row_count) // own_rows) % depth * own_rows
        + jnp.arange(row_count) % own_rows
    )
    local_heads = full_query.shape[1] // (NOPE + ROPE)
    cosine, sine_table = rope_tables(position)
    normed_one, inverse_one = rms_forward(stream, attn_gain)
    normed_one = normed_one.astype(BF16)
    queries = mix_dot(normed_one, full_query).reshape(row_count, local_heads, NOPE + ROPE)
    queries = jnp.concatenate(
        [
            queries[..., :NOPE],
            rotate(queries[..., NOPE:], cosine[:, None, :], sine_table[:, None, :]),
        ],
        axis=-1,
    ).astype(BF16)
    latent = mix_dot(normed_one, w_latent)
    compressed = latent[:, :KVR]
    comp_normed, comp_inverse = rms_forward(compressed, kv_gain)
    comp_normed = comp_normed.astype(BF16)
    key_rope = rotate(latent[:, KVR:], cosine, sine_table).astype(BF16)
    keyval = mix_dot(comp_normed, full_keyval).reshape(row_count, local_heads, NOPE + VD).astype(BF16)
    key_nope = keyval[..., :NOPE]
    values = keyval[..., NOPE:]
    scores = attention_scores(queries, key_nope, key_rope, position)
    top_score = jnp.max(scores, axis=-1, keepdims=True)
    raised = jnp.exp(scores - top_score)
    soft = raised / jnp.sum(raised, axis=-1, keepdims=True)
    soft_low = soft.astype(BF16)
    attended = contract("hqk,khv->qhv", soft_low, values).astype(BF16)
    attended_flat = attended.reshape(row_count, local_heads * VD)
    attention_part = mix_dot(attended_flat, full_output).astype(BF16)
    stream_own = tokens_in.astype(F32)
    residual = stream_own + grid.reduce_depth(split_rows(attention_part, depth))
    normed_two, inverse_two = rms_forward(residual, ffn_gain)
    normed_two = normed_two.astype(BF16)
    all_rows = grid.gather(jnp.concatenate(grid.gather_depth(normed_two)))
    router_rel = jnp.roll(w_router.T, -base, axis=0)
    (
        out_tokens,
        back_tokens,
        grad_expert_in,
        grad_expert_out,
        grad_router_rel,
        grad_shared,
    ) = expert_layer(
        base.astype(jnp.int32)[None],
        all_rows,
        all_grads,
        routes_all,
        router_rel,
        jnp.swapaxes(w_expert_in, 2, 3),
        w_expert_out,
        shared,
    )
    grad_normed = grid.reduce_depth(
        split_rows(grid.reduce(back_tokens).astype(BF16), depth)
    )
    ffn_total = grid.reduce_depth(split_rows(grid.reduce(out_tokens).astype(BF16), depth))
    block_out = (residual + ffn_total).astype(BF16)
    grad_float = out_grad.astype(F32)
    grad_res_part, grad_ffn_gain = rms_backward(residual, inverse_two, ffn_gain, grad_normed)
    grad_residual = grad_float + grad_res_part
    grad_res_low = jnp.concatenate(grid.gather_depth(grad_residual.astype(BF16)))
    grad_output = contract("tv,td->vd", attended_flat, grad_res_low).astype(BF16)
    sum_output = grid.reduce(grid.relative(grad_output, 1))
    grad_attended = (
        contract("td,vd->tv", grad_res_low, full_output)
        .astype(BF16)
        .reshape(row_count, local_heads, VD)
    )
    softmax_scale = (NOPE + ROPE) ** (-0.5)
    grad_soft = contract("qhv,khv->hqk", grad_attended, values)
    row_delta = jnp.sum(grad_attended.astype(F32) * attended.astype(F32), axis=-1).T
    grad_scores = (soft * (grad_soft - row_delta[..., None]) * softmax_scale).astype(BF16)
    grad_query_nope = contract("hqk,khd->qhd", grad_scores, key_nope)
    grad_query_rope = contract("hqk,kr->qhr", grad_scores, key_rope)
    grad_key_nope = contract("hqk,qhd->khd", grad_scores, queries[..., :NOPE])
    grad_key_rope = contract("hqk,qhr->kr", grad_scores, queries[..., NOPE:])
    grad_values = contract("hqk,qhv->khv", soft_low, grad_attended)
    grad_query_raw = (
        jnp.concatenate(
            [
                grad_query_nope,
                rotate(grad_query_rope, cosine[:, None, :], -sine_table[:, None, :]),
            ],
            axis=-1,
        )
        .reshape(row_count, local_heads * (NOPE + ROPE))
        .astype(BF16)
    )
    grad_query_weight = contract("td,tq->dq", normed_one, grad_query_raw).astype(BF16)
    grad_keyval = (
        jnp.concatenate([grad_key_nope, grad_values], axis=-1)
        .reshape(row_count, local_heads * (NOPE + VD))
        .astype(BF16)
    )
    grad_keyval_weight = contract("tc,tk->ck", comp_normed, grad_keyval).astype(BF16)
    sum_query = grid.reduce(grid.relative(grad_query_weight, 0))
    sum_keyval = grid.reduce(grid.relative(grad_keyval_weight, 0))
    grad_comp_normed = contract("tk,ck->tc", grad_keyval, full_keyval)
    grad_compressed, grad_kv_gain = rms_backward(
        compressed, comp_inverse, kv_gain, grad_comp_normed
    )
    grad_latent_out = jnp.concatenate(
        [grad_compressed, rotate(grad_key_rope, cosine, -sine_table)], axis=-1
    ).astype(BF16)
    grad_latent = contract("tk,td->kd", grad_latent_out, normed_one)
    grad_normed_one = contract("tq,dq->td", grad_query_raw, full_query) + contract(
        "tk,dk->td", grad_latent_out, w_latent
    )
    grad_normed_one = grid.reduce_depth(split_rows(grad_normed_one.astype(BF16), depth))
    inverse_own = inverse_one[:own_rows]
    grad_x_part, grad_attn_gain = rms_backward(stream_own, inverse_own, attn_gain, grad_normed_one)
    grad_in = grad_residual + grad_x_part
    grad_shared_parts = [part.astype(BF16) for part in grid.relative(grad_shared, 1)]
    returned = grid.exchange(grad_shared_parts)
    sum_shared_in = jnp.stack(
        [
            grid.absolute([part[:units] for part in returned], 0).T,
            grid.absolute([part[padded_units : padded_units + units] for part in returned], 0).T,
        ]
    ).astype(F32)
    sum_shared_out = grid.absolute([part[2 * padded_units : 2 * padded_units + units] for part in returned], 0).astype(F32)
    gains = jnp.stack(
        [grad_attn_gain, grad_ffn_gain, jnp.pad(grad_kv_gain, (0, width - KVR))]
    )
    replicated = jnp.concatenate([grad_latent, jnp.roll(grad_router_rel, base, axis=0), gains])
    used = replicated.shape[0]
    padded = -(-used // (16 * grid.experts)) * 16 * grid.experts
    replicated = jnp.pad(replicated, ((0, padded - used), (0, 0))).astype(BF16)
    chunk = grid.reduce(grid.relative(replicated, 0)).astype(BF16)
    part = grid.reduce_depth(grid.relative_depth(chunk, 1)).astype(BF16)
    chunk = grid.absolute_depth(grid.gather_depth(part), 1)
    whole = grid.absolute(grid.gather(chunk), 0).astype(F32)
    sum_latent = whole[: KVR + ROPE].T
    sum_router = whole[KVR + ROPE : KVR + ROPE + EXPERTS].T
    sum_attn_gain = whole[KVR + ROPE + EXPERTS]
    sum_ffn_gain = whole[KVR + ROPE + EXPERTS + 1]
    sum_kv_gain = whole[KVR + ROPE + EXPERTS + 2, :KVR]
    return (
        block_out,
        grad_in,
        sum_attn_gain,
        sum_kv_gain,
        sum_ffn_gain,
        sum_query,
        sum_latent,
        sum_keyval,
        sum_output,
        sum_router,
        sum_shared_in,
        sum_shared_out,
        jnp.swapaxes(grad_expert_in, 2, 3),
        grad_expert_out,
    )


def after(array, *earlier):
    return lax.optimization_barrier((array, *earlier))[0]


def square_device(
    tokens_in,
    out_grad,
    routes,
    attn_gain,
    kv_gain,
    ffn_gain,
    w_query,
    w_latent,
    w_keyval,
    w_output,
    w_router,
    w_shared_in,
    w_shared_out,
    w_expert_in,
    w_expert_out,
):
    grid = Grid()
    depth = grid.depth
    sequences = grid.experts
    pairs = range(sequences // 2)
    own_rows, width = tokens_in.shape
    row_count = own_rows * depth
    local = w_expert_in.shape[0]
    hidden_units = w_expert_out.shape[1]
    heads = w_query.shape[1] // (NOPE + ROPE)
    own_depth = lax.axis_index("tensor")
    blocks = jnp.stack([grid.place_of(offset) for offset in grid.offsets]).astype(jnp.int32)
    depths = ((own_depth + jnp.arange(depth)) % depth).astype(jnp.int32)
    base = (lax.axis_index("expert") * local).astype(jnp.int32)[None]

    tokens = grid.ring_gather(tokens_in)
    quarter = own_rows // 2
    along_x = grid.fetch(out_grad, (0, 1, 0))
    along_y = grid.fetch(out_grad, (1, 0, 0))
    crossed = [
        grid.fetch(along_x[:quarter], (1, 0, 0)),
        grid.fetch(along_y[quarter:], (0, 1, 0)),
    ]
    plane = jnp.concatenate([out_grad, along_x, along_y, *crossed])
    packs = grid.gather(
        after(pack_weights(w_query, w_keyval, w_output, heads), *crossed, tokens[1], tokens[4])
    )
    planes = grid.ring_near(after(plane, *tokens))
    far = jnp.concatenate(grid.ring_far(*planes))
    routes_t = jnp.concatenate(grid.relative_depth(routes.T, 1), axis=1)
    routes_all = grid.gather_small(routes_t)

    position = (
        (own_depth + jnp.arange(row_count) // own_rows) % depth * own_rows
        + jnp.arange(row_count) % own_rows
    )
    cosine, sine = (jnp.tile(table, (1, heads)) for table in rope_tables(position))
    bias = jnp.where(position[None, :] <= position[:, None], 0.0, -1e30).astype(F32)
    half = ROPE // 2
    latent_t = w_latent.T
    latent_t = jnp.concatenate(
        [latent_t[:KVR]] + [latent_t[KVR : KVR + half]] * heads + [latent_t[KVR + half :]] * heads
    )
    normed, compressed, low, key = latent_rows(
        tokens, attn_gain, latent_t, kv_gain, cosine, sine
    )

    units = w_shared_out.shape[0] // grid.experts
    padding = ((0, -units % 32), (0, 0))
    shared_parts = [
        jnp.concatenate([jnp.pad(part, padding) for part in parts])
        for parts in zip(
            grid.relative(w_shared_in[0].T, 0),
            grid.relative(w_shared_in[1].T, 0),
            grid.relative(w_shared_out, 0),
        )
    ]
    pieces = grid.exchange([after(part, packs[2], packs[4]) for part in shared_parts])
    router = jnp.roll(w_router.T, -base[0], axis=0)
    padded_units = units + padding[0][1]
    side, shared_out = vmem_call(
        join_columns_kernel,
        "join_columns",
        blocks,
        [*pieces, router],
        [
            jax.ShapeDtypeStruct((2 * padded_units + EXPERTS, width), BF16),
            jax.ShapeDtypeStruct((padded_units, width), BF16),
        ],
        [],
    )

    query, keyval, soft, attended, part = attention_forward(
        heads, blocks, packs, after(normed, far), low, key, bias, cosine, sine
    )
    core_grads = [plane, planes[0], far, planes[1]]
    all_grads = core_grads + [grid.fetch(piece, (0, 0, 1)) for piece in core_grads]
    stream = tokens_in.astype(F32)
    residual = stream + grid.ring_reduce(split_rows(part, depth))
    normed_two, inverse_two = rms_forward(residual, ffn_gain)
    normed_two = normed_two.astype(BF16)

    near_rows = grid.ring_near(after(normed_two, *routes_all))
    far_rows = grid.ring_far(*near_rows)
    group_rows = jnp.concatenate([normed_two, near_rows[0], *far_rows, near_rows[1]])
    group_rows = after(group_rows, *pieces)
    middle = row_count // 2
    along_x = grid.fetch(group_rows, (0, 1, 0))
    along_y = grid.fetch(group_rows, (1, 0, 0))
    pair_rows = grid.fetch(group_rows, (0, 0, 1))
    slot_grads, shared_raw = dispatch_grads(
        local, base, jnp.stack(routes_all), all_grads, after(shared_out, group_rows)
    )
    along_x, along_y = after(along_x, slot_grads), after(along_y, slot_grads)
    first = grid.fetch(along_x[:middle], (1, 0, 0))
    second = grid.fetch(along_y[middle:], (0, 1, 0))
    raw = expert_raw(after(slot_grads, along_x, along_y), w_expert_out)
    first, second = after(first, raw), after(second, raw)
    rows = [group_rows, pair_rows]
    for held in (along_x, along_y):
        rows += [held, grid.fetch(held, (0, 0, 1))]
    rows += [
        jnp.concatenate([first, second]),
        jnp.concatenate([grid.fetch(first, (0, 0, 1)), grid.fetch(second, (0, 0, 1))]),
    ]

    held = [None] * 6
    for m in pairs:
        held = dispatch_rows(
            m,
            sequences,
            local,
            base,
            routes_all[2 * m : 2 * m + 2],
            rows[2 * m : 2 * m + 2],
            side,
            shared_raw,
            held,
        )
    slot_rows, infos, picks, gates, shared_hidden, shared_back = held
    expert_in = jnp.swapaxes(w_expert_in, 2, 3).reshape(local, 2 * hidden_units, width)
    back_rows, extra, hidden, back = expert_rows(slot_rows, infos, expert_in, raw)

    def backs(m, logits, *earlier):
        return combine_back(
            m, picks, after(back_rows, *earlier), extra, gates, shared_back, side, logits
        )

    front, rear = slice(None, row_count // 2), slice(row_count // 2, None)
    (near_6, far_6), logits = backs(3, [None])
    (near_4, far_4), logits = backs(2, logits, near_6)
    own_6 = low_add(near_6, grid.send(far_6, (0, 0, 1)))
    first = grid.send(own_6[front], (0, 1, 0))
    second = grid.send(own_6[rear], (1, 0, 0))
    (near_2, far_2), logits = backs(1, logits, own_6)
    own_4 = low_add(near_4, grid.send(far_4, (0, 0, 1)))
    (near_0, far_0), logits = backs(0, logits, own_4)
    own_2 = low_add(near_2, grid.send(far_2, (0, 0, 1)))
    first, second = after(first, near_0), after(second, near_0)
    to_y = jnp.concatenate([low_add(own_4[front], first), own_4[rear]])
    to_x = jnp.concatenate([own_2[front], low_add(own_2[rear], second)])
    from_x = grid.send(to_x, (0, 1, 0))
    from_y = grid.send(to_y, (1, 0, 0))

    def outs(m, *earlier):
        return combine_out(m, picks, after(out_rows, *earlier), shared_hidden, shared_out)

    out_rows = expert_out_rows(after(hidden, to_x, to_y), w_expert_out)
    own_0 = low_add(near_0, grid.send(far_0, (0, 0, 1)))
    out_6, out_7 = outs(3)
    out_4, out_5 = outs(2, out_6)
    from_x, from_y = after(from_x, out_4), after(from_y, out_4)
    grad_group = (own_0.astype(F32) + from_x.astype(F32) + from_y.astype(F32)).astype(BF16)
    chunks = split_rows(grad_group, depth)
    first, second = grid.ring_start(chunks)
    out_own_6 = low_add(after(out_6, grad_group), grid.send(after(out_7, grad_group), (0, 0, 1)))
    out_own_4 = low_add(out_4, grid.send(after(out_5, grad_group), (0, 0, 1)))
    out_first = grid.send(out_own_6[front], (0, 1, 0))
    out_second = grid.send(out_own_6[rear], (1, 0, 0))
    out_2, out_3 = outs(1, grad_group)
    first, second = after(first, out_2), after(second, out_2)
    ahead, behind, marks = grid.ring_finish(chunks, first, second)
    out_0, out_1 = outs(0, *marks)
    ahead, behind = after(ahead, out_0), after(behind, out_0)
    grad_normed = chunks[0].astype(F32) + ahead.astype(F32) + behind.astype(F32)

    grad_res_part, grad_ffn_gain = rms_backward(residual, inverse_two, ffn_gain, grad_normed)
    grad_residual = out_grad.astype(F32) + grad_res_part
    grad_low = grad_residual.astype(BF16)
    near_grads = grid.ring_near(grad_low)
    out_own_2 = low_add(out_2, grid.send(out_3, (0, 0, 1)))
    out_own_0 = low_add(out_0, grid.send(out_1, (0, 0, 1)))
    out_to_y = jnp.concatenate([low_add(out_own_4[front], out_first), out_own_4[rear]])
    out_to_x = jnp.concatenate([out_own_2[front], low_add(out_own_2[rear], out_second)])
    out_from_x = grid.send(out_to_x, (0, 1, 0))
    out_from_y = grid.send(out_to_y, (1, 0, 0))
    *grad_parts, grad_router = side_grads(
        blocks, base, rows, all_grads, after(logits[0], grad_low, out_to_x, out_to_y), shared_hidden, shared_back
    )
    out_from_x, out_from_y = after(out_from_x, grad_router), after(out_from_y, grad_router)
    far_grads = grid.ring_far(*near_grads)
    grads = [grad_low, near_grads[0], *(after(piece, grad_router) for piece in far_grads), near_grads[1]]

    returned = grid.exchange(grad_parts)
    grads[0] = after(grads[0], out_from_x, out_from_y)
    grad_query, grad_keyval, grad_normed_one, *chunks = attention_backward(
        heads,
        blocks,
        packs,
        tokens,
        grads,
        (query, keyval, key, soft, attended, compressed, low, normed),
        latent_t,
        kv_gain,
        cosine,
        sine,
        grad_router,
        grad_ffn_gain,
    )
    out_group = (
        out_own_0.astype(F32)
        + out_from_x.astype(F32)
        + out_from_y.astype(F32)
    ).astype(BF16)
    grad_packs = attention_weights(
        heads,
        blocks,
        packs[0].shape,
        grads,
        normed,
        low,
        attended,
        after(grad_query, *returned),
        grad_keyval,
    )
    ffn_total = grid.ring_reduce(split_rows(after(out_group, grad_query), depth))
    block_out = (residual + ffn_total).astype(BF16)
    sums, chunk_first, chunk_mark = grid.reduce_parts(chunks)
    share = local // 4
    held = [None, None]

    def weights(step, held, *earlier):
        return weight_grads(
            step * share,
            (step + 1) * share,
            after(slot_rows, *earlier),
            slot_grads,
            hidden,
            back,
            held[:2],
        )

    held = weights(0, held, grad_packs[0], chunk_first)
    held = weights(1, held, held[2], *chunk_mark)
    mark = held[2]
    size = CHUNK_ROWS // depth
    columns = width // grid.experts
    parts = vmem_call(
        sum_split_kernel,
        "sum_split",
        depths,
        [sums[0], after(sums[1], mark), after(sums[2], mark)],
        [jax.ShapeDtypeStruct((size, columns), BF16)] * depth,
        [],
    )
    pack_sums, pack_first, pack_mark = grid.reduce_parts([after(pack, mark) for pack in grad_packs])
    held = weights(2, held, parts[0], pack_first)
    part = grid.reduce_depth([parts[0]] + [after(part, pack_first) for part in parts[1:]])
    part = after(part, held[2]).astype(BF16)
    *held, mark = weights(3, held, part, *pack_mark)
    grad_expert_in, grad_expert_out = held
    parts = [after(piece, mark) for piece in grid.gather_depth(part)]
    sum_shared_in, sum_shared_out = vmem_call(
        functools.partial(join_rows_kernel, units),
        "join_rows",
        blocks,
        [after(returned[0], mark), *returned[1:]],
        [
            jax.ShapeDtypeStruct((2, units * grid.experts, width // grid.experts), F32),
            jax.ShapeDtypeStruct((units * grid.experts, width // grid.experts), F32),
        ],
        [],
    )
    (chunk,) = vmem_call(
        join_depth_kernel,
        "join_depth",
        depths,
        parts,
        [jax.ShapeDtypeStruct((CHUNK_ROWS, columns), BF16)],
        [],
    )
    sum_latent, sum_router, sum_gains = vmem_call(
        functools.partial(replicated_kernel, KVR + ROPE),
        "replicated",
        blocks,
        grid.gather(chunk),
        [
            jax.ShapeDtypeStruct((KVR + ROPE, width), F32),
            jax.ShapeDtypeStruct((EXPERTS, width), F32),
            jax.ShapeDtypeStruct((16, width), F32),
        ],
        [],
    )
    sum_kv_gain = sum_gains[2 : 2 + KVR // columns, :columns].reshape(KVR)

    grad_normed_one = grid.ring_reduce(split_rows(grad_normed_one, depth))
    inverse_one = lax.rsqrt(jnp.mean(stream * stream, axis=-1, keepdims=True) + EPSILON)
    grad_in = grad_residual + rms_backward(stream, inverse_one, attn_gain, grad_normed_one)[0]
    sum_query, sum_keyval, sum_output = unpack_weights(
        sum(array.astype(F32) for array in pack_sums), w_keyval.shape, w_output.shape, heads
    )
    return (
        block_out,
        grad_in,
        sum_gains[0],
        sum_kv_gain,
        sum_gains[1],
        sum_query,
        sum_latent.T,
        sum_keyval,
        sum_output,
        sum_router.T,
        jnp.swapaxes(sum_shared_in, 1, 2),
        sum_shared_out,
        jnp.swapaxes(grad_expert_in.reshape(local, 2, hidden_units, width), 2, 3),
        grad_expert_out,
    )


def solution(mesh):
    placed = (
        P(("expert", "tensor"), None),
        P(("expert", "tensor"), None),
        P("expert", None),
        P(),
        P(),
        P(),
        P("expert", "tensor"),
        P(),
        P("expert", "tensor"),
        P("tensor", "expert"),
        P(),
        P(None, "expert", "tensor"),
        P("tensor", "expert"),
        P("expert", None, None, "tensor"),
        P("expert", "tensor", None),
    )
    square = mesh.shape["expert"] == 8 and mesh.shape["tensor"] == 4
    return jax.shard_map(
        square_device if square else general_device,
        mesh=mesh,
        in_specs=placed,
        out_specs=(
            P(("expert", "tensor"), None),
            P(("expert", "tensor"), None),
            P(),
            P(),
            P(),
            P("expert", "tensor"),
            P(),
            P("expert", "tensor"),
            P("tensor", "expert"),
            P(),
            P(None, "expert", "tensor"),
            P("tensor", "expert"),
            P("expert", None, None, "tensor"),
            P("expert", "tensor", None),
        ),
        check_vma=False,
    )
```

```python
import functools
import math

import jax
import jax.numpy as jnp
from jax import lax
from jax.experimental import pallas as pl
from jax.experimental.pallas import tpu as pltpu
from jax.sharding import PartitionSpec as P

NOPE = 128
ROPE = 64
VD = 128
KVR = 512
EXPERTS = 64
TOP = 6
SLOTS = 32
SLOT_BLOCK = 256
LANES = 128
PARTS = 2
CHUNK_ROWS = 704

EPSILON = 1e-06
ROUTE_SCALE = 2.446
ROPE_BASE = 50000.0
BF16 = jnp.bfloat16
F32 = jnp.float32


def mix_dot(left_side, right_side):
    return jnp.dot(left_side, right_side, preferred_element_type=F32)


def contract(pattern, left_side, right_side):
    return jnp.einsum(pattern, left_side, right_side, preferred_element_type=F32)


def rms_forward(values, gain_vec):
    inverse = lax.rsqrt(jnp.mean(values * values, axis=-1, keepdims=True) + EPSILON)
    return (values * inverse * gain_vec, inverse)


def rms_backward(values, inverse, gain_vec, grad_normed):
    weighted = grad_normed * gain_vec
    grad_values = inverse * weighted - values * (inverse * inverse * inverse) * jnp.mean(
        values * weighted, axis=-1, keepdims=True
    )
    grad_gain = jnp.sum(grad_normed * values * inverse, axis=0)
    return (grad_values, grad_gain)


def rope_tables(position):
    half_rope = ROPE // 2
    frequency = jnp.exp(-jnp.log(ROPE_BASE) * jnp.arange(half_rope).astype(F32) / half_rope)
    angles = position.astype(F32)[:, None] * frequency[None, :]
    return (jnp.cos(angles), jnp.sin(angles))


def rotate(columns, cosine, sine_table):
    half_rope = columns.shape[-1] // 2
    first_half = columns[..., :half_rope]
    second_half = columns[..., half_rope:]
    return jnp.concatenate(
        [
            first_half * cosine - second_half * sine_table,
            first_half * sine_table + second_half * cosine,
        ],
        axis=-1,
    )


def low_add(first, second):
    return (first.astype(F32) + second.astype(F32)).astype(BF16)


class Grid:
    def __init__(self):
        self.experts = lax.axis_size("expert")
        self.depth = lax.axis_size("tensor")
        self.side = math.isqrt(self.experts // 2)
        assert self.side * self.side * 2 == self.experts
        self.offsets = [
            (dy, dx, dc)
            for dy in range(self.side)
            for dx in range(self.side)
            for dc in range(2)
        ]

    def neighbour(self, place, offset):
        side = self.side
        y, x, core = place // (2 * side), place // 2 % side, place % 2
        dy, dx, dc = offset
        return (((y + dy) % side) * side + (x + dx) % side) * 2 + (core + dc) % 2

    def place_of(self, offset):
        return self.neighbour(lax.axis_index("expert"), offset)

    def fetch(self, array, offset):
        pairs = [(self.neighbour(place, offset), place) for place in range(self.experts)]
        return lax.ppermute(array, "expert", pairs)

    def send(self, array, offset):
        pairs = [(place, self.neighbour(place, offset)) for place in range(self.experts)]
        return lax.ppermute(array, "expert", pairs)

    def gather(self, shard):
        if self.side != 2:
            return [shard] + [self.fetch(shard, offset) for offset in self.offsets[1:]]
        half = shard.shape[0] // 2
        along_x = self.fetch(shard, (0, 1, 0))
        along_y = self.fetch(shard, (1, 0, 0))
        pair = self.fetch(shard, (0, 0, 1))
        first = self.fetch(along_x[:half], (1, 0, 0))
        second = self.fetch(along_y[half:], (0, 1, 0))
        pair_x = self.fetch(along_x, (0, 0, 1))
        pair_y = self.fetch(along_y, (0, 0, 1))
        pair_first = self.fetch(first, (0, 0, 1))
        pair_second = self.fetch(second, (0, 0, 1))
        return [
            shard,
            pair,
            along_x,
            pair_x,
            along_y,
            pair_y,
            jnp.concatenate([first, second]),
            jnp.concatenate([pair_first, pair_second]),
        ]

    def reduce(self, chunks):
        if self.side != 2:
            total = chunks[0].astype(F32)
            for offset, chunk in zip(self.offsets[1:], chunks[1:]):
                total = total + self.send(chunk, offset).astype(F32)
            return total
        half = chunks[0].shape[0] // 2
        own = {}
        for place in (6, 2, 4, 0):
            own[place] = low_add(chunks[place], self.send(chunks[place + 1], (0, 0, 1)))
        first = self.send(own[6][:half], (0, 1, 0))
        second = self.send(own[6][half:], (1, 0, 0))
        to_y = jnp.concatenate([low_add(own[4][:half], first), own[4][half:]])
        to_x = jnp.concatenate([own[2][:half], low_add(own[2][half:], second)])
        from_x = self.send(to_x, (0, 1, 0))
        from_y = self.send(to_y, (1, 0, 0))
        return own[0].astype(F32) + from_x.astype(F32) + from_y.astype(F32)

    def gather_small(self, shard):
        along_x = self.fetch(shard, (0, 1, 0))
        along_y = self.fetch(shard, (1, 0, 0))
        near = [shard, along_x, along_y, self.fetch(along_x, (1, 0, 0))]
        return [piece for held in near for piece in (held, self.fetch(held, (0, 0, 1)))]

    def exchange(self, parts):
        pieces = [parts[0]]
        for dy, dx, dc in self.offsets[1:]:
            back = (-dy % self.side, -dx % self.side, dc)
            pieces.append(self.send(parts[self.offsets.index(back)], back))
        return pieces

    def reduce_parts(self, chunks):
        half = chunks[0].shape[0] // 2
        own = {}
        for place in (6, 2, 4, 0):
            own[place] = low_add(chunks[place], self.send(chunks[place + 1], (0, 0, 1)))
        first = self.send(own[6][:half], (0, 1, 0))
        second = self.send(own[6][half:], (1, 0, 0))
        to_y = jnp.concatenate([low_add(own[4][:half], first), own[4][half:]])
        to_x = jnp.concatenate([own[2][:half], low_add(own[2][half:], second)])
        from_x = self.send(to_x, (0, 1, 0))
        from_y = self.send(to_y, (1, 0, 0))
        return [own[0], from_x, from_y], own[6], (to_x, to_y)

    def ring(self, array, step):
        depth = self.depth
        return lax.ppermute(array, "tensor", [(i, (i + step) % depth) for i in range(depth)])

    def ring_near(self, shard):
        return self.ring(shard, -1), self.ring(shard, 1)

    def ring_far(self, ahead, behind):
        half = ahead.shape[0] // 2
        return self.ring(ahead[:half], -1), self.ring(behind[half:], 1)

    def ring_gather(self, shard):
        ahead, behind = self.ring_near(shard)
        return [shard, ahead, *self.ring_far(ahead, behind), behind]

    def ring_start(self, chunks):
        half = chunks[2].shape[0] // 2
        first = self.ring(chunks[2][:half], 1)
        second = self.ring(chunks[2][half:], -1)
        return first, second

    def ring_finish(self, chunks, first, second):
        half = chunks[2].shape[0] // 2
        to_ahead = jnp.concatenate([low_add(chunks[1][:half], first), chunks[1][half:]])
        to_behind = jnp.concatenate([chunks[3][:half], low_add(chunks[3][half:], second)])
        return self.ring(to_ahead, 1), self.ring(to_behind, -1), (to_ahead, to_behind)

    def ring_reduce(self, chunks):
        ahead, behind, _ = self.ring_finish(chunks, *self.ring_start(chunks))
        return chunks[0].astype(F32) + ahead.astype(F32) + behind.astype(F32)

    def gather_depth(self, shard):
        depth = self.depth
        return [shard] + [
            lax.ppermute(shard, "tensor", [((i + k) % depth, i) for i in range(depth)])
            for k in range(1, depth)
        ]

    def reduce_depth(self, chunks):
        depth = self.depth
        total = chunks[0].astype(F32)
        for k in range(1, depth):
            total = total + lax.ppermute(
                chunks[k], "tensor", [(i, (i + k) % depth) for i in range(depth)]
            ).astype(F32)
        return total

    def absolute(self, pieces, axis):
        size = pieces[0].shape[axis]
        shape = list(pieces[0].shape)
        shape[axis] = size * self.experts
        whole = jnp.zeros(shape, pieces[0].dtype)
        for offset, piece in zip(self.offsets, pieces):
            whole = lax.dynamic_update_slice_in_dim(
                whole, piece, self.place_of(offset) * size, axis
            )
        return whole

    def relative(self, whole, axis):
        size = whole.shape[axis] // self.experts
        return [
            lax.dynamic_slice_in_dim(whole, self.place_of(offset) * size, size, axis)
            for offset in self.offsets
        ]

    def absolute_depth(self, pieces, axis):
        size = pieces[0].shape[axis]
        shape = list(pieces[0].shape)
        shape[axis] = size * self.depth
        whole = jnp.zeros(shape, pieces[0].dtype)
        own = lax.axis_index("tensor")
        for k, piece in enumerate(pieces):
            whole = lax.dynamic_update_slice_in_dim(
                whole, piece, (own + k) % self.depth * size, axis
            )
        return whole

    def relative_depth(self, whole, axis):
        size = whole.shape[axis] // self.depth
        own = lax.axis_index("tensor")
        return [
            lax.dynamic_slice_in_dim(whole, (own + k) % self.depth * size, size, axis)
            for k in range(self.depth)
        ]


def split_rows(array, count):
    size = array.shape[0] // count
    return [array[i * size : (i + 1) * size] for i in range(count)]


def attention_scores(queries, key_nope, key_rope, position):
    scores = contract("qhd,khd->hqk", queries[..., :NOPE], key_nope) + contract(
        "qhr,kr->hqk", queries[..., NOPE:], key_rope
    )
    scores = scores * ((NOPE + ROPE) ** (-0.5))
    allowed = position[None, :] <= position[:, None]
    return jnp.where(allowed[None], scores, -1e30)


def dot_nn(left, right):
    return lax.dot_general(left, right, (((1,), (0,)), ((), ())), preferred_element_type=F32)


def dot_nt(left, right):
    return lax.dot_general(left, right, (((1,), (1,)), ((), ())), preferred_element_type=F32)


def dot_tn(left, right):
    return lax.dot_general(left, right, (((0,), (0,)), ((), ())), preferred_element_type=F32)


def silu_parts(gate):
    sigmoid = 1.0 / (1.0 + jnp.exp(-gate))
    return sigmoid, gate * sigmoid


def split_high(value):
    high = value.astype(BF16)
    return high, (value - high.astype(F32)).astype(BF16)


def whole(shape):
    return pl.BlockSpec(shape, lambda *_: (0,) * len(shape))


def params(*semantics):
    return pltpu.CompilerParams(
        dimension_semantics=semantics or None, vmem_limit_bytes=56 * 1024 * 1024
    )


ANYWHERE = pl.BlockSpec(memory_space=pl.ANY)


def pick_rows(routes, base, local):
    count = routes.shape[1]
    expert = lax.broadcasted_iota(jnp.int32, (EXPERTS, count), 0) + base
    expert = jnp.where(expert >= EXPERTS, expert - EXPERTS, expert)
    chosen = expert == routes[0:1]
    for k in range(1, TOP):
        chosen = chosen | (expert == routes[k : k + 1])
    chosen = chosen.astype(F32)
    rows = max(local, 16)
    earlier = lax.broadcasted_iota(jnp.int32, (count, count), 0) < lax.broadcasted_iota(
        jnp.int32, (count, count), 1
    )
    rank = dot_nn(chosen[:rows].astype(BF16), earlier.astype(F32).astype(BF16))
    rank = jnp.where(chosen[:rows] > 0.5, rank, -1.0)
    slot = lax.broadcasted_iota(jnp.int32, (SLOTS, count), 0).astype(F32)
    parts = [(slot == rank[j : j + 1]).astype(F32) for j in range(local)]
    return jnp.concatenate(parts, axis=0), chosen


def dispatch_grads_kernel(local, base_ref, *refs):
    routes, grads, shared_ref = refs[:2], refs[2:4], refs[4]
    slot_ref, raw_ref = refs[-2:]
    for i in range(2):

        @pl.when(pl.program_id(0) == i)
        def _():
            pick, _ = pick_rows(routes[i][...], base_ref[0], local)
            values = grads[i][...]
            slot_ref[...] = (
                dot_nn(pick.astype(BF16), values).astype(BF16).reshape(slot_ref.shape)
            )
            raw_ref[0] = dot_nt(shared_ref[...], values)


def dispatch_rows_kernel(local, units, base_ref, *refs):
    routes, pieces, side_ref, raw_ref = refs[:2], refs[2:4], refs[4], refs[5]
    slot_ref, info_ref, pick_ref, gate_ref, hidden_ref, back_ref = refs[-6:]
    for i in range(2):

        @pl.when(pl.program_id(0) == i)
        def _():
            pick, chosen = pick_rows(routes[i][...], base_ref[0], local)
            rows = pieces[i][...]
            low = pick.astype(BF16)
            pick_ref[0] = low
            slot_ref[...] = dot_nn(low, rows).astype(BF16).reshape(slot_ref.shape)
            side = dot_nt(side_ref[...], rows)
            gate, up, raw = side[:units], side[units : 2 * units], raw_ref[0]
            sigmoid = chosen / (1.0 + jnp.exp(-side[2 * units :]))
            total = jnp.sum(sigmoid, axis=0, keepdims=True)
            gate_ref[0, 0] = sigmoid
            gate_ref[0, 1] = jnp.broadcast_to(total, sigmoid.shape)
            weight = ROUTE_SCALE * sigmoid / total
            scale = jnp.concatenate(
                [
                    jnp.sum(
                        pick[j * SLOTS : (j + 1) * SLOTS] * weight[j : j + 1],
                        axis=1,
                        keepdims=True,
                    )
                    for j in range(local)
                ],
                axis=0,
            )
            high, low_part = split_high(scale)
            lane = lax.broadcasted_iota(jnp.int32, (scale.shape[0], LANES), 1)
            info = jnp.where(
                lane == 0, high.astype(F32), jnp.where(lane == 1, low_part.astype(F32), 0.0)
            )
            info_ref[...] = info.astype(BF16).reshape(info_ref.shape)
            smooth, active = silu_parts(gate)
            hidden_ref[0] = (active * up).astype(BF16)
            back_ref[0] = jnp.concatenate(
                [raw * up * smooth * (1.0 + gate * (1.0 - smooth)), raw * active], axis=0
            ).astype(BF16)


def expert_raw_kernel(grads_ref, out_ref, raw_ref):
    raw_ref[0] = dot_nt(out_ref[0], grads_ref[0])


def expert_kernel(
    units, rows_ref, info_ref, in_ref, raw_ref, back_rows_ref, extra_ref, hidden_ref, back_ref
):
    expert = pl.program_id(0)
    weight_in = in_ref[0]
    gates = dot_nt(weight_in, rows_ref[0])
    raw = raw_ref[0]
    gate, up = gates[:units], gates[units:]
    lane = lax.broadcasted_iota(jnp.int32, (16, LANES), 1)
    select = (lane < 2).astype(F32).astype(BF16)
    scale = dot_nt(select, info_ref[0])[0:1]
    smooth, active = silu_parts(gate)
    hidden = active * up
    grad_gate = jnp.sum(hidden.astype(BF16).astype(F32) * raw, axis=0, keepdims=True)
    hidden_ref[0] = (hidden * scale).astype(BF16)
    raw = raw * scale
    back = jnp.concatenate(
        [raw * up * smooth * (1.0 + gate * (1.0 - smooth)), raw * active], axis=0
    ).astype(BF16)
    back_ref[0] = back
    back_rows_ref[0] = dot_tn(back, weight_in).astype(BF16)
    high, low = split_high(grad_gate)
    row = lax.broadcasted_iota(jnp.int32, (16, grad_gate.shape[1]), 0)
    pair = jnp.where(row == 0, high.astype(F32), jnp.where(row == 1, low.astype(F32), 0.0))
    row = lax.broadcasted_iota(jnp.int32, (16, LANES), 0)
    lane = lax.broadcasted_iota(jnp.int32, (16, LANES), 1)
    place = ((row < 2) & (lane == expert + row * EXPERTS)).astype(F32)
    extra_ref[0] = dot_tn(pair.astype(BF16), place.astype(BF16)).astype(BF16)


def expert_out_kernel(hidden_ref, out_ref, rows_ref):
    rows_ref[0] = dot_tn(hidden_ref[0], out_ref[0]).astype(BF16)


def weight_grad_kernel(rows_ref, grads_ref, hidden_ref, back_ref, *rest):
    in_ref, out_ref, mark_ref = rest[-3:]
    mark_ref[...] = jnp.zeros_like(mark_ref)

    @pl.when(pl.program_id(1) == 0)
    def _():
        in_ref[0] = dot_nn(back_ref[0], rows_ref[0])
        out_ref[0] = dot_nn(hidden_ref[0], grads_ref[0])

    @pl.when(pl.program_id(1) > 0)
    def _():
        in_ref[0] += dot_nn(back_ref[0], rows_ref[0])
        out_ref[0] += dot_nn(hidden_ref[0], grads_ref[0])


def combine_back_kernel(
    pick_ref, slots_ref, extra_ref, gate_ref, back_ref, side_ref, *rest
):
    first_ref, second_ref, logits_ref, left_ref = rest[-4:]
    piece, part = pl.program_id(0), pl.program_id(1)
    flat = pick_ref.shape[1]
    units = back_ref.shape[1]

    @pl.when(part == 0)
    def _():
        merged = dot_tn(extra_ref[...].reshape(flat, LANES), pick_ref[0])
        grad_gate = merged[:EXPERTS] + merged[EXPERTS:]
        sigmoid, total = gate_ref[0, 0], gate_ref[0, 1]
        mixed = jnp.sum(grad_gate * sigmoid, axis=0, keepdims=True)
        logits = (
            ROUTE_SCALE
            * (grad_gate / total - mixed / (total * total))
            * sigmoid
            * (1.0 - sigmoid)
        ).astype(BF16)
        logits_ref[0] = logits
        left_ref[:units] = back_ref[0]
        left_ref[units:] = logits

    value = (
        dot_tn(pick_ref[0], slots_ref[...].reshape(flat, slots_ref.shape[2]))
        + dot_tn(left_ref[...], side_ref[...])
    ).astype(BF16)

    @pl.when(piece == 0)
    def _():
        first_ref[...] = value

    @pl.when(piece == 1)
    def _():
        second_ref[...] = value


def combine_out_kernel(pick_ref, slots_ref, hidden_ref, shared_ref, first_ref, second_ref):
    value = (
        dot_tn(pick_ref[0], slots_ref[...].reshape(pick_ref.shape[1], slots_ref.shape[2]))
        + dot_tn(hidden_ref[0], shared_ref[...])
    ).astype(BF16)

    @pl.when(pl.program_id(0) == 0)
    def _():
        first_ref[...] = value

    @pl.when(pl.program_id(0) == 1)
    def _():
        second_ref[...] = value


def chain_call(kernel, name, grid, prefetch, operands, in_specs, held, out_specs, out_shape, scratch=()):
    chained = [a for a in held if a is not None]
    at = len(prefetch) + len(operands)
    return pl.pallas_call(
        kernel,
        grid_spec=pltpu.PrefetchScalarGridSpec(
            num_scalar_prefetch=len(prefetch),
            grid=grid,
            in_specs=in_specs + [ANYWHERE] * len(chained),
            out_specs=out_specs,
            scratch_shapes=list(scratch),
        ),
        out_shape=out_shape,
        input_output_aliases={at + i: i for i in range(len(chained))},
        compiler_params=params(*["arbitrary"] * len(grid)),
        name=name,
    )(*prefetch, *operands, *chained)


def dispatch_grads(pair, sequences, local, base, routes, grads, shared_out, held):
    count, width = grads[0].shape
    units = shared_out.shape[0]
    operands = [*routes, *grads, shared_out]
    return chain_call(
        functools.partial(dispatch_grads_kernel, local),
        "dispatch_grads",
        (2,),
        [base],
        operands,
        [whole(a.shape) for a in operands],
        held,
        [
            pl.BlockSpec((local, SLOTS, width), lambda i, *_: (0, 2 * pair + i, 0)),
            pl.BlockSpec((1, units, count), lambda i, *_: (2 * pair + i, 0, 0)),
        ],
        [
            jax.ShapeDtypeStruct((local, sequences * SLOTS, width), BF16),
            jax.ShapeDtypeStruct((sequences, units, count), F32),
        ],
    )


def dispatch_rows(pair, sequences, local, base, routes, rows, side, raws, held):
    count, width = rows[0].shape
    units = raws.shape[1]
    operands = [*routes, *rows, side]
    shapes = [
        ((local * SLOTS, count), BF16),
        ((2, EXPERTS, count), F32),
        ((units, count), BF16),
        ((2 * units, count), BF16),
    ]

    def at(shape):
        return pl.BlockSpec((1,) + shape, lambda i, *_: (2 * pair + i,) + (0,) * len(shape))

    return chain_call(
        functools.partial(dispatch_rows_kernel, local, units),
        "dispatch_rows",
        (2,),
        [base],
        operands + [raws],
        [whole(a.shape) for a in operands] + [at((units, count))],
        held,
        [
            pl.BlockSpec((local, SLOTS, width), lambda i, *_: (0, 2 * pair + i, 0)),
            pl.BlockSpec((local, SLOTS, LANES), lambda i, *_: (0, 2 * pair + i, 0)),
        ]
        + [at(shape) for shape, _ in shapes],
        [
            jax.ShapeDtypeStruct((local, sequences * SLOTS, width), BF16),
            jax.ShapeDtypeStruct((local, sequences * SLOTS, LANES), BF16),
        ]
        + [jax.ShapeDtypeStruct((sequences,) + shape, dtype) for shape, dtype in shapes],
    )


def tile(*shape):
    return pl.BlockSpec((1,) + shape, lambda j, b: (j, b) + (0,) * (len(shape) - 1))


def lane_tile(*shape):
    return pl.BlockSpec((1,) + shape, lambda j, b: (j, 0, b))


def one(*shape):
    return pl.BlockSpec((1,) + shape, lambda j, b: (j, 0, 0))


def expert_raw(grads, expert_out):
    local, slots, width = grads.shape
    units = expert_out.shape[1]
    block = min(slots, SLOT_BLOCK)
    return pl.pallas_call(
        expert_raw_kernel,
        grid=(local, slots // block),
        in_specs=[tile(block, width), one(units, width)],
        out_specs=lane_tile(units, block),
        out_shape=jax.ShapeDtypeStruct((local, units, slots), F32),
        compiler_params=params("arbitrary", "arbitrary"),
        name="expert_raw",
    )(grads, expert_out)


def expert_rows(rows, infos, expert_in, raw):
    local, slots, width = rows.shape
    units = raw.shape[1]
    block = min(slots, SLOT_BLOCK)
    return pl.pallas_call(
        functools.partial(expert_kernel, units),
        grid=(local, slots // block),
        in_specs=[
            tile(block, width),
            tile(block, LANES),
            one(2 * units, width),
            lane_tile(units, block),
        ],
        out_specs=[
            tile(block, width),
            tile(block, LANES),
            lane_tile(units, block),
            lane_tile(2 * units, block),
        ],
        out_shape=[
            jax.ShapeDtypeStruct((local, slots, width), BF16),
            jax.ShapeDtypeStruct((local, slots, LANES), BF16),
            jax.ShapeDtypeStruct((local, units, slots), BF16),
            jax.ShapeDtypeStruct((local, 2 * units, slots), BF16),
        ],
        compiler_params=params("arbitrary", "arbitrary"),
        name="expert_rows",
    )(rows, infos, expert_in, raw)


def expert_out_rows(hidden, expert_out):
    local, units, slots = hidden.shape
    width = expert_out.shape[2]
    block = min(slots, SLOT_BLOCK)
    return pl.pallas_call(
        expert_out_kernel,
        grid=(local, slots // block),
        in_specs=[lane_tile(units, block), one(units, width)],
        out_specs=tile(block, width),
        out_shape=jax.ShapeDtypeStruct((local, slots, width), BF16),
        compiler_params=params("arbitrary", "arbitrary"),
        name="expert_out_rows",
    )(hidden, expert_out)


def weight_grads(start, stop, rows, grads, hidden, back, held):
    local, slots, width = rows.shape
    units = hidden.shape[1]
    block = min(slots, SLOT_BLOCK)

    def moved(spec):
        return pl.BlockSpec(
            spec.block_shape, lambda j, b: (lambda at: (at[0] + start,) + at[1:])(spec.index_map(j, b))
        )

    return chain_call(
        weight_grad_kernel,
        "weight_grads",
        (stop - start, slots // block),
        [],
        [rows, grads, hidden, back],
        [
            moved(spec)
            for spec in (
                tile(block, width),
                tile(block, width),
                lane_tile(units, block),
                lane_tile(2 * units, block),
            )
        ],
        held,
        [moved(one(2 * units, width)), moved(one(units, width)), whole((8, LANES))],
        [
            jax.ShapeDtypeStruct((local, 2 * units, width), F32),
            jax.ShapeDtypeStruct((local, units, width), F32),
            jax.ShapeDtypeStruct((8, LANES), F32),
        ],
    )


def piece_specs(width, part):
    return [
        pl.BlockSpec((width[0], part), lambda i, h: (0, jnp.where(i == 0, h, width[1] - 1))),
        pl.BlockSpec((width[0], part), lambda i, h: (0, jnp.where(i == 0, 0, h))),
    ]


def combine_back(pair, picks, slots, extra, gates, backs, side, held):
    sequences, flat, count = picks.shape
    local, _, width = slots.shape
    part = width // PARTS

    def at(array):
        shape = array.shape[1:]
        return pl.BlockSpec((1,) + shape, lambda i, h: (2 * pair + i,) + (0,) * len(shape))

    def strip(size):
        return pl.BlockSpec((local, SLOTS, size), lambda i, h: (0, 2 * pair + i, 0))

    outs = chain_call(
        lambda *refs: combine_back_kernel(*refs[:6], *refs[-3:-1], refs[-4], refs[-1]),
        "combine_back",
        (2, PARTS),
        [],
        [picks, slots, extra, gates, backs, side],
        [
            at(picks),
            pl.BlockSpec((local, SLOTS, part), lambda i, h: (0, 2 * pair + i, h)),
            strip(LANES),
            at(gates),
            at(backs),
            pl.BlockSpec((side.shape[0], part), lambda i, h: (0, h)),
        ],
        held,
        [pl.BlockSpec((1, EXPERTS, count), lambda i, h: (2 * pair + i, 0, 0))]
        + piece_specs((count, PARTS), part),
        [jax.ShapeDtypeStruct((sequences, EXPERTS, count), BF16)]
        + [jax.ShapeDtypeStruct((count, width), BF16)] * 2,
        [pltpu.VMEM((side.shape[0], count), BF16)],
    )
    return outs[1:], outs[:1]


def combine_out(pair, picks, slots, hiddens, shared_out):
    _, flat, count = picks.shape
    local, _, width = slots.shape
    part = width // PARTS
    units = hiddens.shape[1]
    return pl.pallas_call(
        combine_out_kernel,
        grid=(2, PARTS),
        in_specs=[
            pl.BlockSpec((1, flat, count), lambda i, h: (2 * pair + i, 0, 0)),
            pl.BlockSpec((local, SLOTS, part), lambda i, h: (0, 2 * pair + i, h)),
            pl.BlockSpec((1, units, count), lambda i, h: (2 * pair + i, 0, 0)),
            pl.BlockSpec((units, part), lambda i, h: (0, h)),
        ],
        out_specs=piece_specs((count, PARTS), part),
        out_shape=[jax.ShapeDtypeStruct((count, width), BF16)] * 2,
        compiler_params=params("arbitrary", "arbitrary"),
        name="combine_out",
    )(picks, slots, hiddens, shared_out)


def side_grads_kernel(sequences, block_ref, *refs):
    rows, grads, rest = refs[:sequences], refs[sequences : 2 * sequences], refs[2 * sequences :]
    logits_ref, hidden_ref, back_ref, first_ref, *parts, router_ref, left_ref, in_ref, out_ref = rest
    units = hidden_ref.shape[1]
    for s in range(sequences):
        left_ref[: 2 * units] = back_ref[s]
        left_ref[2 * units :] = logits_ref[s]
        value = dot_nn(left_ref[...], rows[s][...])
        other = dot_nn(hidden_ref[s], grads[s][...])
        if s == 0:
            in_ref[...] = value
            out_ref[...] = other
        else:
            in_ref[...] += value
            out_ref[...] += other
    shards, columns = len(parts), parts[0].shape[1]
    for k in range(shards):
        at = pl.ds(pl.multiple_of(block_ref[k] * columns, columns), columns)
        parts[k][: 2 * units] = in_ref[: 2 * units, at].astype(BF16)
        parts[k][2 * units :] = out_ref[:, at].astype(BF16)
    local = EXPERTS // shards
    for k in range(shards):
        start = first_ref[0] + k * local
        start = jnp.where(start >= EXPERTS, start - EXPERTS, start)
        router_ref[pl.ds(pl.multiple_of(start, local), local)] = in_ref[
            2 * units + k * local : 2 * units + (k + 1) * local
        ]


def side_grads(blocks, base, rows, grads, logits, hiddens, backs):
    sequences = len(rows)
    count, width = rows[0].shape
    units = hiddens.shape[1]
    shards = blocks.shape[0]
    operands = [*rows, *grads, logits, hiddens, backs]
    return pl.pallas_call(
        functools.partial(side_grads_kernel, sequences),
        grid_spec=pltpu.PrefetchScalarGridSpec(
            num_scalar_prefetch=1,
            grid=(1,),
            in_specs=[whole(a.shape) for a in operands]
            + [pl.BlockSpec(memory_space=pltpu.SMEM)],
            out_specs=[whole((3 * units, width // shards))] * shards + [whole((EXPERTS, width))],
            scratch_shapes=[
                pltpu.VMEM((2 * units + EXPERTS, count), BF16),
                pltpu.VMEM((2 * units + EXPERTS, width), F32),
                pltpu.VMEM((units, width), F32),
            ],
        ),
        out_shape=[jax.ShapeDtypeStruct((3 * units, width // shards), BF16)] * shards
        + [jax.ShapeDtypeStruct((EXPERTS, width), F32)],
        compiler_params=params("arbitrary"),
        name="side_grads",
    )(blocks, *operands, base)


def join_columns_kernel(used, block_ref, *refs):
    shards = (len(refs) - 3) // 2
    pieces, router_ref, side_ref, out_ref, routes = (
        refs[:shards], refs[shards], refs[shards + 1], refs[shards + 2], refs[shards + 3 :]
    )
    units = out_ref.shape[0]
    columns = pieces[0].shape[1]
    for k, piece in enumerate(pieces):
        at = pl.ds(pl.multiple_of(block_ref[k] * columns, columns), columns)
        side_ref[: 2 * units, at] = piece[: 2 * units]
        out_ref[:, at] = piece[2 * units :]
        routes[k][...] = piece[:units].astype(F32)[used:].astype(jnp.int32)
    side_ref[used:units] = jnp.zeros((units - used, side_ref.shape[1]), BF16)
    side_ref[2 * units :] = router_ref[...]


def join_rows_kernel(units, block_ref, *refs):
    parts, in_ref, out_ref = refs[:-2], refs[-2], refs[-1]
    padded = parts[0].shape[0] // 3
    for k, part in enumerate(parts):
        at = pl.ds(pl.multiple_of(block_ref[k] * units, 8), units)
        value = part[...].astype(F32)
        in_ref[0, at] = value[:units]
        in_ref[1, at] = value[padded : padded + units]
        out_ref[at] = value[2 * padded : 2 * padded + units]


def sum_split_kernel(depth_ref, own_ref, x_ref, y_ref, *outs):
    size = outs[0].shape[0]
    for k, out in enumerate(outs):
        at = pl.ds(pl.multiple_of(depth_ref[k] * size, size), size)
        out[...] = (
            own_ref[at].astype(F32) + x_ref[at].astype(F32) + y_ref[at].astype(F32)
        ).astype(BF16)


def join_depth_kernel(depth_ref, *refs):
    pieces, out_ref = refs[:-1], refs[-1]
    size = pieces[0].shape[0]
    for k, piece in enumerate(pieces):
        out_ref[pl.ds(pl.multiple_of(depth_ref[k] * size, size), size)] = piece[...]


def replicated_kernel(used, block_ref, *refs):
    chunks, latent_ref, router_ref, gains_ref = refs[:-3], refs[-3], refs[-2], refs[-1]
    columns = chunks[0].shape[1]
    for k, chunk in enumerate(chunks):
        at = pl.ds(pl.multiple_of(block_ref[k] * columns, columns), columns)
        latent_ref[:, at] = chunk[:used].astype(F32)
        router_ref[:, at] = chunk[used : used + EXPERTS].astype(F32)
        gains_ref[:, at] = chunk[used + EXPERTS : used + EXPERTS + 16].astype(F32)


def rope_turn(first, second, cosine, sine):
    return first * cosine - second * sine, first * sine + second * cosine


def unit_rows(pieces):
    values = jnp.concatenate([piece[...] for piece in pieces], axis=0).astype(F32)
    inverse = lax.rsqrt(jnp.mean(values * values, axis=-1, keepdims=True) + EPSILON)
    return values * inverse


def latent_kernel(depth, *refs):
    pieces = refs[:depth]
    gain_ref, weight_ref, kv_gain_ref, cosine_ref, sine_ref = refs[depth : depth + 5]
    normed_ref, comp_ref, low_ref, key_ref, wide_ref = refs[depth + 5 :]
    half = ROPE // 2
    wide_ref[:KVR] = weight_ref[:KVR]
    for i in range(2):
        piece = weight_ref[KVR + i * half : KVR + (i + 1) * half]
        for j in range(LANES // half):
            start = KVR + i * LANES + j * half
            wide_ref[start : start + half] = piece
    normed = (unit_rows(pieces) * gain_ref[...]).astype(BF16)
    normed_ref[...] = normed
    latent = dot_nt(normed, wide_ref[...])
    compressed = latent[:, :KVR]
    comp_ref[...] = compressed
    inverse = lax.rsqrt(jnp.mean(compressed * compressed, axis=-1, keepdims=True) + EPSILON)
    low_ref[...] = (compressed * inverse * kv_gain_ref[...]).astype(BF16)
    first, second = rope_turn(
        latent[:, KVR : KVR + LANES], latent[:, KVR + LANES :], cosine_ref[...], sine_ref[...]
    )
    key_ref[...] = jnp.concatenate([first, second], axis=1).astype(BF16)


def head_mask(head):
    lane = lax.broadcasted_iota(jnp.int32, (1, LANES), 1)
    return ((lane // (ROPE // 2)) == head).astype(F32)


def keyval_weight(block_ref, packs, whole_ref, queries):
    share = KVR // len(packs)
    count = packs[0].shape[0] // share
    columns = whole_ref.shape[1] // count
    for k, pack in enumerate(packs):
        start = pl.multiple_of(block_ref[k] * share, share)
        for i in range(count):
            whole_ref[pl.ds(start, share), i * columns : (i + 1) * columns] = pack[
                i * share : (i + 1) * share, queries : queries + columns
            ]


def attention_kernel(heads, block_ref, *refs):
    shards = len(refs) - 13
    packs = refs[:shards]
    normed_ref, low_ref, key_ref, bias_ref, cosine_ref, sine_ref = refs[shards : shards + 6]
    query_ref, keyval_ref, soft_ref, attended_ref, part_ref, total_ref, weight_ref = refs[
        shards + 6 :
    ]
    share = packs[0].shape[0]
    nope = heads * NOPE
    queries = heads * (NOPE + ROPE)
    keyval_columns = keyval_ref.shape[1] * (KVR // shards) // share
    keyval_weight(block_ref, packs, weight_ref, queries)
    for k, pack in enumerate(packs):
        start = pl.multiple_of(block_ref[k] * share, share)
        value = dot_nn(normed_ref[:, pl.ds(start, share)], pack[:, :queries])
        if k == 0:
            total_ref[...] = value
        else:
            total_ref[...] += value
    keyval_ref[...] = dot_nn(low_ref[...], weight_ref[...]).astype(BF16)
    first, second = rope_turn(
        total_ref[:, nope : nope + LANES], total_ref[:, nope + LANES :], cosine_ref[...], sine_ref[...]
    )
    query_ref[:, :nope] = total_ref[:, :nope].astype(BF16)
    query_ref[:, nope : nope + LANES] = first.astype(BF16)
    query_ref[:, nope + LANES :] = second.astype(BF16)
    for head in range(heads):
        mask = head_mask(head)
        at = head * (NOPE + VD)
        turned = jnp.concatenate([first * mask, second * mask], axis=1).astype(BF16)
        scores = dot_nt(
            query_ref[:, head * NOPE : (head + 1) * NOPE], keyval_ref[:, at : at + NOPE]
        ) + dot_nt(turned, key_ref[...])
        scores = scores * ((NOPE + ROPE) ** (-0.5)) + bias_ref[...]
        raised = jnp.exp(scores - jnp.max(scores, axis=-1, keepdims=True))
        soft = raised / jnp.sum(raised, axis=-1, keepdims=True)
        soft_ref[head] = soft
        attended_ref[:, head * VD : (head + 1) * VD] = dot_nn(
            soft.astype(BF16), keyval_ref[:, at + NOPE : at + NOPE + VD]
        ).astype(BF16)
    output = queries + keyval_columns
    columns = part_ref.shape[1] // shards
    for k, pack in enumerate(packs):
        start = pl.multiple_of(block_ref[k] * columns, columns)
        value = dot_nn(attended_ref[:, :share], pack[:, output : output + columns])
        for i in range(1, heads * VD // share):
            value += dot_nn(
                attended_ref[:, i * share : (i + 1) * share],
                pack[:, output + i * columns : output + (i + 1) * columns],
            )
        part_ref[:, pl.ds(start, columns)] = value.astype(BF16)


def attention_back_kernel(heads, depth, block_ref, *refs):
    shards = (len(refs) - 2 * depth - 22) // 2
    packs, refs = refs[:shards], refs[shards:]
    tokens, refs = refs[:depth], refs[depth:]
    grads, refs = refs[:depth], refs[depth:]
    (
        query_ref, keyval_ref, key_ref, soft_ref, attended_ref, comp_ref, low_ref, normed_ref,
        latent_ref, kv_gain_ref, cosine_ref, sine_ref, router_ref, ffn_gain_ref,
        grad_query_ref, grad_keyval_ref, grad_normed_ref, *chunk_refs,
        gains_ref, grad_attended_ref, weight_ref, back_ref, stage_ref,
    ) = refs
    share = packs[0].shape[0]
    nope = heads * NOPE
    queries = heads * (NOPE + ROPE)
    keyval_columns = keyval_ref.shape[1] * (KVR // shards) // share
    output = queries + keyval_columns
    columns = normed_ref.shape[1] // shards
    scale = (NOPE + ROPE) ** (-0.5)
    stage_ref[...] = jnp.concatenate([piece[...] for piece in grads], axis=0)
    blocks = heads * VD // share
    for i in range(blocks):
        value = None
        for k, pack in enumerate(packs):
            start = pl.multiple_of(block_ref[k] * columns, columns)
            part = dot_nt(
                stage_ref[:, pl.ds(start, columns)],
                pack[:, output + i * columns : output + (i + 1) * columns],
            )
            value = part if value is None else value + part
        grad_attended_ref[:, i * share : (i + 1) * share] = value.astype(BF16)
    cosine, sine = cosine_ref[...], sine_ref[...]
    turn_first, turn_second = None, None
    key_turn = None
    for head in range(heads):
        mask = head_mask(head)
        at = head * (NOPE + VD)
        soft = soft_ref[head]
        attended = attended_ref[:, head * VD : (head + 1) * VD]
        grad = grad_attended_ref[:, head * VD : (head + 1) * VD]
        delta = jnp.sum(grad.astype(F32) * attended.astype(F32), axis=-1, keepdims=True)
        grad_soft = dot_nt(grad, keyval_ref[:, at + NOPE : at + NOPE + VD])
        scores = (soft * (grad_soft - delta) * scale).astype(BF16)
        query = query_ref[:, head * NOPE : (head + 1) * NOPE]
        grad_query_ref[:, head * NOPE : (head + 1) * NOPE] = dot_nn(
            scores, keyval_ref[:, at : at + NOPE]
        ).astype(BF16)
        turned = dot_nn(scores, key_ref[...])
        first, second = turned[:, :LANES] * mask, turned[:, LANES:] * mask
        turn_first = first if turn_first is None else turn_first + first
        turn_second = second if turn_second is None else turn_second + second
        wide = jnp.concatenate([mask, mask], axis=1)
        masked = (query_ref[:, nope:].astype(F32) * wide).astype(BF16)
        part = dot_tn(scores, masked)
        key_turn = part if key_turn is None else key_turn + part
        grad_keyval_ref[:, at : at + NOPE] = dot_tn(scores, query).astype(BF16)
        grad_keyval_ref[:, at + NOPE : at + NOPE + VD] = dot_tn(soft.astype(BF16), grad).astype(BF16)
    first, second = rope_turn(turn_first, turn_second, cosine, -sine)
    grad_query_ref[:, nope : nope + LANES] = first.astype(BF16)
    grad_query_ref[:, nope + LANES :] = second.astype(BF16)
    keyval_weight(block_ref, packs, weight_ref, queries)
    grad_comp = dot_nt(grad_keyval_ref[...], weight_ref[...])
    compressed = comp_ref[...]
    inverse = lax.rsqrt(jnp.mean(compressed * compressed, axis=-1, keepdims=True) + EPSILON)
    weighted = grad_comp * kv_gain_ref[...]
    grad_compressed = inverse * weighted - compressed * (inverse * inverse * inverse) * jnp.mean(
        compressed * weighted, axis=-1, keepdims=True
    )
    gains_ref[...] = jnp.zeros_like(gains_ref)
    gains_ref[2:3, :KVR] = jnp.sum(grad_comp * compressed * inverse, axis=0, keepdims=True)
    back_ref[:, :KVR] = grad_compressed.astype(BF16)
    first, second = rope_turn(key_turn[:, :LANES], key_turn[:, LANES:], cosine, -sine)
    back_ref[:, KVR : KVR + LANES] = first.astype(BF16)
    back_ref[:, KVR + LANES :] = second.astype(BF16)
    unit = unit_rows(tokens)
    half = ROPE // 2
    for k, pack in enumerate(packs):
        start = pl.multiple_of(block_ref[k] * columns, columns)
        value = dot_nt(grad_query_ref[...], pack[:, :queries])
        value += dot_nn(back_ref[...], latent_ref[:, pl.ds(start, columns)])
        grad_normed_ref[:, pl.ds(start, columns)] = value.astype(BF16)
        weight = dot_tn(back_ref[...], normed_ref[:, pl.ds(start, columns)])
        turns = [
            sum(weight[KVR + i * LANES + j * half : KVR + i * LANES + (j + 1) * half] for j in range(heads))
            for i in range(2)
        ]
        chunk_refs[k][: KVR + ROPE] = jnp.concatenate([weight[:KVR]] + turns, axis=0).astype(BF16)
    gains_ref[0:1, :] = jnp.sum(grad_normed_ref[...].astype(F32) * unit, axis=0, keepdims=True)
    gains_ref[1:2, :] = ffn_gain_ref[...]
    used = KVR + ROPE
    for k in range(shards):
        at = pl.ds(pl.multiple_of(block_ref[k] * columns, columns), columns)
        chunk_refs[k][used : used + EXPERTS] = router_ref[:, at].astype(BF16)
        rows = [gains_ref[:2, at]]
        rows += [gains_ref[2:3, i * columns : (i + 1) * columns] for i in range(KVR // columns)]
        filled = 2 + KVR // columns
        rows.append(jnp.zeros((CHUNK_ROWS - used - EXPERTS - filled, columns), F32))
        chunk_refs[k][used + EXPERTS :] = jnp.concatenate(rows, axis=0).astype(BF16)


def attention_weights_kernel(heads, depth, block_ref, *refs):
    grads, refs = refs[:depth], refs[depth:]
    normed_ref, low_ref, attended_ref, query_ref, keyval_ref, *packs, stage_ref, whole_ref = refs
    shards, share = len(packs), packs[0].shape[0]
    queries = heads * (NOPE + ROPE)
    columns = normed_ref.shape[1] // shards
    part = KVR // shards
    count = share // part
    keyval_columns = keyval_ref.shape[1] // count
    output = queries + keyval_columns
    stage_ref[...] = jnp.concatenate([piece[...] for piece in grads], axis=0)
    whole_ref[...] = dot_tn(low_ref[...], keyval_ref[...]).astype(BF16)
    for k in range(shards):
        start = pl.multiple_of(block_ref[k] * columns, columns)
        packs[k][:, :queries] = dot_tn(
            normed_ref[:, pl.ds(start, columns)], query_ref[...]
        ).astype(BF16)
        rows = pl.ds(pl.multiple_of(block_ref[k] * part, part), part)
        for i in range(count):
            packs[k][i * part : (i + 1) * part, queries:output] = whole_ref[
                rows, i * keyval_columns : (i + 1) * keyval_columns
            ]
        value = dot_tn(attended_ref[...], stage_ref[:, pl.ds(start, columns)]).astype(BF16)
        for i in range(heads * VD // share):
            packs[k][:, output + i * columns : output + (i + 1) * columns] = value[
                i * share : (i + 1) * share
            ]


def vmem_call(kernel, name, blocks, operands, out_shape, scratch):
    if blocks is None:
        return pl.pallas_call(
            kernel,
            out_shape=out_shape,
            scratch_shapes=scratch,
            compiler_params=params(),
            name=name,
        )(*operands)
    return pl.pallas_call(
        kernel,
        grid_spec=pltpu.PrefetchScalarGridSpec(
            num_scalar_prefetch=1,
            grid=(1,),
            in_specs=[whole(a.shape) for a in operands],
            out_specs=[whole(a.shape) for a in out_shape],
            scratch_shapes=scratch,
        ),
        out_shape=out_shape,
        compiler_params=params("arbitrary"),
        name=name,
    )(blocks, *operands)


def latent_rows(pieces, gain, weight, kv_gain, cosine, sine):
    count = sum(piece.shape[0] for piece in pieces)
    width = pieces[0].shape[1]
    return vmem_call(
        functools.partial(latent_kernel, len(pieces)),
        "latent_rows",
        None,
        [*pieces, gain[None], weight, kv_gain[None], cosine, sine],
        [
            jax.ShapeDtypeStruct((count, width), BF16),
            jax.ShapeDtypeStruct((count, KVR), F32),
            jax.ShapeDtypeStruct((count, KVR), BF16),
            jax.ShapeDtypeStruct((count, 2 * LANES), BF16),
            jax.ShapeDtypeStruct((KVR + 2 * LANES, width), BF16),
        ],
        [],
    )


def attention_forward(heads, blocks, packs, normed, low, key, bias, cosine, sine):
    count, width = normed.shape
    queries = heads * (NOPE + ROPE)
    keyval = heads * (NOPE + VD)
    return vmem_call(
        functools.partial(attention_kernel, heads),
        "attention_forward",
        blocks,
        [*packs, normed, low, key, bias, cosine, sine],
        [
            jax.ShapeDtypeStruct((count, queries), BF16),
            jax.ShapeDtypeStruct((count, keyval), BF16),
            jax.ShapeDtypeStruct((heads, count, count), F32),
            jax.ShapeDtypeStruct((count, heads * VD), BF16),
            jax.ShapeDtypeStruct((count, width), BF16),
        ],
        [pltpu.VMEM((count, queries), F32), pltpu.VMEM((KVR, keyval), BF16)],
    )


def attention_backward(
    heads, blocks, packs, tokens, grads, saved, latent, kv_gain, cosine, sine, router, ffn_gain
):
    query, keyval, key, soft, attended, compressed, low, normed = saved
    count, width = normed.shape
    shards = len(packs)
    return vmem_call(
        functools.partial(attention_back_kernel, heads, len(tokens)),
        "attention_backward",
        blocks,
        [
            *packs, *tokens, *grads, query, keyval, key, soft, attended, compressed, low, normed,
            latent, kv_gain[None], cosine, sine, router, ffn_gain[None],
        ],
        [
            jax.ShapeDtypeStruct(query.shape, BF16),
            jax.ShapeDtypeStruct(keyval.shape, BF16),
            jax.ShapeDtypeStruct((count, width), BF16),
        ]
        + [jax.ShapeDtypeStruct((CHUNK_ROWS, width // shards), BF16)] * shards,
        [
            pltpu.VMEM((8, width), F32),
            pltpu.VMEM((count, heads * VD), BF16),
            pltpu.VMEM((KVR, keyval.shape[1]), BF16),
            pltpu.VMEM((count, latent.shape[0]), BF16),
            pltpu.VMEM((count, width), BF16),
        ],
    )


def attention_weights(heads, blocks, shape, grads, normed, low, attended, grad_query, grad_keyval):
    count, width = normed.shape
    shards = blocks.shape[0]
    return vmem_call(
        functools.partial(attention_weights_kernel, heads, len(grads)),
        "attention_weights",
        blocks,
        [*grads, normed, low, attended, grad_query, grad_keyval],
        [jax.ShapeDtypeStruct(shape, BF16)] * shards,
        [pltpu.VMEM((count, width), BF16), pltpu.VMEM((KVR, grad_keyval.shape[1]), BF16)],
    )


def query_order(heads):
    size, half = NOPE + ROPE, ROPE // 2
    pieces = []
    for start, stop in ((0, NOPE), (NOPE, NOPE + half), (NOPE + half, size)):
        pieces += [(head * size + start, head * size + stop) for head in range(heads)]
    return pieces


def pack_weights(query, keyval, output, heads):
    share, columns = query.shape[0], output.shape[1]
    part = keyval.shape[0]
    count = share // part
    wide = keyval.shape[1] // count
    return jnp.concatenate(
        [query[:, start:stop] for start, stop in query_order(heads)]
        + [
            jnp.concatenate([keyval[:, i * wide : (i + 1) * wide] for i in range(count)], axis=0)
        ]
        + [output[i * share : (i + 1) * share] for i in range(output.shape[0] // share)],
        axis=1,
    )


def unpack_weights(pack, keyval_shape, output_shape, heads):
    size, half = NOPE + ROPE, ROPE // 2
    queries = heads * size
    share = pack.shape[0]
    part = keyval_shape[0]
    count = share // part
    wide = keyval_shape[1] // count
    nope = heads * NOPE
    query = []
    for head in range(heads):
        query += [
            pack[:, head * NOPE : (head + 1) * NOPE],
            pack[:, nope + head * half : nope + (head + 1) * half],
            pack[:, nope + (heads + head) * half : nope + (heads + head + 1) * half],
        ]
    keyval = jnp.concatenate(
        [pack[i * part : (i + 1) * part, queries : queries + wide] for i in range(count)], axis=1
    )
    at, columns = queries + wide, output_shape[1]
    output = jnp.concatenate(
        [
            pack[:, at + i * columns : at + (i + 1) * columns]
            for i in range(output_shape[0] // share)
        ],
        axis=0,
    )
    return jnp.concatenate(query, axis=1), keyval, output


def expert_layer(base, rows, grads, routes, router, expert_in, expert_out, shared):
    local, units, width = expert_out.shape
    sequences = len(rows)
    pairs = range(sequences // 2)
    shared_units = shared.shape[0] // 3
    side = jnp.concatenate([shared[: 2 * shared_units], router])
    shared_out = shared[2 * shared_units :]
    held = [None, None]
    for m in pairs:
        at = slice(2 * m, 2 * m + 2)
        held = dispatch_grads(
            m, sequences, local, base, routes[at], grads[at], shared_out, held
        )
    slot_grads, shared_raw = held
    raw = expert_raw(slot_grads, expert_out)
    held = [None] * 6
    for m in pairs:
        at = slice(2 * m, 2 * m + 2)
        held = dispatch_rows(
            m, sequences, local, base, routes[at], rows[at], side, shared_raw, held
        )
    slot_rows, infos, picks, gates, shared_hidden, shared_back = held
    back_rows, extra, hidden, back = expert_rows(
        slot_rows, infos, expert_in.reshape(local, 2 * units, width), raw
    )
    back_tokens, logits = [], [None]
    for m in pairs:
        tokens, logits = combine_back(
            m, picks, back_rows, extra, gates, shared_back, side, logits
        )
        back_tokens += tokens
    out_rows = expert_out_rows(hidden, expert_out)
    out_tokens = []
    for m in pairs:
        out_tokens += combine_out(m, picks, out_rows, shared_hidden, shared_out)
    grad_in, grad_out, _ = weight_grads(
        0, local, slot_rows, slot_grads, hidden, back, [None, None]
    )
    all_rows = jnp.stack(rows)
    grad_router = contract("set,std->ed", logits[0], all_rows)
    grad_shared = jnp.concatenate(
        [
            contract("sft,std->fd", shared_back, all_rows),
            contract("sft,std->fd", shared_hidden, jnp.stack(grads)),
        ]
    )
    return (
        out_tokens,
        back_tokens,
        grad_in.reshape(local, 2, units, width),
        grad_out,
        grad_router,
        grad_shared,
    )


def general_device(
    tokens_in,
    out_grad,
    routes,
    attn_gain,
    kv_gain,
    ffn_gain,
    w_query,
    w_latent,
    w_keyval,
    w_output,
    w_router,
    w_shared_in,
    w_shared_out,
    w_expert_in,
    w_expert_out,
):
    grid = Grid()
    depth = grid.depth
    own_depth = lax.axis_index("tensor")
    own_rows, width = tokens_in.shape
    row_count = own_rows * depth
    local_experts = w_expert_in.shape[0]
    base = lax.axis_index("expert") * local_experts
    stream = jnp.concatenate(grid.gather_depth(tokens_in)).astype(F32)
    full_query = grid.absolute(grid.gather(w_query), 0)
    full_keyval = grid.absolute(grid.gather(w_keyval), 0)
    full_output = grid.absolute(grid.gather(w_output), 1)
    all_grads = grid.gather(jnp.concatenate(grid.gather_depth(out_grad)))
    routes_rel = jnp.concatenate(grid.relative_depth(routes.T, 1), axis=1)
    routes_all = [routes_rel] + [grid.fetch(routes_rel, offset) for offset in grid.offsets[1:]]
    units = w_shared_out.shape[0] // grid.experts
    padding = ((0, -units % 32), (0, 0))
    padded_units = units + padding[0][1]
    shared_parts = [
        jnp.concatenate([jnp.pad(part, padding) for part in parts])
        for parts in zip(
            grid.relative(w_shared_in[0].T, 0),
            grid.relative(w_shared_in[1].T, 0),
            grid.relative(w_shared_out, 0),
        )
    ]
    shared = grid.absolute(grid.exchange(shared_parts), 1)
    position = (
        (own_depth + jnp.arange(row_count) // own_rows) % depth * own_rows
        + jnp.arange(row_count) % own_rows
    )
    local_heads = full_query.shape[1] // (NOPE + ROPE)
    cosine, sine_table = rope_tables(position)
    normed_one, inverse_one = rms_forward(stream, attn_gain)
    normed_one = normed_one.astype(BF16)
    queries = mix_dot(normed_one, full_query).reshape(row_count, local_heads, NOPE + ROPE)
    queries = jnp.concatenate(
        [
            queries[..., :NOPE],
            rotate(queries[..., NOPE:], cosine[:, None, :], sine_table[:, None, :]),
        ],
        axis=-1,
    ).astype(BF16)
    latent = mix_dot(normed_one, w_latent)
    compressed = latent[:, :KVR]
    comp_normed, comp_inverse = rms_forward(compressed, kv_gain)
    comp_normed = comp_normed.astype(BF16)
    key_rope = rotate(latent[:, KVR:], cosine, sine_table).astype(BF16)
    keyval = mix_dot(comp_normed, full_keyval).reshape(row_count, local_heads, NOPE + VD).astype(BF16)
    key_nope = keyval[..., :NOPE]
    values = keyval[..., NOPE:]
    scores = attention_scores(queries, key_nope, key_rope, position)
    top_score = jnp.max(scores, axis=-1, keepdims=True)
    raised = jnp.exp(scores - top_score)
    soft = raised / jnp.sum(raised, axis=-1, keepdims=True)
    soft_low = soft.astype(BF16)
    attended = contract("hqk,khv->qhv", soft_low, values).astype(BF16)
    attended_flat = attended.reshape(row_count, local_heads * VD)
    attention_part = mix_dot(attended_flat, full_output).astype(BF16)
    stream_own = tokens_in.astype(F32)
    residual = stream_own + grid.reduce_depth(split_rows(attention_part, depth))
    normed_two, inverse_two = rms_forward(residual, ffn_gain)
    normed_two = normed_two.astype(BF16)
    all_rows = grid.gather(jnp.concatenate(grid.gather_depth(normed_two)))
    router_rel = jnp.roll(w_router.T, -base, axis=0)
    (
        out_tokens,
        back_tokens,
        grad_expert_in,
        grad_expert_out,
        grad_router_rel,
        grad_shared,
    ) = expert_layer(
        base.astype(jnp.int32)[None],
        all_rows,
        all_grads,
        routes_all,
        router_rel,
        jnp.swapaxes(w_expert_in, 2, 3),
        w_expert_out,
        shared,
    )
    grad_normed = grid.reduce_depth(
        split_rows(grid.reduce(back_tokens).astype(BF16), depth)
    )
    ffn_total = grid.reduce_depth(split_rows(grid.reduce(out_tokens).astype(BF16), depth))
    block_out = (residual + ffn_total).astype(BF16)
    grad_float = out_grad.astype(F32)
    grad_res_part, grad_ffn_gain = rms_backward(residual, inverse_two, ffn_gain, grad_normed)
    grad_residual = grad_float + grad_res_part
    grad_res_low = jnp.concatenate(grid.gather_depth(grad_residual.astype(BF16)))
    grad_output = contract("tv,td->vd", attended_flat, grad_res_low).astype(BF16)
    sum_output = grid.reduce(grid.relative(grad_output, 1))
    grad_attended = (
        contract("td,vd->tv", grad_res_low, full_output)
        .astype(BF16)
        .reshape(row_count, local_heads, VD)
    )
    softmax_scale = (NOPE + ROPE) ** (-0.5)
    grad_soft = contract("qhv,khv->hqk", grad_attended, values)
    row_delta = jnp.sum(grad_attended.astype(F32) * attended.astype(F32), axis=-1).T
    grad_scores = (soft * (grad_soft - row_delta[..., None]) * softmax_scale).astype(BF16)
    grad_query_nope = contract("hqk,khd->qhd", grad_scores, key_nope)
    grad_query_rope = contract("hqk,kr->qhr", grad_scores, key_rope)
    grad_key_nope = contract("hqk,qhd->khd", grad_scores, queries[..., :NOPE])
    grad_key_rope = contract("hqk,qhr->kr", grad_scores, queries[..., NOPE:])
    grad_values = contract("hqk,qhv->khv", soft_low, grad_attended)
    grad_query_raw = (
        jnp.concatenate(
            [
                grad_query_nope,
                rotate(grad_query_rope, cosine[:, None, :], -sine_table[:, None, :]),
            ],
            axis=-1,
        )
        .reshape(row_count, local_heads * (NOPE + ROPE))
        .astype(BF16)
    )
    grad_query_weight = contract("td,tq->dq", normed_one, grad_query_raw).astype(BF16)
    grad_keyval = (
        jnp.concatenate([grad_key_nope, grad_values], axis=-1)
        .reshape(row_count, local_heads * (NOPE + VD))
        .astype(BF16)
    )
    grad_keyval_weight = contract("tc,tk->ck", comp_normed, grad_keyval).astype(BF16)
    sum_query = grid.reduce(grid.relative(grad_query_weight, 0))
    sum_keyval = grid.reduce(grid.relative(grad_keyval_weight, 0))
    grad_comp_normed = contract("tk,ck->tc", grad_keyval, full_keyval)
    grad_compressed, grad_kv_gain = rms_backward(
        compressed, comp_inverse, kv_gain, grad_comp_normed
    )
    grad_latent_out = jnp.concatenate(
        [grad_compressed, rotate(grad_key_rope, cosine, -sine_table)], axis=-1
    ).astype(BF16)
    grad_latent = contract("tk,td->kd", grad_latent_out, normed_one)
    grad_normed_one = contract("tq,dq->td", grad_query_raw, full_query) + contract(
        "tk,dk->td", grad_latent_out, w_latent
    )
    grad_normed_one = grid.reduce_depth(split_rows(grad_normed_one.astype(BF16), depth))
    inverse_own = inverse_one[:own_rows]
    grad_x_part, grad_attn_gain = rms_backward(stream_own, inverse_own, attn_gain, grad_normed_one)
    grad_in = grad_residual + grad_x_part
    grad_shared_parts = [part.astype(BF16) for part in grid.relative(grad_shared, 1)]
    returned = grid.exchange(grad_shared_parts)
    sum_shared_in = jnp.stack(
        [
            grid.absolute([part[:units] for part in returned], 0).T,
            grid.absolute([part[padded_units : padded_units + units] for part in returned], 0).T,
        ]
    ).astype(F32)
    sum_shared_out = grid.absolute([part[2 * padded_units : 2 * padded_units + units] for part in returned], 0).astype(F32)
    gains = jnp.stack(
        [grad_attn_gain, grad_ffn_gain, jnp.pad(grad_kv_gain, (0, width - KVR))]
    )
    replicated = jnp.concatenate([grad_latent, jnp.roll(grad_router_rel, base, axis=0), gains])
    used = replicated.shape[0]
    padded = -(-used // (16 * grid.experts)) * 16 * grid.experts
    replicated = jnp.pad(replicated, ((0, padded - used), (0, 0))).astype(BF16)
    chunk = grid.reduce(grid.relative(replicated, 0)).astype(BF16)
    part = grid.reduce_depth(grid.relative_depth(chunk, 1)).astype(BF16)
    chunk = grid.absolute_depth(grid.gather_depth(part), 1)
    whole = grid.absolute(grid.gather(chunk), 0).astype(F32)
    sum_latent = whole[: KVR + ROPE].T
    sum_router = whole[KVR + ROPE : KVR + ROPE + EXPERTS].T
    sum_attn_gain = whole[KVR + ROPE + EXPERTS]
    sum_ffn_gain = whole[KVR + ROPE + EXPERTS + 1]
    sum_kv_gain = whole[KVR + ROPE + EXPERTS + 2, :KVR]
    return (
        block_out,
        grad_in,
        sum_attn_gain,
        sum_kv_gain,
        sum_ffn_gain,
        sum_query,
        sum_latent,
        sum_keyval,
        sum_output,
        sum_router,
        sum_shared_in,
        sum_shared_out,
        jnp.swapaxes(grad_expert_in, 2, 3),
        grad_expert_out,
    )


def after(array, *earlier):
    return lax.optimization_barrier((array, *earlier))[0]


def square_device(
    tokens_in,
    out_grad,
    routes,
    attn_gain,
    kv_gain,
    ffn_gain,
    w_query,
    w_latent,
    w_keyval,
    w_output,
    w_router,
    w_shared_in,
    w_shared_out,
    w_expert_in,
    w_expert_out,
):
    grid = Grid()
    depth = grid.depth
    sequences = grid.experts
    pairs = range(sequences // 2)
    own_rows, width = tokens_in.shape
    row_count = own_rows * depth
    local = w_expert_in.shape[0]
    hidden_units = w_expert_out.shape[1]
    heads = w_query.shape[1] // (NOPE + ROPE)
    own_depth = lax.axis_index("tensor")
    blocks = jnp.stack([grid.place_of(offset) for offset in grid.offsets]).astype(jnp.int32)
    depths = ((own_depth + jnp.arange(depth)) % depth).astype(jnp.int32)
    base = (lax.axis_index("expert") * local).astype(jnp.int32)[None]

    tokens = grid.ring_gather(tokens_in)
    packs = grid.gather(pack_weights(w_query, w_keyval, w_output, heads))
    group_grads = jnp.concatenate(grid.ring_gather(after(out_grad, packs[2], packs[4], *tokens)))
    position = (
        (own_depth + jnp.arange(row_count) // own_rows) % depth * own_rows
        + jnp.arange(row_count) % own_rows
    )
    cosine, sine = (jnp.tile(table, (1, heads)) for table in rope_tables(position))
    bias = jnp.where(position[None, :] <= position[:, None], 0.0, -1e30).astype(F32)
    normed, compressed, low, key, latent_t = latent_rows(
        tokens, attn_gain, w_latent.T, kv_gain, cosine, sine
    )

    units = w_shared_out.shape[0] // grid.experts
    padding = -units % 32
    padded_units = units + padding
    shared_in, shared_out = after(w_shared_in, packs[2]), after(w_shared_out, packs[2])
    routes_t = jnp.concatenate(grid.relative_depth(routes.T, 1), axis=1).astype(BF16)
    assert padding >= TOP and padding % 8 == 0 and units % 8 == 0
    fill = jnp.zeros((padding, w_shared_out.shape[1]), BF16)
    routes_fill = lax.dynamic_update_slice(fill, routes_t, (0, 0))
    shared_parts = [
        jnp.concatenate([first, routes_fill, second, fill, third, fill])
        for first, second, third in zip(
            grid.relative(shared_in[0].T, 0),
            grid.relative(shared_in[1].T, 0),
            grid.relative(shared_out, 0),
        )
    ]
    pieces = grid.exchange([after(part, packs[6]) for part in shared_parts])
    router = jnp.roll(after(w_router, packs[2]).T, -base[0], axis=0)
    side, shared_out, *routes_all = vmem_call(
        functools.partial(join_columns_kernel, units),
        "join_columns",
        blocks,
        [*pieces, router],
        [
            jax.ShapeDtypeStruct((2 * padded_units + EXPERTS, width), BF16),
            jax.ShapeDtypeStruct((padded_units, width), BF16),
        ]
        + [jax.ShapeDtypeStruct((padding, row_count), jnp.int32)] * sequences,
        [],
    )

    query, keyval, soft, attended, part = attention_forward(
        heads, blocks, packs, after(normed, group_grads), low, key, bias, cosine, sine
    )
    part = after(part, *pieces)

    middle = row_count // 2
    group_grads = after(group_grads, part)
    along_x = grid.fetch(group_grads, (0, 1, 0))
    along_y = grid.fetch(group_grads, (1, 0, 0))
    stream = tokens_in.astype(F32)
    residual = stream + grid.ring_reduce(split_rows(part, depth))
    normed_two, inverse_two = rms_forward(residual, ffn_gain)
    normed_two = normed_two.astype(BF16)
    near_rows = grid.ring_near(normed_two)
    first = grid.fetch(along_x[:middle], (1, 0, 0))
    second = grid.fetch(along_y[middle:], (0, 1, 0))
    all_grads = [group_grads, grid.fetch(group_grads, (0, 0, 1))]
    for held in (along_x, along_y):
        all_grads += [held, grid.fetch(held, (0, 0, 1))]
    near_rows = [after(piece, along_x, along_y) for piece in near_rows]
    far_rows = grid.ring_far(*near_rows)
    group_rows = jnp.concatenate([normed_two, near_rows[0], *far_rows, near_rows[1]])
    group_rows = after(group_rows, first, second)
    all_grads += [
        jnp.concatenate([first, second]),
        jnp.concatenate([grid.fetch(first, (0, 0, 1)), grid.fetch(second, (0, 0, 1))]),
    ]

    along_x = grid.fetch(group_rows, (0, 1, 0))
    along_y = grid.fetch(group_rows, (1, 0, 0))
    pair_rows = grid.fetch(group_rows, (0, 0, 1))
    held = [None, None]
    for m in pairs:
        held = dispatch_grads(
            m,
            sequences,
            local,
            base,
            routes_all[2 * m : 2 * m + 2],
            all_grads[2 * m : 2 * m + 2],
            after(shared_out, group_rows),
            held,
        )
    slot_grads, shared_raw = held
    along_x, along_y = after(along_x, slot_grads), after(along_y, slot_grads)
    first = grid.fetch(along_x[:middle], (1, 0, 0))
    second = grid.fetch(along_y[middle:], (0, 1, 0))
    raw = expert_raw(after(slot_grads, along_x, along_y), w_expert_out)
    first, second = after(first, raw), after(second, raw)
    rows = [group_rows, pair_rows]
    for held in (along_x, along_y):
        rows += [held, grid.fetch(held, (0, 0, 1))]
    rows += [
        jnp.concatenate([first, second]),
        jnp.concatenate([grid.fetch(first, (0, 0, 1)), grid.fetch(second, (0, 0, 1))]),
    ]

    held = [None] * 6
    for m in pairs:
        held = dispatch_rows(
            m,
            sequences,
            local,
            base,
            routes_all[2 * m : 2 * m + 2],
            rows[2 * m : 2 * m + 2],
            side,
            shared_raw,
            held,
        )
    slot_rows, infos, picks, gates, shared_hidden, shared_back = held
    expert_in = jnp.swapaxes(w_expert_in, 2, 3).reshape(local, 2 * hidden_units, width)
    back_rows, extra, hidden, back = expert_rows(slot_rows, infos, expert_in, raw)

    def backs(m, logits, *earlier):
        return combine_back(
            m, picks, after(back_rows, *earlier), extra, gates, shared_back, side, logits
        )

    front, rear = slice(None, row_count // 2), slice(row_count // 2, None)
    (near_6, far_6), logits = backs(3, [None])
    (near_4, far_4), logits = backs(2, logits, near_6)
    own_6 = low_add(near_6, grid.send(far_6, (0, 0, 1)))
    first = grid.send(own_6[front], (0, 1, 0))
    second = grid.send(own_6[rear], (1, 0, 0))
    (near_2, far_2), logits = backs(1, logits, own_6)
    own_4 = low_add(near_4, grid.send(far_4, (0, 0, 1)))
    (near_0, far_0), logits = backs(0, logits, own_4)
    own_2 = low_add(near_2, grid.send(far_2, (0, 0, 1)))
    first, second = after(first, near_0), after(second, near_0)
    to_y = jnp.concatenate([low_add(own_4[front], first), own_4[rear]])
    to_x = jnp.concatenate([own_2[front], low_add(own_2[rear], second)])
    from_x = grid.send(to_x, (0, 1, 0))
    from_y = grid.send(to_y, (1, 0, 0))

    def outs(m, *earlier):
        return combine_out(m, picks, after(out_rows, *earlier), shared_hidden, shared_out)

    out_rows = expert_out_rows(after(hidden, to_x, to_y), w_expert_out)
    own_0 = low_add(near_0, grid.send(far_0, (0, 0, 1)))
    out_6, out_7 = outs(3)
    out_4, out_5 = outs(2, out_6)
    from_x, from_y = after(from_x, out_4), after(from_y, out_4)
    grad_group = (own_0.astype(F32) + from_x.astype(F32) + from_y.astype(F32)).astype(BF16)
    chunks = split_rows(grad_group, depth)
    first, second = grid.ring_start(chunks)
    out_own_6 = low_add(after(out_6, grad_group), grid.send(after(out_7, grad_group), (0, 0, 1)))
    out_own_4 = low_add(out_4, grid.send(after(out_5, grad_group), (0, 0, 1)))
    out_first = grid.send(out_own_6[front], (0, 1, 0))
    out_second = grid.send(out_own_6[rear], (1, 0, 0))
    out_2, out_3 = outs(1, grad_group)
    first, second = after(first, out_2), after(second, out_2)
    ahead, behind, marks = grid.ring_finish(chunks, first, second)
    out_0, out_1 = outs(0, *marks)
    ahead, behind = after(ahead, out_0), after(behind, out_0)
    grad_normed = chunks[0].astype(F32) + ahead.astype(F32) + behind.astype(F32)

    grad_res_part, grad_ffn_gain = rms_backward(residual, inverse_two, ffn_gain, grad_normed)
    grad_residual = out_grad.astype(F32) + grad_res_part
    grad_low = grad_residual.astype(BF16)
    near_grads = grid.ring_near(grad_low)
    out_own_2 = low_add(out_2, grid.send(out_3, (0, 0, 1)))
    out_own_0 = low_add(out_0, grid.send(out_1, (0, 0, 1)))
    out_first, out_second = after(out_first, *near_grads), after(out_second, *near_grads)
    out_to_y = jnp.concatenate([low_add(out_own_4[front], out_first), out_own_4[rear]])
    out_to_x = jnp.concatenate([out_own_2[front], low_add(out_own_2[rear], out_second)])
    out_from_x = grid.send(out_to_x, (0, 1, 0))
    out_from_y = grid.send(out_to_y, (1, 0, 0))
    *grad_parts, grad_router = side_grads(
        blocks, base, rows, all_grads, after(logits[0], grad_low, out_to_x, out_to_y), shared_hidden, shared_back
    )
    out_from_x, out_from_y = after(out_from_x, grad_router), after(out_from_y, grad_router)
    far_grads = grid.ring_far(*near_grads)
    grads = [grad_low, near_grads[0], *(after(piece, grad_router) for piece in far_grads), near_grads[1]]

    returned = grid.exchange(grad_parts)
    grads[0] = after(grads[0], out_from_x, out_from_y)
    grad_query, grad_keyval, grad_normed_one, *chunks = attention_backward(
        heads,
        blocks,
        packs,
        tokens,
        grads,
        (query, keyval, key, soft, attended, compressed, low, normed),
        latent_t,
        kv_gain,
        cosine,
        sine,
        grad_router,
        grad_ffn_gain,
    )
    out_group = (
        out_own_0.astype(F32)
        + out_from_x.astype(F32)
        + out_from_y.astype(F32)
    ).astype(BF16)
    grad_packs = attention_weights(
        heads,
        blocks,
        packs[0].shape,
        grads,
        normed,
        low,
        attended,
        after(grad_query, *returned),
        grad_keyval,
    )
    sums, chunk_first, chunk_mark = grid.reduce_parts(chunks)
    share = local // 4
    held = [None, None]

    def weights(step, held, *earlier):
        return weight_grads(
            step * share,
            (step + 1) * share,
            after(slot_rows, *earlier),
            slot_grads,
            hidden,
            back,
            held[:2],
        )

    def ring_rounds(rows, start, middle, stop):
        parts = split_rows(after(rows, start), depth)
        first, second = grid.ring_start(parts)
        ahead, behind, _ = grid.ring_finish(parts, after(first, middle), after(second, middle))
        return sum(a.astype(F32) for a in (parts[0], after(ahead, stop), after(behind, stop)))

    held = weights(0, held, grad_packs[0], chunk_first)
    marks = [held[2]]
    held = weights(1, held, held[2], *chunk_mark)
    mark = held[2]
    marks.append(mark)
    size = CHUNK_ROWS // depth
    columns = width // grid.experts
    parts = vmem_call(
        sum_split_kernel,
        "sum_split",
        depths,
        [sums[0], after(sums[1], mark), after(sums[2], mark)],
        [jax.ShapeDtypeStruct((size, columns), BF16)] * depth,
        [],
    )
    pack_sums, pack_first, pack_mark = grid.reduce_parts([after(pack, mark) for pack in grad_packs])
    held = weights(2, held, parts[0], pack_first)
    marks.append(held[2])
    part = grid.reduce_depth([parts[0]] + [after(part, pack_first) for part in parts[1:]])
    part = after(part, held[2]).astype(BF16)
    *held, mark = weights(3, held, part, *pack_mark)
    grad_expert_in, grad_expert_out = held
    marks.append(mark)
    block_out = (residual + ring_rounds(out_group, *marks[:3])).astype(BF16)
    grad_normed_one = ring_rounds(grad_normed_one, *marks[1:])
    parts = [after(piece, mark) for piece in grid.gather_depth(part)]
    (chunk,) = vmem_call(
        join_depth_kernel,
        "join_depth",
        depths,
        parts,
        [jax.ShapeDtypeStruct((CHUNK_ROWS, columns), BF16)],
        [],
    )
    sum_shared_in, sum_shared_out = vmem_call(
        functools.partial(join_rows_kernel, units),
        "join_rows",
        blocks,
        [after(returned[0], chunk), *returned[1:]],
        [
            jax.ShapeDtypeStruct((2, units * grid.experts, width // grid.experts), F32),
            jax.ShapeDtypeStruct((units * grid.experts, width // grid.experts), F32),
        ],
        [],
    )
    gathered = grid.gather(chunk)
    gathered[0] = after(gathered[0], sum_shared_out, *pack_sums[1:])
    sum_latent, sum_router, sum_gains = vmem_call(
        functools.partial(replicated_kernel, KVR + ROPE),
        "replicated",
        blocks,
        gathered,
        [
            jax.ShapeDtypeStruct((KVR + ROPE, width), F32),
            jax.ShapeDtypeStruct((EXPERTS, width), F32),
            jax.ShapeDtypeStruct((16, width), F32),
        ],
        [],
    )
    sum_kv_gain = sum_gains[2 : 2 + KVR // columns, :columns].reshape(KVR)

    inverse_one = lax.rsqrt(jnp.mean(stream * stream, axis=-1, keepdims=True) + EPSILON)
    grad_in = grad_residual + rms_backward(stream, inverse_one, attn_gain, grad_normed_one)[0]
    sum_query, sum_keyval, sum_output = unpack_weights(
        sum(array.astype(F32) for array in pack_sums), w_keyval.shape, w_output.shape, heads
    )
    return (
        block_out,
        grad_in,
        sum_gains[0],
        sum_kv_gain,
        sum_gains[1],
        sum_query,
        sum_latent.T,
        sum_keyval,
        sum_output,
        sum_router.T,
        jnp.swapaxes(sum_shared_in, 1, 2),
        sum_shared_out,
        jnp.swapaxes(grad_expert_in.reshape(local, 2, hidden_units, width), 2, 3),
        grad_expert_out,
    )


def solution(mesh):
    placed = (
        P(("expert", "tensor"), None),
        P(("expert", "tensor"), None),
        P("expert", None),
        P(),
        P(),
        P(),
        P("expert", "tensor"),
        P(),
        P("expert", "tensor"),
        P("tensor", "expert"),
        P(),
        P(None, "expert", "tensor"),
        P("tensor", "expert"),
        P("expert", None, None, "tensor"),
        P("expert", "tensor", None),
    )
    square = mesh.shape["expert"] == 8 and mesh.shape["tensor"] == 4
    return jax.shard_map(
        square_device if square else general_device,
        mesh=mesh,
        in_specs=placed,
        out_specs=(
            P(("expert", "tensor"), None),
            P(("expert", "tensor"), None),
            P(),
            P(),
            P(),
            P("expert", "tensor"),
            P(),
            P("expert", "tensor"),
            P("tensor", "expert"),
            P(),
            P(None, "expert", "tensor"),
            P("tensor", "expert"),
            P("expert", None, None, "tensor"),
            P("expert", "tensor", None),
        ),
        check_vma=False,
    )
```

```python
import functools
import math

import jax
import jax.numpy as jnp
from jax import lax
from jax.experimental import pallas as pl
from jax.experimental.pallas import tpu as pltpu
from jax.sharding import PartitionSpec as P

NOPE = 128
ROPE = 64
VD = 128
KVR = 512
EXPERTS = 64
TOP = 6
SLOTS = 32
SLOT_BLOCK = 256
LANES = 128
PARTS = 2
CHUNK_ROWS = 704

EPSILON = 1e-06
ROUTE_SCALE = 2.446
ROPE_BASE = 50000.0
BF16 = jnp.bfloat16
F32 = jnp.float32


def mix_dot(left_side, right_side):
    return jnp.dot(left_side, right_side, preferred_element_type=F32)


def contract(pattern, left_side, right_side):
    return jnp.einsum(pattern, left_side, right_side, preferred_element_type=F32)


def rms_forward(values, gain_vec):
    inverse = lax.rsqrt(jnp.mean(values * values, axis=-1, keepdims=True) + EPSILON)
    return (values * inverse * gain_vec, inverse)


def rms_backward(values, inverse, gain_vec, grad_normed):
    weighted = grad_normed * gain_vec
    grad_values = inverse * weighted - values * (inverse * inverse * inverse) * jnp.mean(
        values * weighted, axis=-1, keepdims=True
    )
    grad_gain = jnp.sum(grad_normed * values * inverse, axis=0)
    return (grad_values, grad_gain)


def rope_tables(position):
    half_rope = ROPE // 2
    frequency = jnp.exp(-jnp.log(ROPE_BASE) * jnp.arange(half_rope).astype(F32) / half_rope)
    angles = position.astype(F32)[:, None] * frequency[None, :]
    return (jnp.cos(angles), jnp.sin(angles))


def rotate(columns, cosine, sine_table):
    half_rope = columns.shape[-1] // 2
    first_half = columns[..., :half_rope]
    second_half = columns[..., half_rope:]
    return jnp.concatenate(
        [
            first_half * cosine - second_half * sine_table,
            first_half * sine_table + second_half * cosine,
        ],
        axis=-1,
    )


def low_add(first, second):
    return (first.astype(F32) + second.astype(F32)).astype(BF16)


class Grid:
    def __init__(self):
        self.experts = lax.axis_size("expert")
        self.depth = lax.axis_size("tensor")
        self.side = math.isqrt(self.experts // 2)
        assert self.side * self.side * 2 == self.experts
        self.offsets = [
            (dy, dx, dc)
            for dy in range(self.side)
            for dx in range(self.side)
            for dc in range(2)
        ]

    def neighbour(self, place, offset):
        side = self.side
        y, x, core = place // (2 * side), place // 2 % side, place % 2
        dy, dx, dc = offset
        return (((y + dy) % side) * side + (x + dx) % side) * 2 + (core + dc) % 2

    def place_of(self, offset):
        return self.neighbour(lax.axis_index("expert"), offset)

    def fetch(self, array, offset):
        pairs = [(self.neighbour(place, offset), place) for place in range(self.experts)]
        return lax.ppermute(array, "expert", pairs)

    def send(self, array, offset):
        pairs = [(place, self.neighbour(place, offset)) for place in range(self.experts)]
        return lax.ppermute(array, "expert", pairs)

    def gather(self, shard):
        if self.side != 2:
            return [shard] + [self.fetch(shard, offset) for offset in self.offsets[1:]]
        half = shard.shape[0] // 2
        along_x = self.fetch(shard, (0, 1, 0))
        along_y = self.fetch(shard, (1, 0, 0))
        pair = self.fetch(shard, (0, 0, 1))
        first = self.fetch(along_x[:half], (1, 0, 0))
        second = self.fetch(along_y[half:], (0, 1, 0))
        pair_x = self.fetch(along_x, (0, 0, 1))
        pair_y = self.fetch(along_y, (0, 0, 1))
        pair_first = self.fetch(first, (0, 0, 1))
        pair_second = self.fetch(second, (0, 0, 1))
        return [
            shard,
            pair,
            along_x,
            pair_x,
            along_y,
            pair_y,
            jnp.concatenate([first, second]),
            jnp.concatenate([pair_first, pair_second]),
        ]

    def reduce(self, chunks):
        if self.side != 2:
            total = chunks[0].astype(F32)
            for offset, chunk in zip(self.offsets[1:], chunks[1:]):
                total = total + self.send(chunk, offset).astype(F32)
            return total
        half = chunks[0].shape[0] // 2
        own = {}
        for place in (6, 2, 4, 0):
            own[place] = low_add(chunks[place], self.send(chunks[place + 1], (0, 0, 1)))
        first = self.send(own[6][:half], (0, 1, 0))
        second = self.send(own[6][half:], (1, 0, 0))
        to_y = jnp.concatenate([low_add(own[4][:half], first), own[4][half:]])
        to_x = jnp.concatenate([own[2][:half], low_add(own[2][half:], second)])
        from_x = self.send(to_x, (0, 1, 0))
        from_y = self.send(to_y, (1, 0, 0))
        return own[0].astype(F32) + from_x.astype(F32) + from_y.astype(F32)

    def gather_small(self, shard):
        along_x = self.fetch(shard, (0, 1, 0))
        along_y = self.fetch(shard, (1, 0, 0))
        near = [shard, along_x, along_y, self.fetch(along_x, (1, 0, 0))]
        return [piece for held in near for piece in (held, self.fetch(held, (0, 0, 1)))]

    def exchange(self, parts):
        pieces = [parts[0]]
        for dy, dx, dc in self.offsets[1:]:
            back = (-dy % self.side, -dx % self.side, dc)
            pieces.append(self.send(parts[self.offsets.index(back)], back))
        return pieces

    def reduce_parts(self, chunks):
        own, first, marks = self.reduce_first(chunks)
        return [own, *self.reduce_second(*marks)], first, marks

    def reduce_second(self, to_x, to_y):
        return self.send(to_x, (0, 1, 0)), self.send(to_y, (1, 0, 0))

    def reduce_first(self, chunks):
        half = chunks[0].shape[0] // 2
        own = {}
        for place in (6, 2, 4, 0):
            own[place] = low_add(chunks[place], self.send(chunks[place + 1], (0, 0, 1)))
        first = self.send(own[6][:half], (0, 1, 0))
        second = self.send(own[6][half:], (1, 0, 0))
        to_y = jnp.concatenate([low_add(own[4][:half], first), own[4][half:]])
        to_x = jnp.concatenate([own[2][:half], low_add(own[2][half:], second)])
        return own[0], own[6], (to_x, to_y)

    def ring(self, array, step):
        depth = self.depth
        return lax.ppermute(array, "tensor", [(i, (i + step) % depth) for i in range(depth)])

    def ring_near(self, shard):
        return self.ring(shard, -1), self.ring(shard, 1)

    def ring_far(self, ahead, behind):
        half = ahead.shape[0] // 2
        return self.ring(ahead[:half], -1), self.ring(behind[half:], 1)

    def ring_gather(self, shard):
        ahead, behind = self.ring_near(shard)
        return [shard, ahead, *self.ring_far(ahead, behind), behind]

    def ring_start(self, chunks):
        half = chunks[2].shape[0] // 2
        first = self.ring(chunks[2][:half], 1)
        second = self.ring(chunks[2][half:], -1)
        return first, second

    def ring_finish(self, chunks, first, second):
        half = chunks[2].shape[0] // 2
        to_ahead = jnp.concatenate([low_add(chunks[1][:half], first), chunks[1][half:]])
        to_behind = jnp.concatenate([chunks[3][:half], low_add(chunks[3][half:], second)])
        return self.ring(to_ahead, 1), self.ring(to_behind, -1), (to_ahead, to_behind)

    def ring_reduce(self, chunks):
        ahead, behind, _ = self.ring_finish(chunks, *self.ring_start(chunks))
        return chunks[0].astype(F32) + ahead.astype(F32) + behind.astype(F32)

    def gather_depth(self, shard):
        depth = self.depth
        return [shard] + [
            lax.ppermute(shard, "tensor", [((i + k) % depth, i) for i in range(depth)])
            for k in range(1, depth)
        ]

    def reduce_depth(self, chunks):
        depth = self.depth
        total = chunks[0].astype(F32)
        for k in range(1, depth):
            total = total + lax.ppermute(
                chunks[k], "tensor", [(i, (i + k) % depth) for i in range(depth)]
            ).astype(F32)
        return total

    def absolute(self, pieces, axis):
        size = pieces[0].shape[axis]
        shape = list(pieces[0].shape)
        shape[axis] = size * self.experts
        whole = jnp.zeros(shape, pieces[0].dtype)
        for offset, piece in zip(self.offsets, pieces):
            whole = lax.dynamic_update_slice_in_dim(
                whole, piece, self.place_of(offset) * size, axis
            )
        return whole

    def relative(self, whole, axis):
        size = whole.shape[axis] // self.experts
        return [
            lax.dynamic_slice_in_dim(whole, self.place_of(offset) * size, size, axis)
            for offset in self.offsets
        ]

    def absolute_depth(self, pieces, axis):
        size = pieces[0].shape[axis]
        shape = list(pieces[0].shape)
        shape[axis] = size * self.depth
        whole = jnp.zeros(shape, pieces[0].dtype)
        own = lax.axis_index("tensor")
        for k, piece in enumerate(pieces):
            whole = lax.dynamic_update_slice_in_dim(
                whole, piece, (own + k) % self.depth * size, axis
            )
        return whole

    def relative_depth(self, whole, axis):
        size = whole.shape[axis] // self.depth
        own = lax.axis_index("tensor")
        return [
            lax.dynamic_slice_in_dim(whole, (own + k) % self.depth * size, size, axis)
            for k in range(self.depth)
        ]


def split_rows(array, count):
    size = array.shape[0] // count
    return [array[i * size : (i + 1) * size] for i in range(count)]


def attention_scores(queries, key_nope, key_rope, position):
    scores = contract("qhd,khd->hqk", queries[..., :NOPE], key_nope) + contract(
        "qhr,kr->hqk", queries[..., NOPE:], key_rope
    )
    scores = scores * ((NOPE + ROPE) ** (-0.5))
    allowed = position[None, :] <= position[:, None]
    return jnp.where(allowed[None], scores, -1e30)


def dot_nn(left, right):
    return lax.dot_general(left, right, (((1,), (0,)), ((), ())), preferred_element_type=F32)


def dot_nt(left, right):
    return lax.dot_general(left, right, (((1,), (1,)), ((), ())), preferred_element_type=F32)


def dot_tn(left, right):
    return lax.dot_general(left, right, (((0,), (0,)), ((), ())), preferred_element_type=F32)


def silu_parts(gate):
    sigmoid = 1.0 / (1.0 + jnp.exp(-gate))
    return sigmoid, gate * sigmoid


def split_high(value):
    high = value.astype(BF16)
    return high, (value - high.astype(F32)).astype(BF16)


def whole(shape):
    return pl.BlockSpec(shape, lambda *_: (0,) * len(shape))


def params(*semantics):
    return pltpu.CompilerParams(
        dimension_semantics=semantics or None, vmem_limit_bytes=56 * 1024 * 1024
    )


ANYWHERE = pl.BlockSpec(memory_space=pl.ANY)


def pick_rows(routes, base, local):
    count = routes.shape[1]
    expert = lax.broadcasted_iota(jnp.int32, (EXPERTS, count), 0) + base
    expert = jnp.where(expert >= EXPERTS, expert - EXPERTS, expert)
    chosen = expert == routes[0:1]
    for k in range(1, TOP):
        chosen = chosen | (expert == routes[k : k + 1])
    chosen = chosen.astype(F32)
    rows = max(local, 16)
    earlier = lax.broadcasted_iota(jnp.int32, (count, count), 0) < lax.broadcasted_iota(
        jnp.int32, (count, count), 1
    )
    rank = dot_nn(chosen[:rows].astype(BF16), earlier.astype(F32).astype(BF16))
    rank = jnp.where(chosen[:rows] > 0.5, rank, -1.0)
    slot = lax.broadcasted_iota(jnp.int32, (SLOTS, count), 0).astype(F32)
    parts = [(slot == rank[j : j + 1]).astype(F32) for j in range(local)]
    return jnp.concatenate(parts, axis=0), chosen


def dispatch_grads_kernel(local, base_ref, *refs):
    routes, grads, shared_ref = refs[:2], refs[2:4], refs[4]
    slot_ref, raw_ref, mark_ref = refs[-3:]
    mark_ref[...] = jnp.zeros_like(mark_ref)
    for i in range(2):

        @pl.when(pl.program_id(0) == i)
        def _():
            pick, _ = pick_rows(routes[i][...], base_ref[0], local)
            values = grads[i][...]
            slot_ref[...] = (
                dot_nn(pick.astype(BF16), values).astype(BF16).reshape(slot_ref.shape)
            )
            raw_ref[0] = dot_nt(shared_ref[...], values)


def dispatch_rows_kernel(local, units, base_ref, *refs):
    routes, pieces, side_ref, raw_ref = refs[:2], refs[2:4], refs[4], refs[5]
    slot_ref, info_ref, pick_ref, gate_ref, hidden_ref, back_ref = refs[-6:]
    for i in range(2):

        @pl.when(pl.program_id(0) == i)
        def _():
            pick, chosen = pick_rows(routes[i][...], base_ref[0], local)
            rows = pieces[i][...]
            low = pick.astype(BF16)
            pick_ref[0] = low
            slot_ref[...] = dot_nn(low, rows).astype(BF16).reshape(slot_ref.shape)
            side = dot_nt(side_ref[...], rows)
            gate, up, raw = side[:units], side[units : 2 * units], raw_ref[0]
            sigmoid = chosen / (1.0 + jnp.exp(-side[2 * units :]))
            total = jnp.sum(sigmoid, axis=0, keepdims=True)
            gate_ref[0, 0] = sigmoid
            gate_ref[0, 1] = jnp.broadcast_to(total, sigmoid.shape)
            weight = ROUTE_SCALE * sigmoid / total
            scale = jnp.concatenate(
                [
                    jnp.sum(
                        pick[j * SLOTS : (j + 1) * SLOTS] * weight[j : j + 1],
                        axis=1,
                        keepdims=True,
                    )
                    for j in range(local)
                ],
                axis=0,
            )
            high, low_part = split_high(scale)
            lane = lax.broadcasted_iota(jnp.int32, (scale.shape[0], LANES), 1)
            info = jnp.where(
                lane == 0, high.astype(F32), jnp.where(lane == 1, low_part.astype(F32), 0.0)
            )
            info_ref[...] = info.astype(BF16).reshape(info_ref.shape)
            smooth, active = silu_parts(gate)
            hidden_ref[0] = (active * up).astype(BF16)
            back_ref[0] = jnp.concatenate(
                [raw * up * smooth * (1.0 + gate * (1.0 - smooth)), raw * active], axis=0
            ).astype(BF16)


def expert_raw_kernel(grads_ref, out_ref, raw_ref):
    raw_ref[0] = dot_nt(out_ref[0], grads_ref[0])


def expert_kernel(
    units, rows_ref, info_ref, in_ref, raw_ref, back_rows_ref, extra_ref, hidden_ref, back_ref
):
    expert = pl.program_id(0)
    weight_in = in_ref[0]
    gates = dot_nt(weight_in, rows_ref[0])
    raw = raw_ref[0]
    gate, up = gates[:units], gates[units:]
    lane = lax.broadcasted_iota(jnp.int32, (16, LANES), 1)
    select = (lane < 2).astype(F32).astype(BF16)
    scale = dot_nt(select, info_ref[0])[0:1]
    smooth, active = silu_parts(gate)
    hidden = active * up
    grad_gate = jnp.sum(hidden.astype(BF16).astype(F32) * raw, axis=0, keepdims=True)
    hidden_ref[0] = (hidden * scale).astype(BF16)
    raw = raw * scale
    back = jnp.concatenate(
        [raw * up * smooth * (1.0 + gate * (1.0 - smooth)), raw * active], axis=0
    ).astype(BF16)
    back_ref[0] = back
    back_rows_ref[0] = dot_tn(back, weight_in).astype(BF16)
    high, low = split_high(grad_gate)
    row = lax.broadcasted_iota(jnp.int32, (16, grad_gate.shape[1]), 0)
    pair = jnp.where(row == 0, high.astype(F32), jnp.where(row == 1, low.astype(F32), 0.0))
    row = lax.broadcasted_iota(jnp.int32, (16, LANES), 0)
    lane = lax.broadcasted_iota(jnp.int32, (16, LANES), 1)
    place = ((row < 2) & (lane == expert + row * EXPERTS)).astype(F32)
    extra_ref[0] = dot_tn(pair.astype(BF16), place.astype(BF16)).astype(BF16)


def expert_out_kernel(hidden_ref, out_ref, rows_ref):
    rows_ref[0] = dot_tn(hidden_ref[0], out_ref[0]).astype(BF16)


def weight_grad_kernel(rows_ref, grads_ref, hidden_ref, back_ref, *rest):
    in_ref, out_ref, mark_ref = rest[-3:]
    mark_ref[...] = jnp.zeros_like(mark_ref)

    @pl.when(pl.program_id(1) == 0)
    def _():
        in_ref[0] = dot_nn(back_ref[0], rows_ref[0])
        out_ref[0] = dot_nn(hidden_ref[0], grads_ref[0])

    @pl.when(pl.program_id(1) > 0)
    def _():
        in_ref[0] += dot_nn(back_ref[0], rows_ref[0])
        out_ref[0] += dot_nn(hidden_ref[0], grads_ref[0])


def combine_back_kernel(
    pick_ref, slots_ref, extra_ref, gate_ref, back_ref, side_ref, *rest
):
    first_ref, second_ref, logits_ref, left_ref = rest[-4:]
    piece, part = pl.program_id(0), pl.program_id(1)
    flat = pick_ref.shape[1]
    units = back_ref.shape[1]

    @pl.when(part == 0)
    def _():
        merged = dot_tn(extra_ref[...].reshape(flat, LANES), pick_ref[0])
        grad_gate = merged[:EXPERTS] + merged[EXPERTS:]
        sigmoid, total = gate_ref[0, 0], gate_ref[0, 1]
        mixed = jnp.sum(grad_gate * sigmoid, axis=0, keepdims=True)
        logits = (
            ROUTE_SCALE
            * (grad_gate / total - mixed / (total * total))
            * sigmoid
            * (1.0 - sigmoid)
        ).astype(BF16)
        logits_ref[0] = logits
        left_ref[:units] = back_ref[0]
        left_ref[units:] = logits

    value = (
        dot_tn(pick_ref[0], slots_ref[...].reshape(flat, slots_ref.shape[2]))
        + dot_tn(left_ref[...], side_ref[...])
    ).astype(BF16)

    @pl.when(piece == 0)
    def _():
        first_ref[...] = value

    @pl.when(piece == 1)
    def _():
        second_ref[...] = value


def combine_out_kernel(pick_ref, slots_ref, hidden_ref, shared_ref, first_ref, second_ref):
    value = (
        dot_tn(pick_ref[0], slots_ref[...].reshape(pick_ref.shape[1], slots_ref.shape[2]))
        + dot_tn(hidden_ref[0], shared_ref[...])
    ).astype(BF16)

    @pl.when(pl.program_id(0) == 0)
    def _():
        first_ref[...] = value

    @pl.when(pl.program_id(0) == 1)
    def _():
        second_ref[...] = value


def chain_call(kernel, name, grid, prefetch, operands, in_specs, held, out_specs, out_shape, scratch=()):
    chained = [a for a in held if a is not None]
    at = len(prefetch) + len(operands)
    return pl.pallas_call(
        kernel,
        grid_spec=pltpu.PrefetchScalarGridSpec(
            num_scalar_prefetch=len(prefetch),
            grid=grid,
            in_specs=in_specs + [ANYWHERE] * len(chained),
            out_specs=out_specs,
            scratch_shapes=list(scratch),
        ),
        out_shape=out_shape,
        input_output_aliases={at + i: i for i in range(len(chained))},
        compiler_params=params(*["arbitrary"] * len(grid)),
        name=name,
    )(*prefetch, *operands, *chained)


def dispatch_grads(pair, sequences, local, base, routes, grads, shared_out, held):
    count, width = grads[0].shape
    units = shared_out.shape[0]
    operands = [*routes, *grads, shared_out]
    return chain_call(
        functools.partial(dispatch_grads_kernel, local),
        "dispatch_grads",
        (2,),
        [base],
        operands,
        [whole(a.shape) for a in operands],
        held,
        [
            pl.BlockSpec((local, SLOTS, width), lambda i, *_: (0, 2 * pair + i, 0)),
            pl.BlockSpec((1, units, count), lambda i, *_: (2 * pair + i, 0, 0)),
            whole((8, LANES)),
        ],
        [
            jax.ShapeDtypeStruct((local, sequences * SLOTS, width), BF16),
            jax.ShapeDtypeStruct((sequences, units, count), F32),
            jax.ShapeDtypeStruct((8, LANES), F32),
        ],
    )


def dispatch_rows(pair, sequences, local, base, routes, rows, side, raws, held):
    count, width = rows[0].shape
    units = raws.shape[1]
    operands = [*routes, *rows, side]
    shapes = [
        ((local * SLOTS, count), BF16),
        ((2, EXPERTS, count), F32),
        ((units, count), BF16),
        ((2 * units, count), BF16),
    ]

    def at(shape):
        return pl.BlockSpec((1,) + shape, lambda i, *_: (2 * pair + i,) + (0,) * len(shape))

    return chain_call(
        functools.partial(dispatch_rows_kernel, local, units),
        "dispatch_rows",
        (2,),
        [base],
        operands + [raws],
        [whole(a.shape) for a in operands] + [at((units, count))],
        held,
        [
            pl.BlockSpec((local, SLOTS, width), lambda i, *_: (0, 2 * pair + i, 0)),
            pl.BlockSpec((local, SLOTS, LANES), lambda i, *_: (0, 2 * pair + i, 0)),
        ]
        + [at(shape) for shape, _ in shapes],
        [
            jax.ShapeDtypeStruct((local, sequences * SLOTS, width), BF16),
            jax.ShapeDtypeStruct((local, sequences * SLOTS, LANES), BF16),
        ]
        + [jax.ShapeDtypeStruct((sequences,) + shape, dtype) for shape, dtype in shapes],
    )


def tile(*shape):
    return pl.BlockSpec((1,) + shape, lambda j, b: (j, b) + (0,) * (len(shape) - 1))


def lane_tile(*shape):
    return pl.BlockSpec((1,) + shape, lambda j, b: (j, 0, b))


def one(*shape):
    return pl.BlockSpec((1,) + shape, lambda j, b: (j, 0, 0))


def expert_raw(grads, expert_out):
    local, slots, width = grads.shape
    units = expert_out.shape[1]
    block = min(slots, SLOT_BLOCK)
    return pl.pallas_call(
        expert_raw_kernel,
        grid=(local, slots // block),
        in_specs=[tile(block, width), one(units, width)],
        out_specs=lane_tile(units, block),
        out_shape=jax.ShapeDtypeStruct((local, units, slots), F32),
        compiler_params=params("arbitrary", "arbitrary"),
        name="expert_raw",
    )(grads, expert_out)


def expert_rows(rows, infos, expert_in, raw):
    local, slots, width = rows.shape
    units = raw.shape[1]
    block = min(slots, SLOT_BLOCK)
    return pl.pallas_call(
        functools.partial(expert_kernel, units),
        grid=(local, slots // block),
        in_specs=[
            tile(block, width),
            tile(block, LANES),
            one(2 * units, width),
            lane_tile(units, block),
        ],
        out_specs=[
            tile(block, width),
            tile(block, LANES),
            lane_tile(units, block),
            lane_tile(2 * units, block),
        ],
        out_shape=[
            jax.ShapeDtypeStruct((local, slots, width), BF16),
            jax.ShapeDtypeStruct((local, slots, LANES), BF16),
            jax.ShapeDtypeStruct((local, units, slots), BF16),
            jax.ShapeDtypeStruct((local, 2 * units, slots), BF16),
        ],
        compiler_params=params("arbitrary", "arbitrary"),
        name="expert_rows",
    )(rows, infos, expert_in, raw)


def expert_out_rows(hidden, expert_out):
    local, units, slots = hidden.shape
    width = expert_out.shape[2]
    block = min(slots, SLOT_BLOCK)
    return pl.pallas_call(
        expert_out_kernel,
        grid=(local, slots // block),
        in_specs=[lane_tile(units, block), one(units, width)],
        out_specs=tile(block, width),
        out_shape=jax.ShapeDtypeStruct((local, slots, width), BF16),
        compiler_params=params("arbitrary", "arbitrary"),
        name="expert_out_rows",
    )(hidden, expert_out)


def weight_grads(start, stop, rows, grads, hidden, back, held):
    local, slots, width = rows.shape
    units = hidden.shape[1]
    block = min(slots, SLOT_BLOCK)

    def moved(spec):
        return pl.BlockSpec(
            spec.block_shape, lambda j, b: (lambda at: (at[0] + start,) + at[1:])(spec.index_map(j, b))
        )

    return chain_call(
        weight_grad_kernel,
        "weight_grads",
        (stop - start, slots // block),
        [],
        [rows, grads, hidden, back],
        [
            moved(spec)
            for spec in (
                tile(block, width),
                tile(block, width),
                lane_tile(units, block),
                lane_tile(2 * units, block),
            )
        ],
        held,
        [moved(one(2 * units, width)), moved(one(units, width)), whole((8, LANES))],
        [
            jax.ShapeDtypeStruct((local, 2 * units, width), F32),
            jax.ShapeDtypeStruct((local, units, width), F32),
            jax.ShapeDtypeStruct((8, LANES), F32),
        ],
    )


def piece_specs(width, part):
    return [
        pl.BlockSpec((width[0], part), lambda i, h: (0, jnp.where(i == 0, h, width[1] - 1))),
        pl.BlockSpec((width[0], part), lambda i, h: (0, jnp.where(i == 0, 0, h))),
    ]


def combine_back(pair, picks, slots, extra, gates, backs, side, held):
    sequences, flat, count = picks.shape
    local, _, width = slots.shape
    part = width // PARTS

    def at(array):
        shape = array.shape[1:]
        return pl.BlockSpec((1,) + shape, lambda i, h: (2 * pair + i,) + (0,) * len(shape))

    def strip(size):
        return pl.BlockSpec((local, SLOTS, size), lambda i, h: (0, 2 * pair + i, 0))

    outs = chain_call(
        lambda *refs: combine_back_kernel(*refs[:6], *refs[-3:-1], refs[-4], refs[-1]),
        "combine_back",
        (2, PARTS),
        [],
        [picks, slots, extra, gates, backs, side],
        [
            at(picks),
            pl.BlockSpec((local, SLOTS, part), lambda i, h: (0, 2 * pair + i, h)),
            strip(LANES),
            at(gates),
            at(backs),
            pl.BlockSpec((side.shape[0], part), lambda i, h: (0, h)),
        ],
        held,
        [pl.BlockSpec((1, EXPERTS, count), lambda i, h: (2 * pair + i, 0, 0))]
        + piece_specs((count, PARTS), part),
        [jax.ShapeDtypeStruct((sequences, EXPERTS, count), BF16)]
        + [jax.ShapeDtypeStruct((count, width), BF16)] * 2,
        [pltpu.VMEM((side.shape[0], count), BF16)],
    )
    return outs[1:], outs[:1]


def combine_out(pair, picks, slots, hiddens, shared_out):
    _, flat, count = picks.shape
    local, _, width = slots.shape
    part = width // PARTS
    units = hiddens.shape[1]
    return pl.pallas_call(
        combine_out_kernel,
        grid=(2, PARTS),
        in_specs=[
            pl.BlockSpec((1, flat, count), lambda i, h: (2 * pair + i, 0, 0)),
            pl.BlockSpec((local, SLOTS, part), lambda i, h: (0, 2 * pair + i, h)),
            pl.BlockSpec((1, units, count), lambda i, h: (2 * pair + i, 0, 0)),
            pl.BlockSpec((units, part), lambda i, h: (0, h)),
        ],
        out_specs=piece_specs((count, PARTS), part),
        out_shape=[jax.ShapeDtypeStruct((count, width), BF16)] * 2,
        compiler_params=params("arbitrary", "arbitrary"),
        name="combine_out",
    )(picks, slots, hiddens, shared_out)


def side_grads_kernel(sequences, block_ref, *refs):
    rows, grads, rest = refs[:sequences], refs[sequences : 2 * sequences], refs[2 * sequences :]
    logits_ref, hidden_ref, back_ref, first_ref, *parts, router_ref, left_ref, in_ref, out_ref = rest
    units = hidden_ref.shape[1]
    for s in range(sequences):
        left_ref[: 2 * units] = back_ref[s]
        left_ref[2 * units :] = logits_ref[s]
        value = dot_nn(left_ref[...], rows[s][...])
        other = dot_nn(hidden_ref[s], grads[s][...])
        if s == 0:
            in_ref[...] = value
            out_ref[...] = other
        else:
            in_ref[...] += value
            out_ref[...] += other
    shards, columns = len(parts), parts[0].shape[1]
    for k in range(shards):
        at = pl.ds(pl.multiple_of(block_ref[k] * columns, columns), columns)
        parts[k][: 2 * units] = in_ref[: 2 * units, at].astype(BF16)
        parts[k][2 * units :] = out_ref[:, at].astype(BF16)
    local = EXPERTS // shards
    for k in range(shards):
        start = first_ref[0] + k * local
        start = jnp.where(start >= EXPERTS, start - EXPERTS, start)
        router_ref[pl.ds(pl.multiple_of(start, local), local)] = in_ref[
            2 * units + k * local : 2 * units + (k + 1) * local
        ]


def side_grads(blocks, base, rows, grads, logits, hiddens, backs):
    sequences = len(rows)
    count, width = rows[0].shape
    units = hiddens.shape[1]
    shards = blocks.shape[0]
    operands = [*rows, *grads, logits, hiddens, backs]
    return pl.pallas_call(
        functools.partial(side_grads_kernel, sequences),
        grid_spec=pltpu.PrefetchScalarGridSpec(
            num_scalar_prefetch=1,
            grid=(1,),
            in_specs=[whole(a.shape) for a in operands]
            + [pl.BlockSpec(memory_space=pltpu.SMEM)],
            out_specs=[whole((3 * units, width // shards))] * shards + [whole((EXPERTS, width))],
            scratch_shapes=[
                pltpu.VMEM((2 * units + EXPERTS, count), BF16),
                pltpu.VMEM((2 * units + EXPERTS, width), F32),
                pltpu.VMEM((units, width), F32),
            ],
        ),
        out_shape=[jax.ShapeDtypeStruct((3 * units, width // shards), BF16)] * shards
        + [jax.ShapeDtypeStruct((EXPERTS, width), F32)],
        compiler_params=params("arbitrary"),
        name="side_grads",
    )(blocks, *operands, base)


def join_columns_kernel(used, block_ref, *refs):
    shards = (len(refs) - 3) // 2
    pieces, router_ref, side_ref, out_ref, routes = (
        refs[:shards], refs[shards], refs[shards + 1], refs[shards + 2], refs[shards + 3 :]
    )
    units = out_ref.shape[0]
    columns = pieces[0].shape[1]
    for k, piece in enumerate(pieces):
        at = pl.ds(pl.multiple_of(block_ref[k] * columns, columns), columns)
        side_ref[: 2 * units, at] = piece[: 2 * units]
        out_ref[:, at] = piece[2 * units :]
        routes[k][...] = piece[:units].astype(F32)[used:].astype(jnp.int32)
    side_ref[used:units] = jnp.zeros((units - used, side_ref.shape[1]), BF16)
    side_ref[2 * units :] = router_ref[...]


def join_rows_kernel(units, block_ref, *refs):
    parts, in_ref, out_ref = refs[:-2], refs[-2], refs[-1]
    padded = parts[0].shape[0] // 3
    for k, part in enumerate(parts):
        at = pl.ds(pl.multiple_of(block_ref[k] * units, 8), units)
        value = part[...].astype(F32)
        in_ref[0, at] = value[:units]
        in_ref[1, at] = value[padded : padded + units]
        out_ref[at] = value[2 * padded : 2 * padded + units]


def replicated_kernel(used, block_ref, *refs):
    chunks, latent_ref, router_ref, gains_ref = refs[:-3], refs[-3], refs[-2], refs[-1]
    columns = chunks[0].shape[1]
    for k, chunk in enumerate(chunks):
        at = pl.ds(pl.multiple_of(block_ref[k] * columns, columns), columns)
        latent_ref[:, at] = chunk[:used].astype(F32)
        router_ref[:, at] = chunk[used : used + EXPERTS].astype(F32)
        gains_ref[:, at] = chunk[used + EXPERTS : used + EXPERTS + 16].astype(F32)


def rope_turn(first, second, cosine, sine):
    return first * cosine - second * sine, first * sine + second * cosine


def unit_rows(pieces, width):
    values = jnp.concatenate([piece[:, :width] for piece in pieces], axis=0).astype(F32)
    inverse = lax.rsqrt(jnp.mean(values * values, axis=-1, keepdims=True) + EPSILON)
    return values * inverse


def latent_kernel(depth, *refs):
    pieces = refs[:depth]
    gain_ref, weight_ref, kv_gain_ref, cosine_ref, sine_ref = refs[depth : depth + 5]
    normed_ref, comp_ref, low_ref, key_ref, wide_ref = refs[depth + 5 :]
    half = ROPE // 2
    wide_ref[:KVR] = weight_ref[:KVR]
    for i in range(2):
        piece = weight_ref[KVR + i * half : KVR + (i + 1) * half]
        for j in range(LANES // half):
            start = KVR + i * LANES + j * half
            wide_ref[start : start + half] = piece
    normed = (unit_rows(pieces, gain_ref.shape[1]) * gain_ref[...]).astype(BF16)
    normed_ref[...] = normed
    latent = dot_nt(normed, wide_ref[...])
    compressed = latent[:, :KVR]
    comp_ref[...] = compressed
    inverse = lax.rsqrt(jnp.mean(compressed * compressed, axis=-1, keepdims=True) + EPSILON)
    low_ref[...] = (compressed * inverse * kv_gain_ref[...]).astype(BF16)
    first, second = rope_turn(
        latent[:, KVR : KVR + LANES], latent[:, KVR + LANES :], cosine_ref[...], sine_ref[...]
    )
    key_ref[...] = jnp.concatenate([first, second], axis=1).astype(BF16)


def head_mask(head):
    lane = lax.broadcasted_iota(jnp.int32, (1, LANES), 1)
    return ((lane // (ROPE // 2)) == head).astype(F32)


def keyval_weight(block_ref, packs, whole_ref, queries):
    share = KVR // len(packs)
    count = packs[0].shape[0] // share
    columns = whole_ref.shape[1] // count
    for k, pack in enumerate(packs):
        start = pl.multiple_of(block_ref[k] * share, share)
        for i in range(count):
            whole_ref[pl.ds(start, share), i * columns : (i + 1) * columns] = pack[
                i * share : (i + 1) * share, queries : queries + columns
            ]


def attention_kernel(heads, block_ref, *refs):
    shards = len(refs) - 13
    packs = refs[:shards]
    normed_ref, low_ref, key_ref, bias_ref, cosine_ref, sine_ref = refs[shards : shards + 6]
    query_ref, keyval_ref, soft_ref, attended_ref, part_ref, total_ref, weight_ref = refs[
        shards + 6 :
    ]
    share = packs[0].shape[0]
    nope = heads * NOPE
    queries = heads * (NOPE + ROPE)
    keyval_columns = keyval_ref.shape[1] * (KVR // shards) // share
    keyval_weight(block_ref, packs, weight_ref, queries)
    for k, pack in enumerate(packs):
        start = pl.multiple_of(block_ref[k] * share, share)
        value = dot_nn(normed_ref[:, pl.ds(start, share)], pack[:, :queries])
        if k == 0:
            total_ref[...] = value
        else:
            total_ref[...] += value
    keyval_ref[...] = dot_nn(low_ref[...], weight_ref[...]).astype(BF16)
    first, second = rope_turn(
        total_ref[:, nope : nope + LANES], total_ref[:, nope + LANES :], cosine_ref[...], sine_ref[...]
    )
    query_ref[:, :nope] = total_ref[:, :nope].astype(BF16)
    query_ref[:, nope : nope + LANES] = first.astype(BF16)
    query_ref[:, nope + LANES :] = second.astype(BF16)
    for head in range(heads):
        mask = head_mask(head)
        at = head * (NOPE + VD)
        turned = jnp.concatenate([first * mask, second * mask], axis=1).astype(BF16)
        scores = dot_nt(
            query_ref[:, head * NOPE : (head + 1) * NOPE], keyval_ref[:, at : at + NOPE]
        ) + dot_nt(turned, key_ref[...])
        scores = scores * ((NOPE + ROPE) ** (-0.5)) + bias_ref[...]
        raised = jnp.exp(scores - jnp.max(scores, axis=-1, keepdims=True))
        soft = raised / jnp.sum(raised, axis=-1, keepdims=True)
        soft_ref[head] = soft
        attended_ref[:, head * VD : (head + 1) * VD] = dot_nn(
            soft.astype(BF16), keyval_ref[:, at + NOPE : at + NOPE + VD]
        ).astype(BF16)
    output = queries + keyval_columns
    columns = part_ref.shape[1] // shards
    for k, pack in enumerate(packs):
        start = pl.multiple_of(block_ref[k] * columns, columns)
        value = dot_nn(attended_ref[:, :share], pack[:, output : output + columns])
        for i in range(1, heads * VD // share):
            value += dot_nn(
                attended_ref[:, i * share : (i + 1) * share],
                pack[:, output + i * columns : output + (i + 1) * columns],
            )
        part_ref[:, pl.ds(start, columns)] = value.astype(BF16)


def attention_back_kernel(heads, depth, block_ref, *refs):
    shards = (len(refs) - 2 * depth - 22) // 2
    packs, refs = refs[:shards], refs[shards:]
    tokens, refs = refs[:depth], refs[depth:]
    grads, refs = refs[:depth], refs[depth:]
    (
        query_ref, keyval_ref, key_ref, soft_ref, attended_ref, comp_ref, low_ref, normed_ref,
        latent_ref, kv_gain_ref, cosine_ref, sine_ref, router_ref, ffn_gain_ref,
        grad_query_ref, grad_keyval_ref, grad_normed_ref, *chunk_refs,
        gains_ref, grad_attended_ref, weight_ref, back_ref, stage_ref,
    ) = refs
    share = packs[0].shape[0]
    nope = heads * NOPE
    queries = heads * (NOPE + ROPE)
    keyval_columns = keyval_ref.shape[1] * (KVR // shards) // share
    output = queries + keyval_columns
    columns = normed_ref.shape[1] // shards
    scale = (NOPE + ROPE) ** (-0.5)
    stage_ref[...] = jnp.concatenate([piece[...] for piece in grads], axis=0)
    blocks = heads * VD // share
    for i in range(blocks):
        value = None
        for k, pack in enumerate(packs):
            start = pl.multiple_of(block_ref[k] * columns, columns)
            part = dot_nt(
                stage_ref[:, pl.ds(start, columns)],
                pack[:, output + i * columns : output + (i + 1) * columns],
            )
            value = part if value is None else value + part
        grad_attended_ref[:, i * share : (i + 1) * share] = value.astype(BF16)
    cosine, sine = cosine_ref[...], sine_ref[...]
    turn_first, turn_second = None, None
    key_turn = None
    for head in range(heads):
        mask = head_mask(head)
        at = head * (NOPE + VD)
        soft = soft_ref[head]
        attended = attended_ref[:, head * VD : (head + 1) * VD]
        grad = grad_attended_ref[:, head * VD : (head + 1) * VD]
        delta = jnp.sum(grad.astype(F32) * attended.astype(F32), axis=-1, keepdims=True)
        grad_soft = dot_nt(grad, keyval_ref[:, at + NOPE : at + NOPE + VD])
        scores = (soft * (grad_soft - delta) * scale).astype(BF16)
        query = query_ref[:, head * NOPE : (head + 1) * NOPE]
        grad_query_ref[:, head * NOPE : (head + 1) * NOPE] = dot_nn(
            scores, keyval_ref[:, at : at + NOPE]
        ).astype(BF16)
        turned = dot_nn(scores, key_ref[...])
        first, second = turned[:, :LANES] * mask, turned[:, LANES:] * mask
        turn_first = first if turn_first is None else turn_first + first
        turn_second = second if turn_second is None else turn_second + second
        wide = jnp.concatenate([mask, mask], axis=1)
        masked = (query_ref[:, nope:].astype(F32) * wide).astype(BF16)
        part = dot_tn(scores, masked)
        key_turn = part if key_turn is None else key_turn + part
        grad_keyval_ref[:, at : at + NOPE] = dot_tn(scores, query).astype(BF16)
        grad_keyval_ref[:, at + NOPE : at + NOPE + VD] = dot_tn(soft.astype(BF16), grad).astype(BF16)
    first, second = rope_turn(turn_first, turn_second, cosine, -sine)
    grad_query_ref[:, nope : nope + LANES] = first.astype(BF16)
    grad_query_ref[:, nope + LANES :] = second.astype(BF16)
    keyval_weight(block_ref, packs, weight_ref, queries)
    grad_comp = dot_nt(grad_keyval_ref[...], weight_ref[...])
    compressed = comp_ref[...]
    inverse = lax.rsqrt(jnp.mean(compressed * compressed, axis=-1, keepdims=True) + EPSILON)
    weighted = grad_comp * kv_gain_ref[...]
    grad_compressed = inverse * weighted - compressed * (inverse * inverse * inverse) * jnp.mean(
        compressed * weighted, axis=-1, keepdims=True
    )
    gains_ref[...] = jnp.zeros_like(gains_ref)
    gains_ref[2:3, :KVR] = jnp.sum(grad_comp * compressed * inverse, axis=0, keepdims=True)
    back_ref[:, :KVR] = grad_compressed.astype(BF16)
    first, second = rope_turn(key_turn[:, :LANES], key_turn[:, LANES:], cosine, -sine)
    back_ref[:, KVR : KVR + LANES] = first.astype(BF16)
    back_ref[:, KVR + LANES :] = second.astype(BF16)
    unit = unit_rows(tokens, normed_ref.shape[1])
    half = ROPE // 2
    for k, pack in enumerate(packs):
        start = pl.multiple_of(block_ref[k] * columns, columns)
        value = dot_nt(grad_query_ref[...], pack[:, :queries])
        value += dot_nn(back_ref[...], latent_ref[:, pl.ds(start, columns)])
        grad_normed_ref[:, pl.ds(start, columns)] = value.astype(BF16)
        weight = dot_tn(back_ref[...], normed_ref[:, pl.ds(start, columns)])
        turns = [
            sum(weight[KVR + i * LANES + j * half : KVR + i * LANES + (j + 1) * half] for j in range(heads))
            for i in range(2)
        ]
        chunk_refs[k][: KVR + ROPE] = jnp.concatenate([weight[:KVR]] + turns, axis=0).astype(BF16)
    gains_ref[0:1, :] = jnp.sum(grad_normed_ref[...].astype(F32) * unit, axis=0, keepdims=True)
    gains_ref[1:2, :] = ffn_gain_ref[...]
    used = KVR + ROPE
    for k in range(shards):
        at = pl.ds(pl.multiple_of(block_ref[k] * columns, columns), columns)
        chunk_refs[k][used : used + EXPERTS] = router_ref[:, at].astype(BF16)
        rows = [gains_ref[:2, at]]
        rows += [gains_ref[2:3, i * columns : (i + 1) * columns] for i in range(KVR // columns)]
        filled = 2 + KVR // columns
        rows.append(jnp.zeros((CHUNK_ROWS - used - EXPERTS - filled, columns), F32))
        chunk_refs[k][used + EXPERTS :] = jnp.concatenate(rows, axis=0).astype(BF16)


def attention_weights_kernel(heads, depth, block_ref, *refs):
    grads, refs = refs[:depth], refs[depth:]
    normed_ref, low_ref, attended_ref, query_ref, keyval_ref, *packs, stage_ref, whole_ref = refs
    shards, share = len(packs), packs[0].shape[0]
    queries = heads * (NOPE + ROPE)
    columns = normed_ref.shape[1] // shards
    part = KVR // shards
    count = share // part
    keyval_columns = keyval_ref.shape[1] // count
    output = queries + keyval_columns
    stage_ref[...] = jnp.concatenate([piece[...] for piece in grads], axis=0)
    whole_ref[...] = dot_tn(low_ref[...], keyval_ref[...]).astype(BF16)
    for k in range(shards):
        start = pl.multiple_of(block_ref[k] * columns, columns)
        packs[k][:, :queries] = dot_tn(
            normed_ref[:, pl.ds(start, columns)], query_ref[...]
        ).astype(BF16)
        rows = pl.ds(pl.multiple_of(block_ref[k] * part, part), part)
        for i in range(count):
            packs[k][i * part : (i + 1) * part, queries:output] = whole_ref[
                rows, i * keyval_columns : (i + 1) * keyval_columns
            ]
        value = dot_tn(attended_ref[...], stage_ref[:, pl.ds(start, columns)]).astype(BF16)
        for i in range(heads * VD // share):
            packs[k][:, output + i * columns : output + (i + 1) * columns] = value[
                i * share : (i + 1) * share
            ]


def vmem_call(kernel, name, blocks, operands, out_shape, scratch):
    if blocks is None:
        return pl.pallas_call(
            kernel,
            out_shape=out_shape,
            scratch_shapes=scratch,
            compiler_params=params(),
            name=name,
        )(*operands)
    return pl.pallas_call(
        kernel,
        grid_spec=pltpu.PrefetchScalarGridSpec(
            num_scalar_prefetch=1,
            grid=(1,),
            in_specs=[whole(a.shape) for a in operands],
            out_specs=[whole(a.shape) for a in out_shape],
            scratch_shapes=scratch,
        ),
        out_shape=out_shape,
        compiler_params=params("arbitrary"),
        name=name,
    )(blocks, *operands)


def latent_rows(pieces, gain, weight, kv_gain, cosine, sine):
    count = sum(piece.shape[0] for piece in pieces)
    width = gain.shape[0]
    return vmem_call(
        functools.partial(latent_kernel, len(pieces)),
        "latent_rows",
        None,
        [*pieces, gain[None], weight, kv_gain[None], cosine, sine],
        [
            jax.ShapeDtypeStruct((count, width), BF16),
            jax.ShapeDtypeStruct((count, KVR), F32),
            jax.ShapeDtypeStruct((count, KVR), BF16),
            jax.ShapeDtypeStruct((count, 2 * LANES), BF16),
            jax.ShapeDtypeStruct((KVR + 2 * LANES, width), BF16),
        ],
        [],
    )


def attention_forward(heads, blocks, packs, normed, low, key, bias, cosine, sine):
    count, width = normed.shape
    queries = heads * (NOPE + ROPE)
    keyval = heads * (NOPE + VD)
    return vmem_call(
        functools.partial(attention_kernel, heads),
        "attention_forward",
        blocks,
        [*packs, normed, low, key, bias, cosine, sine],
        [
            jax.ShapeDtypeStruct((count, queries), BF16),
            jax.ShapeDtypeStruct((count, keyval), BF16),
            jax.ShapeDtypeStruct((heads, count, count), F32),
            jax.ShapeDtypeStruct((count, heads * VD), BF16),
            jax.ShapeDtypeStruct((count, width), BF16),
        ],
        [pltpu.VMEM((count, queries), F32), pltpu.VMEM((KVR, keyval), BF16)],
    )


def attention_backward(
    heads, blocks, packs, tokens, grads, saved, latent, kv_gain, cosine, sine, router, ffn_gain
):
    query, keyval, key, soft, attended, compressed, low, normed = saved
    count, width = normed.shape
    shards = len(packs)
    return vmem_call(
        functools.partial(attention_back_kernel, heads, len(tokens)),
        "attention_backward",
        blocks,
        [
            *packs, *tokens, *grads, query, keyval, key, soft, attended, compressed, low, normed,
            latent, kv_gain[None], cosine, sine, router, ffn_gain[None],
        ],
        [
            jax.ShapeDtypeStruct(query.shape, BF16),
            jax.ShapeDtypeStruct(keyval.shape, BF16),
            jax.ShapeDtypeStruct((count, width), BF16),
        ]
        + [jax.ShapeDtypeStruct((CHUNK_ROWS, width // shards), BF16)] * shards,
        [
            pltpu.VMEM((8, width), F32),
            pltpu.VMEM((count, heads * VD), BF16),
            pltpu.VMEM((KVR, keyval.shape[1]), BF16),
            pltpu.VMEM((count, latent.shape[0]), BF16),
            pltpu.VMEM((count, width), BF16),
        ],
    )


def attention_weights(heads, blocks, shape, grads, normed, low, attended, grad_query, grad_keyval):
    count, width = normed.shape
    shards = blocks.shape[0]
    return vmem_call(
        functools.partial(attention_weights_kernel, heads, len(grads)),
        "attention_weights",
        blocks,
        [*grads, normed, low, attended, grad_query, grad_keyval],
        [jax.ShapeDtypeStruct(shape, BF16)] * shards,
        [pltpu.VMEM((count, width), BF16), pltpu.VMEM((KVR, grad_keyval.shape[1]), BF16)],
    )


def query_order(heads):
    size, half = NOPE + ROPE, ROPE // 2
    pieces = []
    for start, stop in ((0, NOPE), (NOPE, NOPE + half), (NOPE + half, size)):
        pieces += [(head * size + start, head * size + stop) for head in range(heads)]
    return pieces


def pack_weights(query, keyval, output, heads):
    share, columns = query.shape[0], output.shape[1]
    part = keyval.shape[0]
    count = share // part
    wide = keyval.shape[1] // count
    return jnp.concatenate(
        [query[:, start:stop] for start, stop in query_order(heads)]
        + [
            jnp.concatenate([keyval[:, i * wide : (i + 1) * wide] for i in range(count)], axis=0)
        ]
        + [output[i * share : (i + 1) * share] for i in range(output.shape[0] // share)],
        axis=1,
    )


def unpack_weights(pack, keyval_shape, output_shape, heads):
    size, half = NOPE + ROPE, ROPE // 2
    queries = heads * size
    share = pack.shape[0]
    part = keyval_shape[0]
    count = share // part
    wide = keyval_shape[1] // count
    nope = heads * NOPE
    query = []
    for head in range(heads):
        query += [
            pack[:, head * NOPE : (head + 1) * NOPE],
            pack[:, nope + head * half : nope + (head + 1) * half],
            pack[:, nope + (heads + head) * half : nope + (heads + head + 1) * half],
        ]
    keyval = jnp.concatenate(
        [pack[i * part : (i + 1) * part, queries : queries + wide] for i in range(count)], axis=1
    )
    at, columns = queries + wide, output_shape[1]
    output = jnp.concatenate(
        [
            pack[:, at + i * columns : at + (i + 1) * columns]
            for i in range(output_shape[0] // share)
        ],
        axis=0,
    )
    return jnp.concatenate(query, axis=1), keyval, output


def expert_layer(base, rows, grads, routes, router, expert_in, expert_out, shared):
    local, units, width = expert_out.shape
    sequences = len(rows)
    pairs = range(sequences // 2)
    shared_units = shared.shape[0] // 3
    side = jnp.concatenate([shared[: 2 * shared_units], router])
    shared_out = shared[2 * shared_units :]
    held = [None, None]
    for m in pairs:
        at = slice(2 * m, 2 * m + 2)
        held = dispatch_grads(
            m, sequences, local, base, routes[at], grads[at], shared_out, held[:2]
        )
    slot_grads, shared_raw, _ = held
    raw = expert_raw(slot_grads, expert_out)
    held = [None] * 6
    for m in pairs:
        at = slice(2 * m, 2 * m + 2)
        held = dispatch_rows(
            m, sequences, local, base, routes[at], rows[at], side, shared_raw, held
        )
    slot_rows, infos, picks, gates, shared_hidden, shared_back = held
    back_rows, extra, hidden, back = expert_rows(
        slot_rows, infos, expert_in.reshape(local, 2 * units, width), raw
    )
    back_tokens, logits = [], [None]
    for m in pairs:
        tokens, logits = combine_back(
            m, picks, back_rows, extra, gates, shared_back, side, logits
        )
        back_tokens += tokens
    out_rows = expert_out_rows(hidden, expert_out)
    out_tokens = []
    for m in pairs:
        out_tokens += combine_out(m, picks, out_rows, shared_hidden, shared_out)
    grad_in, grad_out, _ = weight_grads(
        0, local, slot_rows, slot_grads, hidden, back, [None, None]
    )
    all_rows = jnp.stack(rows)
    grad_router = contract("set,std->ed", logits[0], all_rows)
    grad_shared = jnp.concatenate(
        [
            contract("sft,std->fd", shared_back, all_rows),
            contract("sft,std->fd", shared_hidden, jnp.stack(grads)),
        ]
    )
    return (
        out_tokens,
        back_tokens,
        grad_in.reshape(local, 2, units, width),
        grad_out,
        grad_router,
        grad_shared,
    )


def general_device(
    tokens_in,
    out_grad,
    routes,
    attn_gain,
    kv_gain,
    ffn_gain,
    w_query,
    w_latent,
    w_keyval,
    w_output,
    w_router,
    w_shared_in,
    w_shared_out,
    w_expert_in,
    w_expert_out,
):
    grid = Grid()
    depth = grid.depth
    own_depth = lax.axis_index("tensor")
    own_rows, width = tokens_in.shape
    row_count = own_rows * depth
    local_experts = w_expert_in.shape[0]
    base = lax.axis_index("expert") * local_experts
    stream = jnp.concatenate(grid.gather_depth(tokens_in)).astype(F32)
    full_query = grid.absolute(grid.gather(w_query), 0)
    full_keyval = grid.absolute(grid.gather(w_keyval), 0)
    full_output = grid.absolute(grid.gather(w_output), 1)
    all_grads = grid.gather(jnp.concatenate(grid.gather_depth(out_grad)))
    routes_rel = jnp.concatenate(grid.relative_depth(routes.T, 1), axis=1)
    routes_all = [routes_rel] + [grid.fetch(routes_rel, offset) for offset in grid.offsets[1:]]
    units = w_shared_out.shape[0] // grid.experts
    padding = ((0, -units % 32), (0, 0))
    padded_units = units + padding[0][1]
    shared_parts = [
        jnp.concatenate([jnp.pad(part, padding) for part in parts])
        for parts in zip(
            grid.relative(w_shared_in[0].T, 0),
            grid.relative(w_shared_in[1].T, 0),
            grid.relative(w_shared_out, 0),
        )
    ]
    shared = grid.absolute(grid.exchange(shared_parts), 1)
    position = (
        (own_depth + jnp.arange(row_count) // own_rows) % depth * own_rows
        + jnp.arange(row_count) % own_rows
    )
    local_heads = full_query.shape[1] // (NOPE + ROPE)
    cosine, sine_table = rope_tables(position)
    normed_one, inverse_one = rms_forward(stream, attn_gain)
    normed_one = normed_one.astype(BF16)
    queries = mix_dot(normed_one, full_query).reshape(row_count, local_heads, NOPE + ROPE)
    queries = jnp.concatenate(
        [
            queries[..., :NOPE],
            rotate(queries[..., NOPE:], cosine[:, None, :], sine_table[:, None, :]),
        ],
        axis=-1,
    ).astype(BF16)
    latent = mix_dot(normed_one, w_latent)
    compressed = latent[:, :KVR]
    comp_normed, comp_inverse = rms_forward(compressed, kv_gain)
    comp_normed = comp_normed.astype(BF16)
    key_rope = rotate(latent[:, KVR:], cosine, sine_table).astype(BF16)
    keyval = mix_dot(comp_normed, full_keyval).reshape(row_count, local_heads, NOPE + VD).astype(BF16)
    key_nope = keyval[..., :NOPE]
    values = keyval[..., NOPE:]
    scores = attention_scores(queries, key_nope, key_rope, position)
    top_score = jnp.max(scores, axis=-1, keepdims=True)
    raised = jnp.exp(scores - top_score)
    soft = raised / jnp.sum(raised, axis=-1, keepdims=True)
    soft_low = soft.astype(BF16)
    attended = contract("hqk,khv->qhv", soft_low, values).astype(BF16)
    attended_flat = attended.reshape(row_count, local_heads * VD)
    attention_part = mix_dot(attended_flat, full_output).astype(BF16)
    stream_own = tokens_in.astype(F32)
    residual = stream_own + grid.reduce_depth(split_rows(attention_part, depth))
    normed_two, inverse_two = rms_forward(residual, ffn_gain)
    normed_two = normed_two.astype(BF16)
    all_rows = grid.gather(jnp.concatenate(grid.gather_depth(normed_two)))
    router_rel = jnp.roll(w_router.T, -base, axis=0)
    (
        out_tokens,
        back_tokens,
        grad_expert_in,
        grad_expert_out,
        grad_router_rel,
        grad_shared,
    ) = expert_layer(
        base.astype(jnp.int32)[None],
        all_rows,
        all_grads,
        routes_all,
        router_rel,
        jnp.swapaxes(w_expert_in, 2, 3),
        w_expert_out,
        shared,
    )
    grad_normed = grid.reduce_depth(
        split_rows(grid.reduce(back_tokens).astype(BF16), depth)
    )
    ffn_total = grid.reduce_depth(split_rows(grid.reduce(out_tokens).astype(BF16), depth))
    block_out = (residual + ffn_total).astype(BF16)
    grad_float = out_grad.astype(F32)
    grad_res_part, grad_ffn_gain = rms_backward(residual, inverse_two, ffn_gain, grad_normed)
    grad_residual = grad_float + grad_res_part
    grad_res_low = jnp.concatenate(grid.gather_depth(grad_residual.astype(BF16)))
    grad_output = contract("tv,td->vd", attended_flat, grad_res_low).astype(BF16)
    sum_output = grid.reduce(grid.relative(grad_output, 1))
    grad_attended = (
        contract("td,vd->tv", grad_res_low, full_output)
        .astype(BF16)
        .reshape(row_count, local_heads, VD)
    )
    softmax_scale = (NOPE + ROPE) ** (-0.5)
    grad_soft = contract("qhv,khv->hqk", grad_attended, values)
    row_delta = jnp.sum(grad_attended.astype(F32) * attended.astype(F32), axis=-1).T
    grad_scores = (soft * (grad_soft - row_delta[..., None]) * softmax_scale).astype(BF16)
    grad_query_nope = contract("hqk,khd->qhd", grad_scores, key_nope)
    grad_query_rope = contract("hqk,kr->qhr", grad_scores, key_rope)
    grad_key_nope = contract("hqk,qhd->khd", grad_scores, queries[..., :NOPE])
    grad_key_rope = contract("hqk,qhr->kr", grad_scores, queries[..., NOPE:])
    grad_values = contract("hqk,qhv->khv", soft_low, grad_attended)
    grad_query_raw = (
        jnp.concatenate(
            [
                grad_query_nope,
                rotate(grad_query_rope, cosine[:, None, :], -sine_table[:, None, :]),
            ],
            axis=-1,
        )
        .reshape(row_count, local_heads * (NOPE + ROPE))
        .astype(BF16)
    )
    grad_query_weight = contract("td,tq->dq", normed_one, grad_query_raw).astype(BF16)
    grad_keyval = (
        jnp.concatenate([grad_key_nope, grad_values], axis=-1)
        .reshape(row_count, local_heads * (NOPE + VD))
        .astype(BF16)
    )
    grad_keyval_weight = contract("tc,tk->ck", comp_normed, grad_keyval).astype(BF16)
    sum_query = grid.reduce(grid.relative(grad_query_weight, 0))
    sum_keyval = grid.reduce(grid.relative(grad_keyval_weight, 0))
    grad_comp_normed = contract("tk,ck->tc", grad_keyval, full_keyval)
    grad_compressed, grad_kv_gain = rms_backward(
        compressed, comp_inverse, kv_gain, grad_comp_normed
    )
    grad_latent_out = jnp.concatenate(
        [grad_compressed, rotate(grad_key_rope, cosine, -sine_table)], axis=-1
    ).astype(BF16)
    grad_latent = contract("tk,td->kd", grad_latent_out, normed_one)
    grad_normed_one = contract("tq,dq->td", grad_query_raw, full_query) + contract(
        "tk,dk->td", grad_latent_out, w_latent
    )
    grad_normed_one = grid.reduce_depth(split_rows(grad_normed_one.astype(BF16), depth))
    inverse_own = inverse_one[:own_rows]
    grad_x_part, grad_attn_gain = rms_backward(stream_own, inverse_own, attn_gain, grad_normed_one)
    grad_in = grad_residual + grad_x_part
    grad_shared_parts = [part.astype(BF16) for part in grid.relative(grad_shared, 1)]
    returned = grid.exchange(grad_shared_parts)
    sum_shared_in = jnp.stack(
        [
            grid.absolute([part[:units] for part in returned], 0).T,
            grid.absolute([part[padded_units : padded_units + units] for part in returned], 0).T,
        ]
    ).astype(F32)
    sum_shared_out = grid.absolute([part[2 * padded_units : 2 * padded_units + units] for part in returned], 0).astype(F32)
    gains = jnp.stack(
        [grad_attn_gain, grad_ffn_gain, jnp.pad(grad_kv_gain, (0, width - KVR))]
    )
    replicated = jnp.concatenate([grad_latent, jnp.roll(grad_router_rel, base, axis=0), gains])
    used = replicated.shape[0]
    padded = -(-used // (16 * grid.experts)) * 16 * grid.experts
    replicated = jnp.pad(replicated, ((0, padded - used), (0, 0))).astype(BF16)
    chunk = grid.reduce(grid.relative(replicated, 0)).astype(BF16)
    part = grid.reduce_depth(grid.relative_depth(chunk, 1)).astype(BF16)
    chunk = grid.absolute_depth(grid.gather_depth(part), 1)
    whole = grid.absolute(grid.gather(chunk), 0).astype(F32)
    sum_latent = whole[: KVR + ROPE].T
    sum_router = whole[KVR + ROPE : KVR + ROPE + EXPERTS].T
    sum_attn_gain = whole[KVR + ROPE + EXPERTS]
    sum_ffn_gain = whole[KVR + ROPE + EXPERTS + 1]
    sum_kv_gain = whole[KVR + ROPE + EXPERTS + 2, :KVR]
    return (
        block_out,
        grad_in,
        sum_attn_gain,
        sum_kv_gain,
        sum_ffn_gain,
        sum_query,
        sum_latent,
        sum_keyval,
        sum_output,
        sum_router,
        sum_shared_in,
        sum_shared_out,
        jnp.swapaxes(grad_expert_in, 2, 3),
        grad_expert_out,
    )


def after(array, *earlier):
    return lax.optimization_barrier((array, *earlier))[0]


def square_device(
    tokens_in,
    out_grad,
    routes,
    attn_gain,
    kv_gain,
    ffn_gain,
    w_query,
    w_latent,
    w_keyval,
    w_output,
    w_router,
    w_shared_in,
    w_shared_out,
    w_expert_in,
    w_expert_out,
):
    grid = Grid()
    depth = grid.depth
    sequences = grid.experts
    pairs = range(sequences // 2)
    own_rows, width = tokens_in.shape
    row_count = own_rows * depth
    local = w_expert_in.shape[0]
    hidden_units = w_expert_out.shape[1]
    heads = w_query.shape[1] // (NOPE + ROPE)
    own_depth = lax.axis_index("tensor")
    blocks = jnp.stack([grid.place_of(offset) for offset in grid.offsets]).astype(jnp.int32)
    base = (lax.axis_index("expert") * local).astype(jnp.int32)[None]

    both = jnp.concatenate([tokens_in, out_grad], axis=1)
    near = grid.ring_near(both)
    packs = grid.gather(pack_weights(w_query, w_keyval, w_output, heads))
    near = [after(piece, packs[2], packs[4]) for piece in near]
    tokens = [both, near[0], *grid.ring_far(*near), near[1]]
    group_grads = jnp.concatenate([piece[:, width:] for piece in tokens])

    position = (
        (own_depth + jnp.arange(row_count) // own_rows) % depth * own_rows
        + jnp.arange(row_count) % own_rows
    )
    cosine, sine = (jnp.tile(table, (1, heads)) for table in rope_tables(position))
    bias = jnp.where(position[None, :] <= position[:, None], 0.0, -1e30).astype(F32)
    normed, compressed, low, key, latent_t = latent_rows(
        [after(tokens[0], packs[6]), *tokens[1:]], attn_gain, w_latent.T, kv_gain, cosine, sine
    )

    units = w_shared_out.shape[0] // grid.experts
    padding = -units % 32
    padded_units = units + padding
    shared_in, shared_out = after(w_shared_in, packs[2]), after(w_shared_out, packs[2])
    routes_t = jnp.concatenate(grid.relative_depth(routes.T, 1), axis=1).astype(BF16)
    assert padding >= TOP and padding % 8 == 0 and units % 8 == 0
    fill = jnp.zeros((padding, w_shared_out.shape[1]), BF16)
    routes_fill = lax.dynamic_update_slice(fill, routes_t, (0, 0))
    shared_parts = [
        jnp.concatenate([first, routes_fill, second, fill, third, fill])
        for first, second, third in zip(
            grid.relative(shared_in[0].T, 0),
            grid.relative(shared_in[1].T, 0),
            grid.relative(shared_out, 0),
        )
    ]
    pieces = grid.exchange([after(part, packs[6]) for part in shared_parts])
    router = jnp.roll(after(w_router, packs[2]).T, -base[0], axis=0)
    side, shared_out, *routes_all = vmem_call(
        functools.partial(join_columns_kernel, units),
        "join_columns",
        blocks,
        [*pieces, router],
        [
            jax.ShapeDtypeStruct((2 * padded_units + EXPERTS, width), BF16),
            jax.ShapeDtypeStruct((padded_units, width), BF16),
        ]
        + [jax.ShapeDtypeStruct((padding, row_count), jnp.int32)] * sequences,
        [],
    )

    query, keyval, soft, attended, part = attention_forward(
        heads, blocks, packs, normed, low, key, bias, cosine, sine
    )

    def slots(m, held, *earlier):
        return dispatch_grads(
            m,
            sequences,
            local,
            base,
            routes_all[2 * m : 2 * m + 2],
            all_grads[2 * m : 2 * m + 2],
            after(shared_out, *earlier),
            held[:2],
        )

    middle = row_count // 2
    group_grads = after(group_grads, part)
    along_x = grid.fetch(group_grads, (0, 1, 0))
    along_y = grid.fetch(group_grads, (1, 0, 0))
    all_grads = [group_grads, grid.fetch(group_grads, (0, 0, 1))]
    parts = split_rows(part, depth)
    first, second = grid.ring_start(parts)
    first, second = after(first, *pieces), after(second, *pieces)
    ahead, behind, _ = grid.ring_finish(parts, first, second)
    ahead, behind = after(ahead, side), after(behind, side)
    stream = tokens_in.astype(F32)
    residual = stream + sum(array.astype(F32) for array in (parts[0], ahead, behind))
    normed_two, inverse_two = rms_forward(residual, ffn_gain)
    normed_two = normed_two.astype(BF16)
    near_rows = grid.ring_near(normed_two)
    held = slots(0, [None, None], normed_two)
    near_rows = [after(piece, held[2]) for piece in near_rows]
    along_x, along_y = after(along_x, *near_rows), after(along_y, *near_rows)
    first = grid.fetch(along_x[:middle], (1, 0, 0))
    second = grid.fetch(along_y[middle:], (0, 1, 0))
    for piece in (along_x, along_y):
        all_grads += [piece, grid.fetch(piece, (0, 0, 1))]
    far_rows = grid.ring_far(*near_rows)
    held = slots(1, held, *near_rows)
    far_rows = [after(piece, held[2]) for piece in far_rows]
    group_rows = jnp.concatenate([normed_two, near_rows[0], *far_rows, near_rows[1]])
    all_grads += [
        jnp.concatenate([first, second]),
        jnp.concatenate([grid.fetch(first, (0, 0, 1)), grid.fetch(second, (0, 0, 1))]),
    ]

    along_x = grid.fetch(group_rows, (0, 1, 0))
    along_y = grid.fetch(group_rows, (1, 0, 0))
    pair_rows = grid.fetch(group_rows, (0, 0, 1))
    for m in pairs[2:]:
        held = slots(m, held, group_rows)
    slot_grads, shared_raw, mark = held
    along_x, along_y = after(along_x, mark), after(along_y, mark)
    first = grid.fetch(along_x[:middle], (1, 0, 0))
    second = grid.fetch(along_y[middle:], (0, 1, 0))
    raw = expert_raw(after(slot_grads, along_x, along_y), w_expert_out)
    first, second = after(first, raw), after(second, raw)
    rows = [group_rows, pair_rows]
    for held in (along_x, along_y):
        rows += [held, grid.fetch(held, (0, 0, 1))]
    rows += [
        jnp.concatenate([first, second]),
        jnp.concatenate([grid.fetch(first, (0, 0, 1)), grid.fetch(second, (0, 0, 1))]),
    ]

    held = [None] * 6
    for m in pairs:
        held = dispatch_rows(
            m,
            sequences,
            local,
            base,
            routes_all[2 * m : 2 * m + 2],
            rows[2 * m : 2 * m + 2],
            side,
            shared_raw,
            held,
        )
    slot_rows, infos, picks, gates, shared_hidden, shared_back = held
    expert_in = jnp.swapaxes(w_expert_in, 2, 3).reshape(local, 2 * hidden_units, width)
    back_rows, extra, hidden, back = expert_rows(slot_rows, infos, expert_in, raw)

    def backs(m, logits, *earlier):
        return combine_back(
            m, picks, after(back_rows, *earlier), extra, gates, shared_back, side, logits
        )

    front, rear = slice(None, row_count // 2), slice(row_count // 2, None)
    (near_6, far_6), logits = backs(3, [None])
    (near_4, far_4), logits = backs(2, logits, near_6)
    own_6 = low_add(near_6, grid.send(far_6, (0, 0, 1)))
    first = grid.send(own_6[front], (0, 1, 0))
    second = grid.send(own_6[rear], (1, 0, 0))
    (near_2, far_2), logits = backs(1, logits, own_6)
    own_4 = low_add(near_4, grid.send(far_4, (0, 0, 1)))
    (near_0, far_0), logits = backs(0, logits, own_4)
    own_2 = low_add(near_2, grid.send(far_2, (0, 0, 1)))
    first, second = after(first, near_0), after(second, near_0)
    to_y = jnp.concatenate([low_add(own_4[front], first), own_4[rear]])
    to_x = jnp.concatenate([own_2[front], low_add(own_2[rear], second)])
    from_x = grid.send(to_x, (0, 1, 0))
    from_y = grid.send(to_y, (1, 0, 0))

    def outs(m, *earlier):
        return combine_out(m, picks, after(out_rows, *earlier), shared_hidden, shared_out)

    out_rows = expert_out_rows(after(hidden, to_x, to_y), w_expert_out)
    own_0 = low_add(near_0, grid.send(far_0, (0, 0, 1)))
    out_6, out_7 = outs(3)
    out_4, out_5 = outs(2, out_6)
    from_x, from_y = after(from_x, out_4), after(from_y, out_4)
    grad_group = (own_0.astype(F32) + from_x.astype(F32) + from_y.astype(F32)).astype(BF16)
    chunks = split_rows(grad_group, depth)
    first, second = grid.ring_start(chunks)
    out_own_6 = low_add(after(out_6, grad_group), grid.send(after(out_7, grad_group), (0, 0, 1)))
    out_own_4 = low_add(out_4, grid.send(after(out_5, grad_group), (0, 0, 1)))
    out_first = grid.send(out_own_6[front], (0, 1, 0))
    out_second = grid.send(out_own_6[rear], (1, 0, 0))
    out_2, out_3 = outs(1, grad_group)
    first, second = after(first, out_2), after(second, out_2)
    ahead, behind, marks = grid.ring_finish(chunks, first, second)
    out_0, out_1 = outs(0, *marks, out_own_6, out_own_4)
    ahead, behind = after(ahead, out_0, out_first, out_second), after(behind, out_0)
    grad_normed = chunks[0].astype(F32) + ahead.astype(F32) + behind.astype(F32)

    grad_res_part, grad_ffn_gain = rms_backward(residual, inverse_two, ffn_gain, grad_normed)
    grad_residual = out_grad.astype(F32) + grad_res_part
    grad_low = grad_residual.astype(BF16)
    near_grads = grid.ring_near(grad_low)
    out_own_2 = low_add(out_2, grid.send(out_3, (0, 0, 1)))
    out_own_0 = low_add(out_0, grid.send(out_1, (0, 0, 1)))
    out_to_y = jnp.concatenate([low_add(out_own_4[front], out_first), out_own_4[rear]])
    out_to_x = jnp.concatenate([out_own_2[front], low_add(out_own_2[rear], out_second)])
    out_from_x = grid.send(out_to_x, (0, 1, 0))
    out_from_y = grid.send(out_to_y, (1, 0, 0))
    *grad_parts, grad_router = side_grads(
        blocks, base, rows, all_grads, after(logits[0], grad_low, out_to_x, out_to_y), shared_hidden, shared_back
    )
    out_from_x, out_from_y = after(out_from_x, grad_router), after(out_from_y, grad_router)
    near_grads = [after(piece, grad_router) for piece in near_grads]
    far_grads = grid.ring_far(*near_grads)
    grads = [grad_low, near_grads[0], *far_grads, near_grads[1]]

    returned = grid.exchange([after(piece, *near_grads) for piece in grad_parts])
    grads[0] = after(grads[0], out_from_x, out_from_y)
    grad_query, grad_keyval, grad_normed_one, *chunks = attention_backward(
        heads,
        blocks,
        packs,
        tokens,
        grads,
        (query, keyval, key, soft, attended, compressed, low, normed),
        latent_t,
        kv_gain,
        cosine,
        sine,
        grad_router,
        grad_ffn_gain,
    )
    out_group = (
        out_own_0.astype(F32)
        + out_from_x.astype(F32)
        + out_from_y.astype(F32)
    ).astype(BF16)
    grad_packs = attention_weights(
        heads,
        blocks,
        packs[0].shape,
        grads,
        normed,
        low,
        attended,
        after(grad_query, *returned),
        grad_keyval,
    )
    sums, chunk_first, chunk_mark = grid.reduce_parts(chunks)
    share = local // 4
    held = [None, None]

    def weights(step, held, *earlier):
        return weight_grads(
            step * share,
            (step + 1) * share,
            after(slot_rows, *earlier),
            slot_grads,
            hidden,
            back,
            held[:2],
        )

    def ring_rounds(rows, start, middle, stop):
        parts = split_rows(after(rows, start), depth)
        first, second = grid.ring_start(parts)
        ahead, behind, _ = grid.ring_finish(parts, after(first, middle), after(second, middle))
        return sum(a.astype(F32) for a in (parts[0], after(ahead, stop), after(behind, stop)))

    held = weights(0, held, grad_packs[0], chunk_first)
    marks = [held[2]]
    held = weights(1, held, held[2], *chunk_mark)
    mark = held[2]
    marks.append(mark)
    columns = width // grid.experts
    chunk = sum(a.astype(F32) for a in (sums[0], after(sums[1], mark), after(sums[2], mark)))
    chunk = chunk.astype(BF16)
    pack_own, pack_first, pack_mark = grid.reduce_first([after(pack, mark) for pack in grad_packs])
    flip = [(i, i ^ 1) for i in range(depth)]
    other = lax.ppermute(chunk, "tensor", flip)
    held = weights(2, held, chunk, pack_first)
    marks.append(held[2])
    chunk = (chunk.astype(F32) + other.astype(F32) + held[2][:1, :1]).astype(BF16)
    flip = [(i, i ^ 2) for i in range(depth)]
    other = lax.ppermute(chunk, "tensor", flip)
    *held, mark = weights(3, held, chunk, *pack_mark)
    grad_expert_in, grad_expert_out = held
    marks.append(mark)
    block_out = (residual + ring_rounds(out_group, *marks[:3])).astype(BF16)
    grad_normed_one = ring_rounds(grad_normed_one, *marks[1:])
    chunk = (chunk.astype(F32) + other.astype(F32) + mark[:1, :1]).astype(BF16)
    sum_shared_in, sum_shared_out = vmem_call(
        functools.partial(join_rows_kernel, units),
        "join_rows",
        blocks,
        [after(returned[0], chunk), *returned[1:]],
        [
            jax.ShapeDtypeStruct((2, units * grid.experts, width // grid.experts), F32),
            jax.ShapeDtypeStruct((units * grid.experts, width // grid.experts), F32),
        ],
        [],
    )
    gathered = grid.gather(chunk)
    pack_mark = [after(part, gathered[2], gathered[4]) for part in pack_mark]
    pack_sums = [pack_own, *grid.reduce_second(*pack_mark)]
    gathered[0] = after(gathered[0], sum_shared_out)
    sum_latent, sum_router, sum_gains = vmem_call(
        functools.partial(replicated_kernel, KVR + ROPE),
        "replicated",
        blocks,
        gathered,
        [
            jax.ShapeDtypeStruct((KVR + ROPE, width), F32),
            jax.ShapeDtypeStruct((EXPERTS, width), F32),
            jax.ShapeDtypeStruct((16, width), F32),
        ],
        [],
    )
    sum_kv_gain = sum_gains[2 : 2 + KVR // columns, :columns].reshape(KVR)

    inverse_one = lax.rsqrt(jnp.mean(stream * stream, axis=-1, keepdims=True) + EPSILON)
    grad_in = grad_residual + rms_backward(stream, inverse_one, attn_gain, grad_normed_one)[0]
    sum_query, sum_keyval, sum_output = unpack_weights(
        sum(array.astype(F32) for array in pack_sums), w_keyval.shape, w_output.shape, heads
    )
    return (
        block_out,
        grad_in,
        sum_gains[0],
        sum_kv_gain,
        sum_gains[1],
        sum_query,
        sum_latent.T,
        sum_keyval,
        sum_output,
        sum_router.T,
        jnp.swapaxes(sum_shared_in, 1, 2),
        sum_shared_out,
        jnp.swapaxes(grad_expert_in.reshape(local, 2, hidden_units, width), 2, 3),
        grad_expert_out,
    )


def solution(mesh):
    placed = (
        P(("expert", "tensor"), None),
        P(("expert", "tensor"), None),
        P("expert", None),
        P(),
        P(),
        P(),
        P("expert", "tensor"),
        P(),
        P("expert", "tensor"),
        P("tensor", "expert"),
        P(),
        P(None, "expert", "tensor"),
        P("tensor", "expert"),
        P("expert", None, None, "tensor"),
        P("expert", "tensor", None),
    )
    square = mesh.shape["expert"] == 8 and mesh.shape["tensor"] == 4
    return jax.shard_map(
        square_device if square else general_device,
        mesh=mesh,
        in_specs=placed,
        out_specs=(
            P(("expert", "tensor"), None),
            P(("expert", "tensor"), None),
            P(),
            P(),
            P(),
            P("expert", "tensor"),
            P(),
            P("expert", "tensor"),
            P("tensor", "expert"),
            P(),
            P(None, "expert", "tensor"),
            P("tensor", "expert"),
            P("expert", None, None, "tensor"),
            P("expert", "tensor", None),
        ),
        check_vma=False,
    )
```
